32 devices in a mesh: grp: 2 (over x), seq: 16 (over z, y, core).
Axes of the slice: x: 2, y: 2, z: 4, core: 2. Of those that a mesh axis runs over, the one named last changes fastest.
Arguments:
- events_in: bfloat16 [16384, 1024], P(('grp', 'seq')), parts along dimension 0, may hold values from -6 to 6
- w_in: bfloat16 [1024, 4096], replicated, may hold values from -0.1875 to 0.1875
- w_out: bfloat16 [1024, 1024], replicated, may hold values from -0.1875 to 0.1875
- kv_list: int32 [128, 3], P(('grp', 'seq')), parts along dimension 0, may hold values from -8 to 62, as said below
- counts: int32 [128], P(('grp', 'seq')), parts along dimension 0, may hold values from 32 to 128
- grad_out: bfloat16 [16384, 1024], P(('grp', 'seq')), parts along dimension 0, may hold values from -6 to 6
Outputs:
- events_out: bfloat16 [16384, 1024], P(('grp', 'seq')), parts along dimension 0
- grad_x: bfloat16 [16384, 1024], P(('grp', 'seq')), parts along dimension 0
- grad_w_in: float32 [2048, 4096], P(('grp', 'seq')), parts along dimension 0
- grad_w_out: float32 [2048, 1024], P(('grp', 'seq')), parts along dimension 0
The draws below stay inside these ranges and needn't reach their ends.
There are 2 independent parts, one for each index of `grp`. The reference program is written for one: setup_inputs(seed, part) draws one part's arguments, and reference() takes and returns one part's arrays. A program takes and returns all parts, laid end to end along the dimension named above; an argument that names none is the same for every part. Nothing has to cross between parts.
Inputs may be any that keep to these rules, and one draw needn't show every extreme that they name: `kv_list`: row b's entries are distinct and lie from b - 8 to b - 1; the first is b - 8; a negative entry names no block.
All inputs are finite; a program needn't handle non-finite values.
Results may differ from the reference program's by a relative error of at most 0.014.
Values may be sent and summed in bfloat16 or wider, within the bound.
No kernel may reach another device: no remote copies, remote signals or barrier semaphores. Data moves between devices by JAX's collectives and lax.ppermute only.
A program may use at most 192 MiB of HBM per device.

```python
import jax
import jax.numpy as jnp
from jax import lax

D = 1024
HEADS = 16
BLK = 128
LISTS = 3
REACH = 8
BLOCKS = 64
EVENTS = 8192


def draw_kv_list(key, part):
    query = jnp.arange(BLOCKS, dtype=jnp.int32)[:, None]
    scores = jax.random.randint(key, (BLOCKS, REACH - 1), 0, 1 << 20).astype(jnp.int32)
    scores = scores * REACH + jnp.arange(REACH - 1, dtype=jnp.int32)[None, :]
    order = jnp.argsort(scores, axis=1).astype(jnp.int32)
    offsets = jnp.concatenate([jnp.full((BLOCKS, 1), REACH, jnp.int32), order[:, :LISTS - 1] + 1], axis=1)
    return (query - offsets).astype(jnp.int32)


def with_ends(result, own_key, least, largest):
    dims = result.shape
    spot = [jax.random.randint(jax.random.fold_in(own_key, axis), (), 0, dims[axis]) for axis in range(len(dims))]
    result = result.at[tuple(spot)].set(least)
    longest = dims.index(max(dims))
    spot[longest] = (spot[longest] + 1) % dims[longest]
    return result.at[tuple(spot)].set(largest)


def block_scale(key, dims, split, smallest, top_value):
    def one(axis_at, parts):
        heights = jax.random.uniform(jax.random.fold_in(jax.random.fold_in(key, 6), axis_at), (parts,), jnp.float32, smallest / len(split), top_value / len(split))
        return jnp.repeat(jnp.exp(heights), dims[axis_at] // parts).reshape((-1,) + (1,) * (len(dims) - axis_at - 1))

    loudness = one(*split[0])
    for cut in split[1:]:
        loudness = loudness * one(*cut)
    return loudness


def bell_draw(key, shape, scale, reach, pieces=(), kind=jnp.bfloat16):
    entries = scale * jax.random.normal(key, shape, jnp.float32)
    if pieces:
        entries = entries * block_scale(key, shape, pieces, -0.22, 0.18)
    return jnp.clip(entries, -reach, reach).astype(kind)


def setup_inputs(seed: int = 0, part: int = 0) -> dict:
    key_of = jax.random.split(jax.random.key(seed), 7)
    part_keys = jax.random.split(jax.random.fold_in(key_of[6], part), 7)
    return {
        "events_in": bell_draw(part_keys[0], (EVENTS, D), 1.0, 6.0, ((0, 16),)),
        "w_in": bell_draw(key_of[1], (D, 4 * D), D ** -0.5, 0.1875),
        "w_out": bell_draw(key_of[2], (D, D), D ** -0.5, 0.1875),
        "kv_list": draw_kv_list(jax.random.fold_in(jax.random.fold_in(key_of[6], part), 71), part),
        "counts": with_ends(jax.random.randint(part_keys[4], (BLOCKS,), BLK // 4, BLK + 1), jax.random.fold_in(part_keys[4], 1), BLK // 4, BLK).astype(jnp.int32),
        "grad_out": bell_draw(part_keys[5], (EVENTS, D), 1.0, 6.0, ((0, 16),)),
    }


EPS = 1e-05

def normalize(vals):
    mean = lax.optimization_barrier(jnp.mean(vals, axis=-1, keepdims=True))
    cent = vals - mean
    var = lax.optimization_barrier(jnp.mean(cent * cent, axis=-1, keepdims=True))
    return cent * lax.rsqrt(var + EPS)

def mult(form, left, right):
    return jnp.einsum(form, left.astype(jnp.float32), right.astype(jnp.float32))

def weigh(query, keys, lengths):
    blk, width = query.shape
    slots = keys.shape[0]
    head_dim = width // HEADS
    qh = query.reshape(blk, HEADS, head_dim)
    kh = keys.reshape(slots * blk, HEADS, head_dim)
    scores = mult('ihd,jhd->hij', qh, kh) * head_dim ** (-0.5)
    spots = jnp.arange(slots * blk, dtype=jnp.int32)
    within = spots % blk
    slot = spots // blk
    limit = jnp.repeat(lengths, blk, total_repeat_length=slots * blk)
    places = jnp.arange(blk, dtype=jnp.int32)
    keep = (within[None, :] < limit[None, :]) & ((slot[None, :] < slots - 1) | (within[None, :] <= places[:, None]))
    weights = jnp.where(keep[None], jax.nn.silu(scores) / blk, 0.0).astype(jnp.bfloat16)
    return (qh, kh, scores, keep, weights)

def attend(query, keys, values, lengths):
    blk, width = query.shape
    qh, kh, scores, keep, weights = weigh(query, keys, lengths)
    vh = values.reshape(kh.shape)
    return mult('hij,jhd->ihd', weights, vh).reshape(blk, width)

def attend_back(query, keys, values, lengths, dmix):
    blk, width = query.shape
    slots = keys.shape[0]
    head_dim = width // HEADS
    qh, kh, scores, keep, weights = weigh(query, keys, lengths)
    vh = values.reshape(kh.shape)
    dh = dmix.reshape(blk, HEADS, head_dim)
    dweight = mult('ihd,jhd->hij', dh, vh)
    sig = jax.nn.sigmoid(scores)
    dscore = jnp.where(keep[None], dweight * sig * (1.0 + scores * (1.0 - sig)) / blk, 0.0).astype(jnp.bfloat16)
    scale = head_dim ** (-0.5)
    dval = mult('hij,ihd->jhd', weights, dh)
    dque = mult('hij,jhd->ihd', dscore, kh) * scale
    dkey = mult('hij,ihd->jhd', dscore, qh) * scale
    return (dque.reshape(blk, width), dkey.reshape(slots, blk, width), dval.reshape(slots, blk, width))

def project(x32, w_in):
    normed = normalize(x32).astype(jnp.bfloat16)
    pre = jnp.dot(normed, w_in, preferred_element_type=jnp.float32)
    acts = jax.nn.silu(pre).astype(jnp.bfloat16)
    return (normed, pre, acts)

def reference(events_in, w_in, w_out, kv_list, counts, grad_out):
    events, width = events_in.shape
    blk = BLK
    nblk = events // blk
    x32 = events_in.astype(jnp.float32)
    normed, pre, acts = project(x32, w_in)
    u_part = acts[:, :width]
    v_part = acts[:, width:2 * width]
    q_part = acts[:, 2 * width:3 * width]
    k_part = acts[:, 3 * width:]
    kb = k_part.reshape(nblk, blk, width)
    vb = v_part.reshape(nblk, blk, width)
    qb = q_part.reshape(nblk, blk, width)
    own = jnp.arange(nblk, dtype=jnp.int32)
    index = jnp.concatenate([kv_list, own[:, None]], axis=1)
    valid = index >= 0
    safe = jnp.maximum(index, 0).astype(jnp.int32)
    lengths = jnp.where(valid, counts[safe], 0).astype(jnp.int32)

    def forward_block(items):
        query, idx, lens = items
        return attend(query, kb[idx], vb[idx], lens)
    attn = lax.map(forward_block, (qb, safe, lengths)).reshape(events, width)
    u32 = u_part.astype(jnp.float32)
    y_out = (normalize(attn) * u32).astype(jnp.bfloat16)
    events_out = (x32 + jnp.dot(y_out, w_out, preferred_element_type=jnp.float32)).astype(jnp.bfloat16)
    grad_w_out = jnp.dot(y_out.T, grad_out, preferred_element_type=jnp.float32)
    dy_full = jnp.dot(grad_out, w_out.T, preferred_element_type=jnp.float32)
    _, tail_vjp = jax.vjp(lambda first, second: normalize(first) * second, attn, u32)
    dattn, du_part = tail_vjp(dy_full)
    dmix = dattn.astype(jnp.bfloat16).reshape(nblk, blk, width)

    def backward_block(items):
        query, idx, lens, dblock = items
        return attend_back(query, kb[idx], vb[idx], lens, dblock)
    dq_part, dkeys, dvals = lax.map(backward_block, (qb, safe, lengths, dmix))
    dk_part = jnp.zeros((nblk, blk, width), jnp.float32).at[safe].add(dkeys)
    dv_part = jnp.zeros((nblk, blk, width), jnp.float32).at[safe].add(dvals)
    dact = jnp.concatenate([du_part, dv_part.reshape(events, width), dq_part.reshape(events, width), dk_part.reshape(events, width)], axis=1)
    sig = jax.nn.sigmoid(pre)
    dpre = (dact * sig * (1.0 + pre * (1.0 - sig))).astype(jnp.bfloat16)
    grad_w_in = jnp.dot(normed.T, dpre, preferred_element_type=jnp.float32)
    dnormed = jnp.dot(dpre, w_in.T, preferred_element_type=jnp.float32)
    _, norm_vjp = jax.vjp(normalize, x32)
    grad_x = (grad_out.astype(jnp.float32) + norm_vjp(dnormed)[0]).astype(jnp.bfloat16)
    return (events_out, grad_x, grad_w_in, grad_w_out)
```

```python
import jax
import jax.numpy as jnp
from jax import lax
from jax.experimental import pallas as pl
from jax.experimental.pallas import tpu as pltpu
from jax.sharding import PartitionSpec as P

HEADS = 16
HD = 64
BLK = 128
WIDE = 1024
BACK = 2
EPS = 1e-05
F32 = jnp.float32
BF16 = jnp.bfloat16
VMEM_LIMIT = 60 * 1024 * 1024


def nn(left, right):
    return lax.dot_general(left, right, (((1,), (0,)), ((), ())), preferred_element_type=F32)


def nt(left, right):
    return lax.dot_general(left, right, (((1,), (1,)), ((), ())), preferred_element_type=F32)


def params(*kinds):
    return pltpu.CompilerParams(dimension_semantics=kinds or None, vmem_limit_bytes=VMEM_LIMIT)


def whole(shape):
    zeros = (0,) * len(shape)
    return pl.BlockSpec(shape, lambda *_: zeros, pipeline_mode=pl.Buffered(1))


def sds(shape, dtype):
    return jax.ShapeDtypeStruct(shape, dtype)


def norm_parts(rows):
    mean = jnp.mean(rows, axis=-1, keepdims=True)
    cent = rows - mean
    var = jnp.mean(cent * cent, axis=-1, keepdims=True)
    return cent, lax.rsqrt(var + EPS)


def normed_of(x):
    cent, rstd = norm_parts(x.astype(F32))
    return (cent * rstd).astype(BF16)


def silu_both(pre):
    t = jnp.tanh(0.5 * pre)
    sig = 0.5 + 0.5 * t
    act = pre * sig
    slope = sig + act * (0.5 - 0.5 * t)
    return act, slope


def uq_kernel(x_ref, w_ref, acts_ref, slope_ref, normed_ref):
    step = pl.program_id(0)

    @pl.when(step == 0)
    def _():
        normed_ref[...] = normed_of(x_ref[...])

    scale = jnp.where(step >= 2, HD ** (-0.5) * 0.5, 1.0).astype(F32)
    for part in range(2):
        rows = pl.ds(part * 256, 256)
        act, slope = silu_both(nn(normed_ref[rows, :], w_ref[...]))
        acts_ref[rows, :] = (act * scale).astype(BF16)
        slope_ref[rows, :] = slope.astype(BF16)


def project_uq(x, w_in):
    rows = x.shape[0]
    out = pl.BlockSpec((rows, 512), lambda j: (0, j))
    return pl.pallas_call(
        uq_kernel,
        grid=(4,),
        in_specs=[whole(x.shape), pl.BlockSpec((WIDE, 512), lambda j: (0, j + 2 * (j // 2)))],
        out_specs=[out, out],
        out_shape=[sds((rows, 2 * WIDE), BF16)] * 2,
        scratch_shapes=[pltpu.VMEM((rows, WIDE), BF16)],
        compiler_params=params("arbitrary"),
        name="project_uq",
    )(x, w_in)


def kv_body(counts_ref, x_refs, w_ref, kv_ref, slope_ref, normed_t_ref, base):
    step = pl.program_id(0)
    rows = x_refs[0].shape[0]

    @pl.when(step == 0)
    def _():
        for at, x_ref in enumerate(x_refs):
            normed_t_ref[:, at * rows : (at + 1) * rows] = normed_of(x_ref[...]).T

    lane = lax.broadcasted_iota(jnp.int32, (1, BLK), 1)
    for pair in range(len(x_refs) * rows // 256):
        act, slope = silu_both(nn(w_ref[...], normed_t_ref[:, pair * 256 : (pair + 1) * 256]))
        slope_ref[:, pair * 256 : (pair + 1) * 256] = slope.astype(BF16)
        for half in range(2):
            place = 2 * pair + half
            live = lane < counts_ref[base + place]
            part = act[:, half * BLK : (half + 1) * BLK]
            kv_ref[place] = jnp.where(live, part, 0.0).astype(BF16)


def kv_own_kernel(counts_ref, x_ref, w_ref, kv_ref, slope_ref, normed_t_ref):
    kv_body(counts_ref, [x_ref], w_ref, kv_ref, slope_ref, normed_t_ref, 8)


def kv_win_kernel(counts_ref, xa_ref, xb_ref, w_ref, _, kv_ref, slope_ref, normed_t_ref):
    kv_body(counts_ref, [xa_ref, xb_ref], w_ref, kv_ref, slope_ref, normed_t_ref, 0)


def project_kv_own(counts, x, w_kv_t):
    rows = x.shape[0]
    nblk = rows // BLK
    return pl.pallas_call(
        kv_own_kernel,
        grid_spec=pltpu.PrefetchScalarGridSpec(
            num_scalar_prefetch=1,
            grid=(4,),
            in_specs=[whole(x.shape), pl.BlockSpec((512, WIDE), lambda j, _: (j, 0))],
            out_specs=[
                pl.BlockSpec((nblk, 512, BLK), lambda j, _: (BACK, j, 0)),
                pl.BlockSpec((512, rows), lambda j, _: (j, 0)),
                whole((WIDE, rows)),
            ],
        ),
        out_shape=[
            sds(((BACK + 1) * nblk, 2 * WIDE, BLK), BF16),
            sds((2 * WIDE, rows), BF16),
            sds((WIDE, rows), BF16),
        ],
        compiler_params=params("arbitrary"),
        name="project_kv_own",
    )(counts, x, w_kv_t)


def project_kv_window(counts, x_far, x_near, w_kv_t, kv):
    rows = x_far.shape[0]
    nblk = rows // BLK
    return pl.pallas_call(
        kv_win_kernel,
        grid_spec=pltpu.PrefetchScalarGridSpec(
            num_scalar_prefetch=1,
            grid=(4,),
            in_specs=[
                whole(x_far.shape),
                whole(x_near.shape),
                pl.BlockSpec((512, WIDE), lambda j, _: (j, 0)),
                pl.BlockSpec(memory_space=pl.ANY),
            ],
            out_specs=[
                pl.BlockSpec((2 * nblk, 512, BLK), lambda j, _: (0, j, 0)),
                pl.BlockSpec((512, 2 * rows), lambda j, _: (j, 0)),
                whole((WIDE, 2 * rows)),
            ],
        ),
        out_shape=[
            sds(kv.shape, BF16),
            sds((2 * WIDE, 2 * rows), BF16),
            sds((WIDE, 2 * rows), BF16),
        ],
        input_output_aliases={4: 0},
        compiler_params=params("arbitrary"),
        name="project_kv_window",
    )(counts, x_far, x_near, w_kv_t, kv)


def dy_kernel(g_ref, w_ref, dy_ref):
    dy_ref[...] = nt(g_ref[...], w_ref[...])


def back_out(grad_out, w_out):
    rows = grad_out.shape[0]
    return pl.pallas_call(
        dy_kernel,
        grid=(2,),
        in_specs=[whole(grad_out.shape), pl.BlockSpec((512, WIDE), lambda j: (j, 0))],
        out_specs=pl.BlockSpec((rows, 512), lambda j: (0, j)),
        out_shape=sds((rows, WIDE), F32),
        compiler_params=params("arbitrary"),
        name="back_out",
    )(grad_out, w_out)


def slot_rows(kv_ref, idx_ref, blk, at):
    return [kv_ref[idx_ref[blk, slot], at : at + HD, :] for slot in range(4)]


def fwd_kernel(
    idx_ref, q_ref, u_ref, uslope_ref, kv_ref, dy_ref,
    w_ref, g_ref, y_ref, yt_ref, dpu_ref, do_ref, dot_ref, qt_ref, attn_ref,
):
    blk = pl.program_id(0)
    row = lax.broadcasted_iota(jnp.int32, (BLK, BLK), 0)
    col = lax.broadcasted_iota(jnp.int32, (BLK, BLK), 1)
    causal = col <= row
    qt_ref[...] = q_ref[...].T
    for pair in range(HEADS // 2):
        outs = []
        for half in range(2):
            head = 2 * pair + half
            query = q_ref[:, pair * 128 + half * HD : pair * 128 + half * HD + HD]
            keys = slot_rows(kv_ref, idx_ref, blk, WIDE + head * HD)
            vals = slot_rows(kv_ref, idx_ref, blk, head * HD)
            total = None
            for duo in range(2):
                s_half = nn(query, jnp.concatenate(keys[2 * duo : 2 * duo + 2], axis=1))
                t = jnp.tanh(s_half)
                p = 1.0 + t
                w = s_half * p
                g = p + w * (1.0 - t)
                if duo == 1:
                    keep = jnp.concatenate([jnp.full((BLK, BLK), True), causal], axis=1)
                    w = jnp.where(keep, w, 0.0)
                    g = jnp.where(keep, g, 0.0)
                w = w.astype(BF16)
                w_ref[0, head, :, duo * 256 : duo * 256 + 256] = w
                g_ref[0, head, :, duo * 256 : duo * 256 + 256] = g.astype(BF16)
                part = nt(w, jnp.concatenate(vals[2 * duo : 2 * duo + 2], axis=1))
                total = part if total is None else total + part
            outs.append(total)
        attn_ref[:, pair * 128 : pair * 128 + 128] = jnp.concatenate(outs, axis=1) * (1.0 / BLK)
    cent, rstd = norm_parts(attn_ref[...])
    z = cent * rstd
    u = u_ref[...].astype(F32)
    dy = dy_ref[...]
    y = (z * u).astype(BF16)
    y_ref[...] = y
    yt_ref[...] = y.T
    dpu_ref[...] = (dy * z * uslope_ref[...].astype(F32)).astype(BF16)
    dz = dy * u
    dattn = rstd * (
        dz - jnp.mean(dz, axis=-1, keepdims=True) - z * jnp.mean(dz * z, axis=-1, keepdims=True)
    )
    dattn = dattn.astype(BF16)
    do_ref[...] = dattn
    dot_ref[...] = dattn.T


def attend(idx, acts, slopes, kv, dy):
    rows = dy.shape[0]
    nblk = rows // BLK
    rowblk = pl.BlockSpec((BLK, WIDE), lambda b, _: (b, 0))
    colblk = pl.BlockSpec((WIDE, BLK), lambda b, _: (0, b))
    scores = pl.BlockSpec((1, HEADS, BLK, 4 * BLK), lambda b, _: (b, 0, 0, 0))
    return pl.pallas_call(
        fwd_kernel,
        grid_spec=pltpu.PrefetchScalarGridSpec(
            num_scalar_prefetch=1,
            grid=(nblk,),
            in_specs=[
                pl.BlockSpec((BLK, WIDE), lambda b, _: (b, 1)),
                rowblk,
                rowblk,
                whole(kv.shape),
                rowblk,
            ],
            out_specs=[scores, scores, rowblk, colblk, rowblk, rowblk, colblk, colblk],
            scratch_shapes=[pltpu.VMEM((BLK, WIDE), F32)],
        ),
        out_shape=[
            sds((nblk, HEADS, BLK, 4 * BLK), BF16),
            sds((nblk, HEADS, BLK, 4 * BLK), BF16),
            sds((rows, WIDE), BF16),
            sds((WIDE, rows), BF16),
            sds((rows, WIDE), BF16),
            sds((rows, WIDE), BF16),
            sds((WIDE, rows), BF16),
            sds((WIDE, rows), BF16),
        ],
        compiler_params=params("arbitrary"),
        name="attend",
    )(idx, acts, acts, slopes, kv, dy)


def early_kernel(yt_ref, grad_ref, nt_ref, dpu_ref, x_ref, y_ref, wo_ref, gwo_ref, gwu_ref, ev_ref):
    gwo_ref[...] = nn(yt_ref[...], grad_ref[...]).astype(BF16)
    gwu_ref[...] = nn(nt_ref[...], dpu_ref[...]).astype(BF16)
    ev_ref[...] = (x_ref[...].astype(F32) + nn(y_ref[...], wo_ref[...])).astype(BF16)


def early(yt, grad_out, normed_t, dpu, x, y, w_out):
    rows = x.shape[0]
    tile = pl.BlockSpec((256, rows), lambda i: (i, 0))
    wide = pl.BlockSpec((256, WIDE), lambda i: (i, 0))
    small = pl.BlockSpec((rows // 4, WIDE), lambda i: (i, 0))
    return pl.pallas_call(
        early_kernel,
        grid=(4,),
        in_specs=[
            tile, whole(grad_out.shape), tile, whole(dpu.shape), small, small, whole(w_out.shape)
        ],
        out_specs=[wide, wide, small],
        out_shape=[sds((WIDE, WIDE), BF16), sds((WIDE, WIDE), BF16), sds((rows, WIDE), BF16)],
        compiler_params=params("arbitrary"),
        name="early_grads",
    )(yt, grad_out, normed_t, dpu, x, y, w_out)


def bwd_kernel(
    idx_ref, w_ref, g_ref, kv_ref, do_ref, dot_ref, qt_ref, qslope_ref, sown_ref, swin_ref,
    dpq_ref, dpt_ref, acc_ref,
):
    blk = pl.program_id(0)

    @pl.when(blk == 0)
    def _():
        acc_ref[...] = jnp.zeros_like(acc_ref)

    for pair in range(HEADS // 2):
        outs = []
        for half in range(2):
            head = 2 * pair + half
            at = head * HD
            dhead = do_ref[:, at : at + HD]
            dhead_t = dot_ref[at : at + HD, :]
            query_t = qt_ref[at : at + HD, :]
            keys = slot_rows(kv_ref, idx_ref, blk, WIDE + at)
            vals = slot_rows(kv_ref, idx_ref, blk, at)
            total = None
            for duo in range(2):
                span = slice(duo * 256, duo * 256 + 256)
                dw = nn(dhead, jnp.concatenate(vals[2 * duo : 2 * duo + 2], axis=1))
                ds = (dw * g_ref[0, head, :, span].astype(F32)).astype(BF16)
                part = nt(ds, jnp.concatenate(keys[2 * duo : 2 * duo + 2], axis=1))
                total = part if total is None else total + part
                dk = nn(query_t, ds)
                dv = nn(dhead_t, w_ref[0, head, :, span])
                for side in range(2):
                    place = idx_ref[blk, 2 * duo + side]
                    lanes = slice(side * BLK, side * BLK + BLK)
                    acc_ref[place, at : at + HD, :] += dv[:, lanes]
                    acc_ref[place, WIDE + at : WIDE + at + HD, :] += dk[:, lanes]
            outs.append(total)
        lanes = slice(pair * 128, pair * 128 + 128)
        dq = jnp.concatenate(outs, axis=1) * (HD ** (-0.5) / (2 * BLK))
        dpq_ref[:, lanes] = (dq * qslope_ref[:, lanes].astype(F32)).astype(BF16)

    @pl.when(blk == pl.num_programs(0) - 1)
    def _():
        for place in range(acc_ref.shape[0]):
            lanes = slice(place * BLK, place * BLK + BLK)
            if place < 8:
                slope = swin_ref[:, lanes]
            else:
                slope = sown_ref[:, (place - 8) * BLK : (place - 7) * BLK]
            dpt_ref[:, lanes] = (acc_ref[place] * (1.0 / BLK) * slope.astype(F32)).astype(BF16)


def attend_back(idx, w, g, kv, do, do_t, q_t, slopes, slope_own, slope_win):
    rows = do.shape[0]
    nblk = rows // BLK
    rowblk = pl.BlockSpec((BLK, WIDE), lambda b, _: (b, 0))
    colblk = pl.BlockSpec((WIDE, BLK), lambda b, _: (0, b))
    scores = pl.BlockSpec((1, HEADS, BLK, 4 * BLK), lambda b, _: (b, 0, 0, 0))
    return pl.pallas_call(
        bwd_kernel,
        grid_spec=pltpu.PrefetchScalarGridSpec(
            num_scalar_prefetch=1,
            grid=(nblk,),
            in_specs=[
                scores, scores, whole(kv.shape), rowblk, colblk, colblk,
                pl.BlockSpec((BLK, WIDE), lambda b, _: (b, 1)),
                whole(slope_own.shape), whole(slope_win.shape),
            ],
            out_specs=[rowblk, whole((2 * WIDE, 3 * rows))],
            scratch_shapes=[pltpu.VMEM(kv.shape, F32)],
        ),
        out_shape=[sds((rows, WIDE), BF16), sds((2 * WIDE, 3 * rows), BF16)],
        compiler_params=params("arbitrary"),
        name="attend_back",
    )(idx, w, g, kv, do, do_t, q_t, slopes, slope_own, slope_win)


def dn_kernel(w_ref, dpu_ref, dpq_ref, dpt_ref, far_ref, near_ref, own_ref):
    rows = dpu_ref.shape[0]
    w_u = w_ref[:, :WIDE]
    w_v = w_ref[:, WIDE : 2 * WIDE]
    w_q = w_ref[:, 2 * WIDE : 3 * WIDE]
    w_k = w_ref[:, 3 * WIDE :]
    for at, ref in enumerate((far_ref, near_ref, own_ref)):
        lanes = slice(at * rows, at * rows + rows)
        val = nn(w_v, dpt_ref[:WIDE, lanes]) + nn(w_k, dpt_ref[WIDE:, lanes])
        if ref is own_ref:
            val = val + nt(w_u, dpu_ref[...]) + nt(w_q, dpq_ref[...])
        ref[...] = val.astype(ref.dtype)


def grad_normed(w_in, dpu, dpq, dpt):
    rows = dpu.shape[0]
    out = pl.BlockSpec((256, rows), lambda i: (i, 0))
    return pl.pallas_call(
        dn_kernel,
        grid=(4,),
        in_specs=[
            pl.BlockSpec((256, 4 * WIDE), lambda i: (i, 0)),
            whole(dpu.shape), whole(dpq.shape), whole(dpt.shape),
        ],
        out_specs=[out, out, out],
        out_shape=[sds((WIDE, rows), BF16), sds((WIDE, rows), BF16), sds((WIDE, rows), F32)],
        compiler_params=params("arbitrary"),
        name="grad_normed",
    )(w_in, dpu, dpq, dpt)


def late_kernel(nown_ref, nwin_ref, dpq_ref, dpt_ref, out_ref):
    wins = nwin_ref.shape[1]
    for at, lo in ((0, 0), (2, WIDE)):
        val = nt(nwin_ref[...], dpt_ref[lo : lo + WIDE, :wins])
        val = val + nt(nown_ref[...], dpt_ref[lo : lo + WIDE, wins:])
        out_ref[:, at * WIDE : (at + 1) * WIDE] = val.astype(BF16)
    out_ref[:, WIDE : 2 * WIDE] = nn(nown_ref[...], dpq_ref[...]).astype(BF16)


def late(normed_own, normed_win, dpq, dpt):
    return pl.pallas_call(
        late_kernel,
        grid=(4,),
        in_specs=[
            pl.BlockSpec((256, normed_own.shape[1]), lambda i: (i, 0)),
            pl.BlockSpec((256, normed_win.shape[1]), lambda i: (i, 0)),
            whole(dpq.shape), whole(dpt.shape),
        ],
        out_specs=pl.BlockSpec((256, 3 * WIDE), lambda i: (i, 0)),
        out_shape=sds((WIDE, 3 * WIDE), BF16),
        compiler_params=params("arbitrary"),
        name="late_grads",
    )(normed_own, normed_win, dpq, dpt)


def last_kernel(own_ref, near_ref, far_ref, x_ref, grad_ref, out_ref):
    dn_t = own_ref[...] + near_ref[...].astype(F32) + far_ref[...].astype(F32)
    dn = dn_t.T
    cent, rstd = norm_parts(x_ref[...].astype(F32))
    z = cent * rstd
    dx = rstd * (
        dn - jnp.mean(dn, axis=-1, keepdims=True) - z * jnp.mean(dn * z, axis=-1, keepdims=True)
    )
    out_ref[...] = (grad_ref[...].astype(F32) + dx).astype(BF16)


def last(own, near, far, x, grad_out):
    rows = x.shape[0]
    colblk = pl.BlockSpec((WIDE, BLK), lambda b: (0, b))
    rowblk = pl.BlockSpec((BLK, WIDE), lambda b: (b, 0))
    return pl.pallas_call(
        last_kernel,
        grid=(rows // BLK,),
        in_specs=[colblk, colblk, colblk, rowblk, rowblk],
        out_specs=rowblk,
        out_shape=sds((rows, WIDE), BF16),
        compiler_params=params("arbitrary"),
        name="grad_x",
    )(own, near, far, x, grad_out)


def send(array, pairs):
    return lax.ppermute(array, "seq", pairs)


def on_device(events_in, w_in, w_out, kv_list, counts, grad_out):
    size = lax.axis_size("seq")
    nblk = kv_list.shape[0]
    first = lax.axis_index("seq") * nblk
    up = [(i, i + 1) for i in range(size - 1)]
    up_even = [(i, i + 2) for i in range(0, size - 2, 2)]
    across = [(i, i + 1) for i in range(0, size, 2)]
    x_near = send(events_in, up)
    x_even = send(events_in, up_even)
    x_odd = send(x_near, across)
    odd = lax.axis_index("seq") % 2
    x_far = jnp.where(odd == 1, x_odd, x_even)
    c_near = send(counts, up)
    c_far = send(counts, [(i, i + 2) for i in range(size - 2)])
    counts_win = jnp.concatenate([c_far, c_near, counts])
    local = jnp.arange(nblk, dtype=jnp.int32)
    index = jnp.concatenate([kv_list - first + BACK * nblk, (local + BACK * nblk)[:, None]], axis=1)
    index = jnp.clip(index, 0, (BACK + 1) * nblk - 1)

    w_kv_t = jnp.concatenate([w_in[:, WIDE : 2 * WIDE].T, w_in[:, 3 * WIDE :].T], axis=0)
    acts, slopes = project_uq(events_in, w_in)
    dy = back_out(grad_out, w_out)
    kv, slope_own, normed_own = project_kv_own(counts_win, events_in, w_kv_t)
    kv, slope_win, normed_win = project_kv_window(counts_win, x_far, x_near, w_kv_t, kv)
    w, g, y, y_t, dpu, do, do_t, q_t = attend(index, acts, slopes, kv, dy)
    gwo, gwu, events_out = early(y_t, grad_out, normed_own, dpu, events_in, y, w_out)
    early_sum = lax.psum_scatter(
        jnp.concatenate([gwo, gwu], axis=1), "seq", scatter_dimension=0, tiled=True
    )
    dpq, dpt = attend_back(index, w, g, kv, do, do_t, q_t, slopes, slope_own, slope_win)
    far, near, own = grad_normed(w_in, dpu, dpq, dpt)
    far_in = send(far, [(i + 2, i) for i in range(size - 2)])
    near_in = send(near, [(i + 1, i) for i in range(size - 1)])
    late_sum = lax.psum_scatter(
        late(normed_own, normed_win, dpq, dpt), "seq", scatter_dimension=0, tiled=True
    )
    grad_x = last(own, near_in, far_in, events_in, grad_out)
    grad_w_in = jnp.concatenate([early_sum[:, WIDE:], late_sum], axis=1).astype(F32)
    grad_w_out = early_sum[:, :WIDE].astype(F32)
    return (events_out, grad_x, grad_w_in, grad_w_out)


def solution(mesh):
    rows = P(("grp", "seq"), None)
    return jax.shard_map(
        on_device,
        mesh=mesh,
        in_specs=(rows, P(), P(), rows, P(("grp", "seq")), rows),
        out_specs=(rows, rows, rows, rows),
        check_vma=False,
    )
```

```python
import jax
import jax.numpy as jnp
from jax import lax
from jax.experimental import pallas as pl
from jax.experimental.pallas import tpu as pltpu
from jax.sharding import PartitionSpec as P

HEADS = 16
HD = 64
BLK = 128
WIDE = 1024
BACK = 2
EPS = 1e-05
F32 = jnp.float32
BF16 = jnp.bfloat16
VMEM_LIMIT = 60 * 1024 * 1024


def nn(left, right):
    return lax.dot_general(left, right, (((1,), (0,)), ((), ())), preferred_element_type=F32)


def nt(left, right):
    return lax.dot_general(left, right, (((1,), (1,)), ((), ())), preferred_element_type=F32)


def params(*kinds):
    return pltpu.CompilerParams(dimension_semantics=kinds or None, vmem_limit_bytes=VMEM_LIMIT)


def whole(shape):
    zeros = (0,) * len(shape)
    return pl.BlockSpec(shape, lambda *_: zeros, pipeline_mode=pl.Buffered(1))


def sds(shape, dtype):
    return jax.ShapeDtypeStruct(shape, dtype)


def norm_parts(rows):
    mean = jnp.mean(rows, axis=-1, keepdims=True)
    cent = rows - mean
    var = jnp.mean(cent * cent, axis=-1, keepdims=True)
    return cent, lax.rsqrt(var + EPS)


def normed_of(x):
    cent, rstd = norm_parts(x.astype(F32))
    return (cent * rstd).astype(BF16)


def silu_both(pre):
    t = jnp.tanh(0.5 * pre)
    sig = 0.5 + 0.5 * t
    act = pre * sig
    slope = sig + act * (0.5 - 0.5 * t)
    return act, slope


def uq_kernel(x_ref, w_ref, acts_ref, slope_ref, normed_ref):
    step = pl.program_id(0)

    @pl.when(step == 0)
    def _():
        normed_ref[...] = normed_of(x_ref[...])

    scale = jnp.where(step >= 2, HD ** (-0.5) * 0.5, 1.0).astype(F32)
    act, slope = silu_both(nn(normed_ref[...], w_ref[...]))
    acts_ref[...] = (act * scale).astype(BF16)
    slope_ref[...] = slope.astype(BF16)


def project_uq(x, w_in):
    rows = x.shape[0]
    out = pl.BlockSpec((rows, 512), lambda j: (0, j))
    return pl.pallas_call(
        uq_kernel,
        grid=(4,),
        in_specs=[whole(x.shape), pl.BlockSpec((WIDE, 512), lambda j: (0, j + 2 * (j // 2)))],
        out_specs=[out, out],
        out_shape=[sds((rows, 2 * WIDE), BF16)] * 2,
        scratch_shapes=[pltpu.VMEM((rows, WIDE), BF16)],
        compiler_params=params("arbitrary"),
        name="project_uq",
    )(x, w_in)


def kv_tile(w_t, normed_t_ref, kv_ref, slope_ref, counts_ref):
    act, slope = silu_both(nn(w_t, normed_t_ref[...]))
    slope_ref[...] = slope.astype(BF16)
    lane = lax.broadcasted_iota(jnp.int32, (1, BLK), 1)
    for place in range(act.shape[1] // BLK):
        part = act[:, place * BLK : (place + 1) * BLK]
        if counts_ref is not None:
            part = jnp.where(lane < counts_ref[place], part, 0.0)
        kv_ref[place] = part.astype(BF16)


def kv_own_kernel(counts_ref, x_ref, w_ref, kv_ref, slope_ref, normed_t_ref, w_t_ref):
    @pl.when(pl.program_id(0) == 0)
    def _():
        normed_t_ref[...] = normed_of(x_ref[...]).T

    w_t_ref[...] = w_ref[...].T
    kv_tile(w_t_ref[...], normed_t_ref, kv_ref, slope_ref, counts_ref)


def kv_win_kernel(
    odd_ref, x_even_ref, x_odd_ref, x_near_ref, w_ref, _, kv_ref, slope_ref, normed_t_ref
):
    rows = x_near_ref.shape[0]

    @pl.when(pl.program_id(0) == 0)
    def _():
        far = jnp.where(odd_ref[0] == 1, x_odd_ref[...].astype(F32), x_even_ref[...].astype(F32))
        normed_t_ref[:, :rows] = normed_of(far).T
        normed_t_ref[:, rows:] = normed_of(x_near_ref[...]).T

    kv_tile(w_ref[...], normed_t_ref, kv_ref, slope_ref, None)


def project_kv_own(counts, x, w_in):
    rows = x.shape[0]
    nblk = rows // BLK
    return pl.pallas_call(
        kv_own_kernel,
        grid_spec=pltpu.PrefetchScalarGridSpec(
            num_scalar_prefetch=1,
            grid=(4,),
            in_specs=[
                whole(x.shape),
                pl.BlockSpec((WIDE, 512), lambda j, _: (0, j + 2 + 2 * (j // 2))),
            ],
            out_specs=[
                pl.BlockSpec((nblk, 512, BLK), lambda j, _: (BACK, j, 0)),
                pl.BlockSpec((512, rows), lambda j, _: (j, 0)),
                whole((WIDE, rows)),
                pl.BlockSpec((512, WIDE), lambda j, _: (j, 0)),
            ],
        ),
        out_shape=[
            sds(((BACK + 1) * nblk, 2 * WIDE, BLK), BF16),
            sds((2 * WIDE, rows), BF16),
            sds((WIDE, rows), BF16),
            sds((2 * WIDE, WIDE), BF16),
        ],
        compiler_params=params("arbitrary"),
        name="project_kv_own",
    )(counts, x, w_in)


def project_kv_window(odd, x_even, x_odd, x_near, w_kv_t, kv):
    rows = x_near.shape[0]
    nblk = rows // BLK
    return pl.pallas_call(
        kv_win_kernel,
        grid_spec=pltpu.PrefetchScalarGridSpec(
            num_scalar_prefetch=1,
            grid=(2,),
            in_specs=[
                whole(x_near.shape),
                whole(x_near.shape),
                whole(x_near.shape),
                pl.BlockSpec((WIDE, WIDE), lambda j, _: (j, 0)),
                pl.BlockSpec(memory_space=pl.ANY),
            ],
            out_specs=[
                pl.BlockSpec((2 * nblk, WIDE, BLK), lambda j, _: (0, j, 0)),
                pl.BlockSpec((WIDE, 2 * rows), lambda j, _: (j, 0)),
                whole((WIDE, 2 * rows)),
            ],
        ),
        out_shape=[
            sds(kv.shape, BF16),
            sds((2 * WIDE, 2 * rows), BF16),
            sds((WIDE, 2 * rows), BF16),
        ],
        input_output_aliases={5: 0},
        compiler_params=params("arbitrary"),
        name="project_kv_window",
    )(odd, x_even, x_odd, x_near, w_kv_t, kv)


def dy_kernel(g_ref, w_ref, dy_ref):
    dy_ref[...] = nt(g_ref[...], w_ref[...])


def back_out(grad_out, w_out):
    rows = grad_out.shape[0]
    return pl.pallas_call(
        dy_kernel,
        grid=(2,),
        in_specs=[whole(grad_out.shape), pl.BlockSpec((512, WIDE), lambda j: (j, 0))],
        out_specs=pl.BlockSpec((rows, 512), lambda j: (0, j)),
        out_shape=sds((rows, WIDE), F32),
        compiler_params=params("arbitrary"),
        name="back_out",
    )(grad_out, w_out)


def slot_rows(kv_ref, idx_ref, blk, at):
    return [kv_ref[idx_ref[blk, slot], at : at + HD, :] for slot in range(4)]


def fwd_kernel(
    idx_ref, q_ref, u_ref, uslope_ref, kv_ref, dy_ref,
    w_ref, g_ref, y_ref, yt_ref, dpu_ref, do_ref, dot_ref, qt_ref, attn_ref,
):
    blk = pl.program_id(0)
    row = lax.broadcasted_iota(jnp.int32, (BLK, BLK), 0)
    col = lax.broadcasted_iota(jnp.int32, (BLK, BLK), 1)
    causal = col <= row
    qt_ref[...] = q_ref[...].T
    for pair in range(HEADS // 2):
        outs = []
        for half in range(2):
            head = 2 * pair + half
            query = q_ref[:, pair * 128 + half * HD : pair * 128 + half * HD + HD]
            keys = slot_rows(kv_ref, idx_ref, blk, WIDE + head * HD)
            vals = slot_rows(kv_ref, idx_ref, blk, head * HD)
            total = None
            for duo in range(2):
                s_half = nn(query, jnp.concatenate(keys[2 * duo : 2 * duo + 2], axis=1))
                t = jnp.tanh(s_half)
                p = 1.0 + t
                w = s_half * p
                g = p + w * (1.0 - t)
                if duo == 1:
                    keep = jnp.concatenate([jnp.full((BLK, BLK), True), causal], axis=1)
                    w = jnp.where(keep, w, 0.0)
                    g = jnp.where(keep, g, 0.0)
                w = w.astype(BF16)
                w_ref[0, head, :, duo * 256 : duo * 256 + 256] = w
                g_ref[0, head, :, duo * 256 : duo * 256 + 256] = g.astype(BF16)
                part = nt(w, jnp.concatenate(vals[2 * duo : 2 * duo + 2], axis=1))
                total = part if total is None else total + part
            outs.append(total)
        attn_ref[:, pair * 128 : pair * 128 + 128] = jnp.concatenate(outs, axis=1) * (1.0 / BLK)
    cent, rstd = norm_parts(attn_ref[...])
    z = cent * rstd
    u = u_ref[...].astype(F32)
    dy = dy_ref[...]
    y = (z * u).astype(BF16)
    y_ref[...] = y
    yt_ref[...] = y.T
    dpu_ref[...] = (dy * z * uslope_ref[...].astype(F32)).astype(BF16)
    dz = dy * u
    dattn = rstd * (
        dz - jnp.mean(dz, axis=-1, keepdims=True) - z * jnp.mean(dz * z, axis=-1, keepdims=True)
    )
    dattn = dattn.astype(BF16)
    do_ref[...] = dattn
    dot_ref[...] = dattn.T


def attend(idx, acts, slopes, kv, dy):
    rows = dy.shape[0]
    nblk = rows // BLK
    rowblk = pl.BlockSpec((BLK, WIDE), lambda b, _: (b, 0))
    colblk = pl.BlockSpec((WIDE, BLK), lambda b, _: (0, b))
    scores = pl.BlockSpec((1, HEADS, BLK, 4 * BLK), lambda b, _: (b, 0, 0, 0))
    return pl.pallas_call(
        fwd_kernel,
        grid_spec=pltpu.PrefetchScalarGridSpec(
            num_scalar_prefetch=1,
            grid=(nblk,),
            in_specs=[
                pl.BlockSpec((BLK, WIDE), lambda b, _: (b, 1)),
                rowblk,
                rowblk,
                whole(kv.shape),
                rowblk,
            ],
            out_specs=[scores, scores, rowblk, colblk, rowblk, rowblk, colblk, colblk],
            scratch_shapes=[pltpu.VMEM((BLK, WIDE), F32)],
        ),
        out_shape=[
            sds((nblk, HEADS, BLK, 4 * BLK), BF16),
            sds((nblk, HEADS, BLK, 4 * BLK), BF16),
            sds((rows, WIDE), BF16),
            sds((WIDE, rows), BF16),
            sds((rows, WIDE), BF16),
            sds((rows, WIDE), BF16),
            sds((WIDE, rows), BF16),
            sds((WIDE, rows), BF16),
        ],
        compiler_params=params("arbitrary"),
        name="attend",
    )(idx, acts, acts, slopes, kv, dy)


def put_split(core_ref, val, mine_ref, theirs_ref):
    pieces, height, cols = mine_ref.shape
    split = val.astype(BF16).reshape(pieces, 2, height, cols)

    @pl.when(core_ref[0] == 0)
    def _():
        mine_ref[...] = split[:, 0]
        theirs_ref[...] = split[:, 1]

    @pl.when(core_ref[0] != 0)
    def _():
        mine_ref[...] = split[:, 1]
        theirs_ref[...] = split[:, 0]


def early_kernel(
    core_ref, yt_ref, grad_ref, nt_ref, dpu_ref, x_ref, y_ref, wo_ref, mine_ref, theirs_ref, ev_ref
):
    step = pl.program_id(0)

    @pl.when(step < 2)
    def _():
        put_split(core_ref, nn(yt_ref[...], grad_ref[...]), mine_ref, theirs_ref)
        ev_ref[...] = (x_ref[...].astype(F32) + nn(y_ref[...], wo_ref[...])).astype(BF16)

    @pl.when(step >= 2)
    def _():
        put_split(core_ref, nn(nt_ref[...], dpu_ref[...]), mine_ref, theirs_ref)


def early(core, size, yt, grad_out, normed_t, dpu, x, y, w_out):
    rows = x.shape[0]
    first = pl.BlockSpec((rows, 512), lambda j, _: (0, jnp.minimum(j, 1)))
    second = pl.BlockSpec((rows, 512), lambda j, _: (0, jnp.maximum(j - 2, 0)))
    half = (size // 2, WIDE // size, 512)
    out = pl.BlockSpec(half, lambda j, _: (0, 0, j))
    shape = sds((size // 2, WIDE // size, 2 * WIDE), BF16)
    return pl.pallas_call(
        early_kernel,
        grid_spec=pltpu.PrefetchScalarGridSpec(
            num_scalar_prefetch=1,
            grid=(4,),
            in_specs=[
                whole(yt.shape), first, whole(normed_t.shape), second, first, whole(y.shape),
                pl.BlockSpec((WIDE, 512), lambda j, _: (0, jnp.minimum(j, 1))),
            ],
            out_specs=[out, out, first],
        ),
        out_shape=[shape, shape, sds((rows, WIDE), BF16)],
        compiler_params=params("arbitrary"),
        name="early_grads",
    )(core, yt, grad_out, normed_t, dpu, x, y, w_out)


def bwd_kernel(
    idx_ref, w_ref, g_ref, kv_ref, do_ref, dot_ref, qt_ref, qslope_ref, sown_ref, swin_ref,
    dpq_ref, dpt_ref, acc_ref,
):
    blk = pl.program_id(0)

    @pl.when(blk == 0)
    def _():
        acc_ref[...] = jnp.zeros_like(acc_ref)

    for pair in range(HEADS // 2):
        outs = []
        for half in range(2):
            head = 2 * pair + half
            at = head * HD
            dhead = do_ref[:, at : at + HD]
            dhead_t = dot_ref[at : at + HD, :]
            query_t = qt_ref[at : at + HD, :]
            keys = slot_rows(kv_ref, idx_ref, blk, WIDE + at)
            vals = slot_rows(kv_ref, idx_ref, blk, at)
            total = None
            for duo in range(2):
                span = slice(duo * 256, duo * 256 + 256)
                dw = nn(dhead, jnp.concatenate(vals[2 * duo : 2 * duo + 2], axis=1))
                ds = (dw * g_ref[0, head, :, span].astype(F32)).astype(BF16)
                part = nt(ds, jnp.concatenate(keys[2 * duo : 2 * duo + 2], axis=1))
                total = part if total is None else total + part
                dk = nn(query_t, ds)
                dv = nn(dhead_t, w_ref[0, head, :, span])
                for side in range(2):
                    place = idx_ref[blk, 2 * duo + side]
                    lanes = slice(side * BLK, side * BLK + BLK)
                    acc_ref[place, at : at + HD, :] += dv[:, lanes]
                    acc_ref[place, WIDE + at : WIDE + at + HD, :] += dk[:, lanes]
            outs.append(total)
        lanes = slice(pair * 128, pair * 128 + 128)
        dq = jnp.concatenate(outs, axis=1) * (HD ** (-0.5) / (2 * BLK))
        dpq_ref[:, lanes] = (dq * qslope_ref[:, lanes].astype(F32)).astype(BF16)

    @pl.when(blk == pl.num_programs(0) - 1)
    def _():
        for place in range(acc_ref.shape[0]):
            lanes = slice(place * BLK, place * BLK + BLK)
            if place < 8:
                slope = swin_ref[:, lanes]
            else:
                slope = sown_ref[:, (place - 8) * BLK : (place - 7) * BLK]
            dpt_ref[:, lanes] = (acc_ref[place] * (1.0 / BLK) * slope.astype(F32)).astype(BF16)


def attend_back(idx, w, g, kv, do, do_t, q_t, slopes, slope_own, slope_win):
    rows = do.shape[0]
    nblk = rows // BLK
    rowblk = pl.BlockSpec((BLK, WIDE), lambda b, _: (b, 0))
    colblk = pl.BlockSpec((WIDE, BLK), lambda b, _: (0, b))
    scores = pl.BlockSpec((1, HEADS, BLK, 4 * BLK), lambda b, _: (b, 0, 0, 0))
    return pl.pallas_call(
        bwd_kernel,
        grid_spec=pltpu.PrefetchScalarGridSpec(
            num_scalar_prefetch=1,
            grid=(nblk,),
            in_specs=[
                scores, scores, whole(kv.shape), rowblk, colblk, colblk,
                pl.BlockSpec((BLK, WIDE), lambda b, _: (b, 1)),
                whole(slope_own.shape), whole(slope_win.shape),
            ],
            out_specs=[rowblk, whole((2 * WIDE, 3 * rows))],
            scratch_shapes=[pltpu.VMEM(kv.shape, F32)],
        ),
        out_shape=[sds((rows, WIDE), BF16), sds((2 * WIDE, 3 * rows), BF16)],
        compiler_params=params("arbitrary"),
        name="attend_back",
    )(idx, w, g, kv, do, do_t, q_t, slopes, slope_own, slope_win)


def dn_kernel(w_ref, dpu_ref, dpq_ref, dpt_ref, far_ref, near_ref, own_ref, acc_ref):
    rows = dpu_ref.shape[0]
    step = pl.program_id(0)

    @pl.when(step == 0)
    def _():
        own_ref[...] = nt(w_ref[...], dpu_ref[...])

    @pl.when(step == 1)
    def _():
        own_ref[...] += nt(w_ref[...], dpq_ref[...])

    @pl.when(step == 2)
    def _():
        acc_ref[...] = nn(w_ref[...], dpt_ref[:, : 2 * rows])
        own_ref[...] += nn(w_ref[...], dpt_ref[:, 2 * rows :])

    @pl.when(step == 3)
    def _():
        val = acc_ref[...] + nn(w_ref[...], dpt_ref[:, : 2 * rows])
        far_ref[...] = val[:, :rows].astype(BF16)
        near_ref[...] = val[:, rows:].astype(BF16)
        own_ref[...] += nn(w_ref[...], dpt_ref[:, 2 * rows :])


def grad_normed(w_in, dpu, dpq, dpt):
    rows = dpu.shape[0]
    out = whole((WIDE, rows))
    return pl.pallas_call(
        dn_kernel,
        grid=(4,),
        in_specs=[
            pl.BlockSpec((WIDE, WIDE), lambda j: (0, 2 * (j % 2) + j // 2)),
            whole(dpu.shape), whole(dpq.shape),
            pl.BlockSpec((WIDE, 3 * rows), lambda j: (j // 3, 0)),
        ],
        out_specs=[out, out, out],
        out_shape=[sds((WIDE, rows), BF16), sds((WIDE, rows), BF16), sds((WIDE, rows), F32)],
        scratch_shapes=[pltpu.VMEM((WIDE, 2 * rows), F32)],
        compiler_params=params("arbitrary"),
        name="grad_normed",
    )(w_in, dpu, dpq, dpt)


def late_kernel(core_ref, nown_ref, nwin_ref, dpq_ref, dpt_ref, mine_ref, theirs_ref, *, start):
    wins = nwin_ref.shape[1]
    tile = pl.program_id(0) + start
    from_q = jnp.logical_and(tile >= 2, tile < 4)

    @pl.when(from_q)
    def _():
        put_split(core_ref, nn(nown_ref[...], dpq_ref[...]), mine_ref, theirs_ref)

    @pl.when(jnp.logical_not(from_q))
    def _():
        val = nt(nwin_ref[...], dpt_ref[:, :wins]) + nt(nown_ref[...], dpt_ref[:, wins:])
        put_split(core_ref, val, mine_ref, theirs_ref)


def late(core, size, start, count, normed_own, normed_win, dpq, dpt):
    rows = dpq.shape[0]
    out = pl.BlockSpec((size // 2, WIDE // size, 512), lambda j, _: (0, 0, j))
    shape = sds((size // 2, WIDE // size, 512 * count), BF16)

    def q_at(j, _):
        return (0, jnp.clip(j + start - 2, 0, 1))

    def t_at(j, _):
        tile = j + start
        return (jnp.where(tile < 2, tile, jnp.where(tile < 4, 1 if start < 2 else 2, tile - 2)), 0)

    return pl.pallas_call(
        lambda *refs: late_kernel(*refs, start=start),
        grid_spec=pltpu.PrefetchScalarGridSpec(
            num_scalar_prefetch=1,
            grid=(count,),
            in_specs=[
                whole(normed_own.shape), whole(normed_win.shape),
                pl.BlockSpec((rows, 512), q_at), pl.BlockSpec((512, 3 * rows), t_at),
            ],
            out_specs=[out, out],
        ),
        out_shape=[shape, shape],
        compiler_params=params("arbitrary"),
        name="late_grads_%d" % start,
    )(core, normed_own, normed_win, dpq, dpt)


def last_kernel(own_ref, a_ref, b_ref, c_ref, x_ref, grad_ref, out_ref):
    dn_t = own_ref[...] + a_ref[...].astype(F32) + b_ref[...].astype(F32) + c_ref[...].astype(F32)
    dn = dn_t.T
    cent, rstd = norm_parts(x_ref[...].astype(F32))
    z = cent * rstd
    dx = rstd * (
        dn - jnp.mean(dn, axis=-1, keepdims=True) - z * jnp.mean(dn * z, axis=-1, keepdims=True)
    )
    out_ref[...] = (grad_ref[...].astype(F32) + dx).astype(BF16)


def last(own, one, two, three, x, grad_out):
    rows = x.shape[0]
    colblk = pl.BlockSpec((WIDE, BLK), lambda b: (0, b))
    rowblk = pl.BlockSpec((BLK, WIDE), lambda b: (b, 0))
    return pl.pallas_call(
        last_kernel,
        grid=(rows // BLK,),
        in_specs=[colblk, colblk, colblk, colblk, rowblk, rowblk],
        out_specs=rowblk,
        out_shape=sds((rows, WIDE), BF16),
        compiler_params=params("arbitrary"),
        name="grad_x",
    )(own, one, two, three, x, grad_out)


def send(array, pairs):
    return lax.ppermute(array, "seq", pairs)


def sum_pieces(mine, theirs, size):
    place = lax.axis_index("seq")
    bits = size.bit_length() - 1
    keep, got = mine, send(theirs, [(i, i ^ 1) for i in range(size)])
    for bit in range(1, bits):
        half, height, cols = keep.shape
        shape = (half // 2, 2, height, cols)
        keep, got = keep.reshape(shape), got.reshape(shape)
        side = (place >> bit) & 1

        def added(which):
            parts = [
                lax.dynamic_index_in_dim(a, which, 1, keepdims=False).astype(F32)
                for a in (keep, got)
            ]
            return (parts[0] + parts[1]).astype(BF16)

        moved = send(added(1 - side), [(i, i ^ (1 << bit)) for i in range(size)])
        keep, got = added(side), moved
    return (keep.astype(F32) + got.astype(F32))[0]


def on_device(events_in, w_in, w_out, kv_list, counts, grad_out):
    size = lax.axis_size("seq")
    nblk = kv_list.shape[0]
    place = lax.axis_index("seq")
    core = (place % 2).astype(jnp.int32)[None]
    pairs = range(0, size, 2)
    live = jnp.arange(BLK, dtype=jnp.int32)[None, :] < counts[:, None]
    shown = jnp.where(live.reshape(-1)[:, None], events_in, jnp.zeros((), BF16))
    x_near = send(shown, [(i, i + 1) for i in range(size - 1)])
    x_even = send(shown, [(i, i + 2) for i in range(0, size - 2, 2)])
    x_odd = send(x_near, [(i, i + 1) for i in pairs])
    local = jnp.arange(nblk, dtype=jnp.int32)
    index = jnp.concatenate(
        [kv_list + (BACK - place) * nblk, (local + BACK * nblk)[:, None]], axis=1
    )
    index = jnp.clip(index, 0, (BACK + 1) * nblk - 1)

    acts, slopes = project_uq(events_in, w_in)
    dy = back_out(grad_out, w_out)
    kv, slope_own, normed_own, w_kv_t = project_kv_own(counts, events_in, w_in)
    kv, slope_win, normed_win = project_kv_window(core, x_even, x_odd, x_near, w_kv_t, kv)
    w, g, y, y_t, dpu, do, do_t, q_t = attend(index, acts, slopes, kv, dy)
    mine, theirs, events_out = early(
        core, size, y_t, grad_out, normed_own, dpu, events_in, y, w_out
    )
    sum_early = sum_pieces(mine, theirs, size)
    dpq, dpt = attend_back(index, w, g, kv, do, do_t, q_t, slopes, slope_own, slope_win)
    sums = [
        sum_pieces(*late(core, size, start, 3, normed_own, normed_win, dpq, dpt), size)
        for start in (0, 3)
    ]
    far, near, own = grad_normed(w_in, dpu, dpq, dpt)
    to_even = [(i + 1, i) for i in pairs]
    near_odd = send(near, to_even)
    far_odd = send(far, to_even)
    far_even = send(far, [(i + 2, i) for i in range(0, size - 2, 2)])
    joined = (near.astype(F32) + far_odd.astype(F32)).astype(BF16)
    joined = send(joined, [(i, i - 1) for i in range(2, size, 2)])
    grad_x = last(own, near_odd, far_even, joined, events_in, grad_out)
    grad_w_in = jnp.concatenate([sum_early[:, WIDE:], *sums], axis=1)
    return (events_out, grad_x, grad_w_in, sum_early[:, :WIDE])


def solution(mesh):
    rows = P(("grp", "seq"), None)
    return jax.shard_map(
        on_device,
        mesh=mesh,
        in_specs=(rows, P(), P(), rows, P(("grp", "seq")), rows),
        out_specs=(rows, rows, rows, rows),
        check_vma=False,
    )
```

```python
import jax
import jax.numpy as jnp
from jax import lax
from jax.experimental import pallas as pl
from jax.experimental.pallas import tpu as pltpu
from jax.sharding import PartitionSpec as P

HEADS = 16
HD = 64
BLK = 128
WIDE = 1024
BACK = 2
EPS = 1e-05
F32 = jnp.float32
BF16 = jnp.bfloat16
VMEM_LIMIT = 60 * 1024 * 1024


def nn(left, right):
    return lax.dot_general(left, right, (((1,), (0,)), ((), ())), preferred_element_type=F32)


def nt(left, right):
    return lax.dot_general(left, right, (((1,), (1,)), ((), ())), preferred_element_type=F32)


def params(*kinds):
    return pltpu.CompilerParams(dimension_semantics=kinds or None, vmem_limit_bytes=VMEM_LIMIT)


def cost(micros):
    return pl.CostEstimate(flops=int(micros * 1e9), transcendentals=0, bytes_accessed=1 << 20)


def tie(value, *others):
    return lax.optimization_barrier((value, *others))[0]


def whole(shape):
    zeros = (0,) * len(shape)
    return pl.BlockSpec(shape, lambda *_: zeros, pipeline_mode=pl.Buffered(1))


def sds(shape, dtype):
    return jax.ShapeDtypeStruct(shape, dtype)


def norm_parts(rows):
    mean = jnp.mean(rows, axis=-1, keepdims=True)
    cent = rows - mean
    var = jnp.mean(cent * cent, axis=-1, keepdims=True)
    return cent, lax.rsqrt(var + EPS)


def normed_of(x):
    cent, rstd = norm_parts(x.astype(F32))
    return (cent * rstd).astype(BF16)


def silu_both(pre):
    t = jnp.tanh(0.5 * pre)
    sig = 0.5 + 0.5 * t
    act = pre * sig
    slope = sig + act * (0.5 - 0.5 * t)
    return act, slope


def uq_kernel(x_ref, w_ref, acts_ref, slope_ref, normed_ref):
    step = pl.program_id(0)

    @pl.when(step == 0)
    def _():
        normed_ref[...] = normed_of(x_ref[...])

    scale = jnp.where(step >= 2, HD ** (-0.5) * 0.5, 1.0).astype(F32)
    act, slope = silu_both(nn(normed_ref[...], w_ref[...]))
    acts_ref[...] = (act * scale).astype(BF16)
    slope_ref[...] = slope.astype(BF16)


def project_uq(x, w_in):
    rows = x.shape[0]
    out = pl.BlockSpec((rows, 512), lambda j: (0, j))
    return pl.pallas_call(
        uq_kernel,
        grid=(4,),
        in_specs=[whole(x.shape), pl.BlockSpec((WIDE, 512), lambda j: (0, j + 2 * (j // 2)))],
        out_specs=[out, out],
        out_shape=[sds((rows, 2 * WIDE), BF16)] * 2,
        scratch_shapes=[pltpu.VMEM((rows, WIDE), BF16)],
        compiler_params=params("arbitrary"),
        name="project_uq",
        cost_estimate=cost(8),
    )(x, w_in)


def kv_tile(w_t, normed_t_ref, kv_ref, slope_ref, counts_ref):
    act, slope = silu_both(nn(w_t, normed_t_ref[...]))
    slope_ref[...] = slope.astype(BF16)
    lane = lax.broadcasted_iota(jnp.int32, (1, BLK), 1)
    for place in range(act.shape[1] // BLK):
        part = act[:, place * BLK : (place + 1) * BLK]
        if counts_ref is not None:
            part = jnp.where(lane < counts_ref[place], part, 0.0)
        kv_ref[place] = part.astype(BF16)


def kv_own_kernel(counts_ref, x_ref, w_ref, kv_ref, slope_ref, normed_t_ref, w_t_ref):
    @pl.when(pl.program_id(0) == 0)
    def _():
        normed_t_ref[...] = normed_of(x_ref[...]).T

    w_t_ref[...] = w_ref[...].T
    kv_tile(w_t_ref[...], normed_t_ref, kv_ref, slope_ref, counts_ref)


def kv_near_kernel(x_ref, w_ref, _, kv_ref, slope_ref, normed_t_ref):
    @pl.when(pl.program_id(0) == 0)
    def _():
        normed_t_ref[...] = normed_of(x_ref[...]).T

    kv_tile(w_ref[...], normed_t_ref, kv_ref, slope_ref, None)


def kv_far_kernel(x_even_ref, x_odd_ref, w_ref, _, kv_ref, slope_ref, normed_t_ref):
    @pl.when(pl.program_id(0) == 0)
    def _():
        far = x_odd_ref[...].astype(F32) + x_even_ref[...].astype(F32)
        normed_t_ref[...] = normed_of(far).T

    kv_tile(w_ref[...], normed_t_ref, kv_ref, slope_ref, None)


def project_kv_own(counts, x, w_in):
    rows = x.shape[0]
    nblk = rows // BLK
    return pl.pallas_call(
        kv_own_kernel,
        grid_spec=pltpu.PrefetchScalarGridSpec(
            num_scalar_prefetch=1,
            grid=(4,),
            in_specs=[
                whole(x.shape),
                pl.BlockSpec((WIDE, 512), lambda j, _: (0, j + 2 + 2 * (j // 2))),
            ],
            out_specs=[
                pl.BlockSpec((nblk, 512, BLK), lambda j, _: (BACK, j, 0)),
                pl.BlockSpec((512, rows), lambda j, _: (j, 0)),
                whole((WIDE, rows)),
                pl.BlockSpec((512, WIDE), lambda j, _: (j, 0)),
            ],
        ),
        out_shape=[
            sds(((BACK + 1) * nblk, 2 * WIDE, BLK), BF16),
            sds((2 * WIDE, rows), BF16),
            sds((WIDE, rows), BF16),
            sds((2 * WIDE, WIDE), BF16),
        ],
        compiler_params=params("arbitrary"),
        name="project_kv_own",
        cost_estimate=cost(10),
    )(counts, x, w_in)


def project_kv_window(name, kernel, group, xs, w_kv_t, kv):
    rows = xs[0].shape[0]
    nblk = rows // BLK
    return pl.pallas_call(
        kernel,
        grid=(4,),
        in_specs=[whole(x.shape) for x in xs]
        + [pl.BlockSpec((512, WIDE), lambda j: (j, 0)), pl.BlockSpec(memory_space=pl.ANY)],
        out_specs=[
            pl.BlockSpec((nblk, 512, BLK), lambda j: (group, j, 0)),
            pl.BlockSpec((512, rows), lambda j: (j, 0)),
            whole((WIDE, rows)),
        ],
        out_shape=[
            sds(kv.shape, BF16),
            sds((2 * WIDE, rows), BF16),
            sds((WIDE, rows), BF16),
        ],
        input_output_aliases={len(xs) + 1: 0},
        compiler_params=params("arbitrary"),
        name=name,
        cost_estimate=cost(7),
    )(*xs, w_kv_t, kv)


def dy_kernel(g_ref, w_ref, dy_ref):
    dy_ref[...] = nt(g_ref[...], w_ref[...])


def back_out(grad_out, w_out):
    rows = grad_out.shape[0]
    return pl.pallas_call(
        dy_kernel,
        grid=(2,),
        in_specs=[whole(grad_out.shape), pl.BlockSpec((512, WIDE), lambda j: (j, 0))],
        out_specs=pl.BlockSpec((rows, 512), lambda j: (0, j)),
        out_shape=sds((rows, WIDE), F32),
        compiler_params=params("arbitrary"),
        name="back_out",
        cost_estimate=cost(4),
    )(grad_out, w_out)


def slot_rows(kv_ref, idx_ref, blk, at):
    return [kv_ref[idx_ref[blk, slot], at : at + HD, :] for slot in range(4)]


def fwd_kernel(
    idx_ref, q_ref, u_ref, uslope_ref, kv_ref, dy_ref,
    w_ref, g_ref, y_ref, yt_ref, dpu_ref, do_ref, dot_ref, qt_ref, attn_ref,
):
    blk = pl.program_id(0)
    row = lax.broadcasted_iota(jnp.int32, (BLK, BLK), 0)
    col = lax.broadcasted_iota(jnp.int32, (BLK, BLK), 1)
    causal = col <= row
    qt_ref[...] = q_ref[...].T
    for pair in range(HEADS // 2):
        outs = []
        for half in range(2):
            head = 2 * pair + half
            query = q_ref[:, pair * 128 + half * HD : pair * 128 + half * HD + HD]
            keys = slot_rows(kv_ref, idx_ref, blk, WIDE + head * HD)
            vals = slot_rows(kv_ref, idx_ref, blk, head * HD)
            total = None
            for duo in range(2):
                s_half = nn(query, jnp.concatenate(keys[2 * duo : 2 * duo + 2], axis=1))
                t = jnp.tanh(s_half)
                p = 1.0 + t
                w = s_half * p
                g = p + w * (1.0 - t)
                if duo == 1:
                    keep = jnp.concatenate([jnp.full((BLK, BLK), True), causal], axis=1)
                    w = jnp.where(keep, w, 0.0)
                    g = jnp.where(keep, g, 0.0)
                w = w.astype(BF16)
                w_ref[0, head, :, duo * 256 : duo * 256 + 256] = w
                g_ref[0, head, :, duo * 256 : duo * 256 + 256] = g.astype(BF16)
                part = nt(w, jnp.concatenate(vals[2 * duo : 2 * duo + 2], axis=1))
                total = part if total is None else total + part
            outs.append(total)
        attn_ref[:, pair * 128 : pair * 128 + 128] = jnp.concatenate(outs, axis=1) * (1.0 / BLK)
    cent, rstd = norm_parts(attn_ref[...])
    z = cent * rstd
    u = u_ref[...].astype(F32)
    dy = dy_ref[...]
    y = (z * u).astype(BF16)
    y_ref[...] = y
    yt_ref[...] = y.T
    dpu_ref[...] = (dy * z * uslope_ref[...].astype(F32)).astype(BF16)
    dz = dy * u
    dattn = rstd * (
        dz - jnp.mean(dz, axis=-1, keepdims=True) - z * jnp.mean(dz * z, axis=-1, keepdims=True)
    )
    dattn = dattn.astype(BF16)
    do_ref[...] = dattn
    dot_ref[...] = dattn.T


def attend(idx, acts, slopes, kv, dy):
    rows = dy.shape[0]
    nblk = rows // BLK
    rowblk = pl.BlockSpec((BLK, WIDE), lambda b, _: (b, 0))
    colblk = pl.BlockSpec((WIDE, BLK), lambda b, _: (0, b))
    scores = pl.BlockSpec((1, HEADS, BLK, 4 * BLK), lambda b, _: (b, 0, 0, 0))
    return pl.pallas_call(
        fwd_kernel,
        grid_spec=pltpu.PrefetchScalarGridSpec(
            num_scalar_prefetch=1,
            grid=(nblk,),
            in_specs=[
                pl.BlockSpec((BLK, WIDE), lambda b, _: (b, 1)),
                rowblk,
                rowblk,
                whole(kv.shape),
                rowblk,
            ],
            out_specs=[scores, scores, rowblk, colblk, rowblk, rowblk, colblk, colblk],
            scratch_shapes=[pltpu.VMEM((BLK, WIDE), F32)],
        ),
        out_shape=[
            sds((nblk, HEADS, BLK, 4 * BLK), BF16),
            sds((nblk, HEADS, BLK, 4 * BLK), BF16),
            sds((rows, WIDE), BF16),
            sds((WIDE, rows), BF16),
            sds((rows, WIDE), BF16),
            sds((rows, WIDE), BF16),
            sds((WIDE, rows), BF16),
            sds((WIDE, rows), BF16),
        ],
        compiler_params=params("arbitrary"),
        name="attend",
        cost_estimate=cost(16),
    )(idx, acts, acts, slopes, kv, dy)


def put_split(core_ref, val, mine_ref, theirs_ref):
    pieces, height, cols = mine_ref.shape
    split = val.astype(BF16).reshape(pieces, 2, height, cols)

    @pl.when(core_ref[0] == 0)
    def _():
        mine_ref[...] = split[:, 0]
        theirs_ref[...] = split[:, 1]

    @pl.when(core_ref[0] != 0)
    def _():
        mine_ref[...] = split[:, 1]
        theirs_ref[...] = split[:, 0]


def early_kernel(core_ref, yt_ref, grad_ref, nt_ref, dpu_ref, mine_ref, theirs_ref):
    step = pl.program_id(0)

    @pl.when(step < 2)
    def _():
        put_split(core_ref, nn(yt_ref[...], grad_ref[...]), mine_ref, theirs_ref)

    @pl.when(step >= 2)
    def _():
        put_split(core_ref, nn(nt_ref[...], dpu_ref[...]), mine_ref, theirs_ref)


def early(core, size, yt, grad_out, normed_t, dpu):
    rows = grad_out.shape[0]
    first = pl.BlockSpec((rows, 512), lambda j, _: (0, jnp.minimum(j, 1)))
    second = pl.BlockSpec((rows, 512), lambda j, _: (0, jnp.maximum(j - 2, 0)))
    out = pl.BlockSpec((size // 2, WIDE // size, 512), lambda j, _: (0, 0, j))
    shape = sds((size // 2, WIDE // size, 2 * WIDE), BF16)
    return pl.pallas_call(
        early_kernel,
        grid_spec=pltpu.PrefetchScalarGridSpec(
            num_scalar_prefetch=1,
            grid=(4,),
            in_specs=[whole(yt.shape), first, whole(normed_t.shape), second],
            out_specs=[out, out],
        ),
        out_shape=[shape, shape],
        compiler_params=params("arbitrary"),
        name="early_grads",
        cost_estimate=cost(7),
    )(core, yt, grad_out, normed_t, dpu)


def events_kernel(x_ref, y_ref, wo_ref, ev_ref):
    ev_ref[...] = (x_ref[...].astype(F32) + nn(y_ref[...], wo_ref[...])).astype(BF16)


def events(x, y, w_out):
    rows = x.shape[0]
    tile = pl.BlockSpec((rows, 512), lambda j: (0, j))
    return pl.pallas_call(
        events_kernel,
        grid=(2,),
        in_specs=[tile, whole(y.shape), pl.BlockSpec((WIDE, 512), lambda j: (0, j))],
        out_specs=tile,
        out_shape=sds((rows, WIDE), BF16),
        compiler_params=params("arbitrary"),
        name="events_out",
        cost_estimate=cost(4),
    )(x, y, w_out)


def bwd_kernel(
    idx_ref, w_ref, g_ref, kv_ref, do_ref, dot_ref, qt_ref, qslope_ref, sfar_ref, snear_ref, sown_ref,
    dpq_ref, dpt_ref, acc_ref,
):
    blk = pl.program_id(0)

    @pl.when(blk == 0)
    def _():
        acc_ref[...] = jnp.zeros_like(acc_ref)

    for pair in range(HEADS // 2):
        outs = []
        for half in range(2):
            head = 2 * pair + half
            at = head * HD
            dhead = do_ref[:, at : at + HD]
            dhead_t = dot_ref[at : at + HD, :]
            query_t = qt_ref[at : at + HD, :]
            keys = slot_rows(kv_ref, idx_ref, blk, WIDE + at)
            vals = slot_rows(kv_ref, idx_ref, blk, at)
            total = None
            for duo in range(2):
                span = slice(duo * 256, duo * 256 + 256)
                dw = nn(dhead, jnp.concatenate(vals[2 * duo : 2 * duo + 2], axis=1))
                ds = (dw * g_ref[0, head, :, span].astype(F32)).astype(BF16)
                part = nt(ds, jnp.concatenate(keys[2 * duo : 2 * duo + 2], axis=1))
                total = part if total is None else total + part
                dk = nn(query_t, ds)
                dv = nn(dhead_t, w_ref[0, head, :, span])
                for side in range(2):
                    place = idx_ref[blk, 2 * duo + side]
                    lanes = slice(side * BLK, side * BLK + BLK)
                    acc_ref[place, at : at + HD, :] += dv[:, lanes]
                    acc_ref[place, WIDE + at : WIDE + at + HD, :] += dk[:, lanes]
            outs.append(total)
        lanes = slice(pair * 128, pair * 128 + 128)
        dq = jnp.concatenate(outs, axis=1) * (HD ** (-0.5) / (2 * BLK))
        dpq_ref[:, lanes] = (dq * qslope_ref[:, lanes].astype(F32)).astype(BF16)

    @pl.when(blk == pl.num_programs(0) - 1)
    def _():
        for place in range(acc_ref.shape[0]):
            lanes = slice(place * BLK, place * BLK + BLK)
            source = (sfar_ref, snear_ref, sown_ref)[place // 4]
            slope = source[:, (place % 4) * BLK : (place % 4 + 1) * BLK]
            dpt_ref[:, lanes] = (acc_ref[place] * (1.0 / BLK) * slope.astype(F32)).astype(BF16)


def attend_back(idx, w, g, kv, do, do_t, q_t, slopes, kv_slopes):
    rows = do.shape[0]
    nblk = rows // BLK
    rowblk = pl.BlockSpec((BLK, WIDE), lambda b, _: (b, 0))
    colblk = pl.BlockSpec((WIDE, BLK), lambda b, _: (0, b))
    scores = pl.BlockSpec((1, HEADS, BLK, 4 * BLK), lambda b, _: (b, 0, 0, 0))
    return pl.pallas_call(
        bwd_kernel,
        grid_spec=pltpu.PrefetchScalarGridSpec(
            num_scalar_prefetch=1,
            grid=(nblk,),
            in_specs=[
                scores, scores, whole(kv.shape), rowblk, colblk, colblk,
                pl.BlockSpec((BLK, WIDE), lambda b, _: (b, 1)),
                *(whole(a.shape) for a in kv_slopes),
            ],
            out_specs=[rowblk, whole((2 * WIDE, 3 * rows))],
            scratch_shapes=[pltpu.VMEM(kv.shape, F32)],
        ),
        out_shape=[sds((rows, WIDE), BF16), sds((2 * WIDE, 3 * rows), BF16)],
        compiler_params=params("arbitrary"),
        name="attend_back",
        cost_estimate=cost(28),
    )(idx, w, g, kv, do, do_t, q_t, slopes, *kv_slopes)


def dn_window_kernel(w_ref, dpt_ref, far_ref, near_ref, acc_ref):
    rows = far_ref.shape[1]

    @pl.when(pl.program_id(0) == 0)
    def _():
        acc_ref[...] = nn(w_ref[...], dpt_ref[...])

    @pl.when(pl.program_id(0) == 1)
    def _():
        val = acc_ref[...] + nn(w_ref[...], dpt_ref[...])
        far_ref[...] = val[:, :rows].astype(BF16)
        near_ref[...] = val[:, rows:].astype(BF16)


def grad_normed_window(w_in, dpt):
    rows = dpt.shape[1] // 3
    out = whole((WIDE, rows))
    return pl.pallas_call(
        dn_window_kernel,
        grid=(2,),
        in_specs=[
            pl.BlockSpec((WIDE, WIDE), lambda j: (0, 1 + 2 * j)),
            pl.BlockSpec((WIDE, 2 * rows), lambda j: (j, 0)),
        ],
        out_specs=[out, out],
        out_shape=[sds((WIDE, rows), BF16)] * 2,
        scratch_shapes=[pltpu.VMEM((WIDE, 2 * rows), F32)],
        compiler_params=params("arbitrary"),
        name="grad_normed_window",
        cost_estimate=cost(9),
    )(w_in, dpt)


def dn_own_kernel(w_ref, dpu_ref, dpq_ref, dpt_ref, own_ref):
    step = pl.program_id(0)

    @pl.when(step == 0)
    def _():
        own_ref[...] = nt(w_ref[...], dpu_ref[...])

    @pl.when(step == 1)
    def _():
        own_ref[...] += nt(w_ref[...], dpq_ref[...])

    @pl.when(step >= 2)
    def _():
        own_ref[...] += nn(w_ref[...], dpt_ref[...])


def grad_normed_own(w_in, dpu, dpq, dpt):
    rows = dpu.shape[0]
    return pl.pallas_call(
        dn_own_kernel,
        grid=(4,),
        in_specs=[
            pl.BlockSpec((WIDE, WIDE), lambda j: (0, 2 * (j % 2) + j // 2)),
            whole(dpu.shape), whole(dpq.shape),
            pl.BlockSpec((WIDE, rows), lambda j: (j // 3, 2)),
        ],
        out_specs=whole((WIDE, rows)),
        out_shape=sds((WIDE, rows), F32),
        compiler_params=params("arbitrary"),
        name="grad_normed_own",
        cost_estimate=cost(9),
    )(w_in, dpu, dpq, dpt)


def late_kernel(
    core_ref, nfar_ref, nnear_ref, nown_ref, dpq_ref, dpt_ref, mine_ref, theirs_ref, *, start
):
    rows = nown_ref.shape[1]
    tile = pl.program_id(0) + start
    from_q = jnp.logical_and(tile >= 2, tile < 4)

    @pl.when(from_q)
    def _():
        put_split(core_ref, nn(nown_ref[...], dpq_ref[...]), mine_ref, theirs_ref)

    @pl.when(jnp.logical_not(from_q))
    def _():
        val = nt(nfar_ref[...], dpt_ref[:, :rows]) + nt(nnear_ref[...], dpt_ref[:, rows : 2 * rows])
        val = val + nt(nown_ref[...], dpt_ref[:, 2 * rows :])
        put_split(core_ref, val, mine_ref, theirs_ref)


def late(core, size, start, count, normed, dpq, dpt):
    rows = dpq.shape[0]
    out = pl.BlockSpec((size // 2, WIDE // size, 512), lambda j, _: (0, 0, j))
    shape = sds((size // 2, WIDE // size, 512 * count), BF16)

    def q_at(j, _):
        return (0, jnp.clip(j + start - 2, 0, 1))

    def t_at(j, _):
        tile = j + start
        return (jnp.where(tile < 2, tile, jnp.where(tile < 4, 1 if start < 2 else 2, tile - 2)), 0)

    return pl.pallas_call(
        lambda *refs: late_kernel(*refs, start=start),
        grid_spec=pltpu.PrefetchScalarGridSpec(
            num_scalar_prefetch=1,
            grid=(count,),
            in_specs=[
                *(whole(a.shape) for a in normed),
                pl.BlockSpec((rows, 512), q_at), pl.BlockSpec((512, 3 * rows), t_at),
            ],
            out_specs=[out, out],
        ),
        out_shape=[shape, shape],
        compiler_params=params("arbitrary"),
        name="late_grads_%d" % start,
        cost_estimate=cost(8),
    )(core, *normed, dpq, dpt)


def last_kernel(own_ref, a_ref, b_ref, c_ref, x_ref, grad_ref, out_ref):
    dn_t = own_ref[...] + a_ref[...].astype(F32) + b_ref[...].astype(F32) + c_ref[...].astype(F32)
    dn = dn_t.T
    cent, rstd = norm_parts(x_ref[...].astype(F32))
    z = cent * rstd
    dx = rstd * (
        dn - jnp.mean(dn, axis=-1, keepdims=True) - z * jnp.mean(dn * z, axis=-1, keepdims=True)
    )
    out_ref[...] = (grad_ref[...].astype(F32) + dx).astype(BF16)


def last(own, one, two, three, x, grad_out):
    rows = x.shape[0]
    colblk = pl.BlockSpec((WIDE, BLK), lambda b: (0, b))
    rowblk = pl.BlockSpec((BLK, WIDE), lambda b: (b, 0))
    return pl.pallas_call(
        last_kernel,
        grid=(rows // BLK,),
        in_specs=[colblk, colblk, colblk, colblk, rowblk, rowblk],
        out_specs=rowblk,
        out_shape=sds((rows, WIDE), BF16),
        compiler_params=params("arbitrary"),
        name="grad_x",
        cost_estimate=cost(6),
    )(own, one, two, three, x, grad_out)


def send(array, pairs):
    return lax.ppermute(array, "seq", pairs)


class Halving:
    def __init__(self, mine, theirs, size, bits):
        self.size, self.bits, self.at = size, bits, 0
        self.left = list(range(1, size.bit_length() - 1))
        self.keep, self.got = mine, self.swap(theirs, 0)

    def swap(self, array, bit):
        return send(array, [(i, i ^ (1 << bit)) for i in range(self.size)])

    def step(self, *after):
        bit = self.bits[self.at]
        low = self.left.index(bit)
        self.at += 1
        count, height, cols = self.keep.shape
        inner = 1 << low
        shape = (count // (2 * inner), 2, inner * height, cols)
        keep, got = self.keep.reshape(shape), self.got.reshape(shape)
        if after:
            got = tie(got, *after)
        side = (lax.axis_index("seq") >> bit) & 1

        def added(which):
            parts = [lax.dynamic_index_in_dim(a, which, 1, keepdims=False) for a in (keep, got)]
            total = parts[0].astype(F32) + parts[1].astype(F32)
            return total.astype(BF16).reshape(count // 2, height, cols)

        moving = added(1 - side)
        self.keep, self.got = added(side), self.swap(moving, bit)
        self.left.remove(bit)
        return moving

    def finish(self):
        while self.at < len(self.bits):
            self.step()
        return (self.keep.astype(F32) + self.got.astype(F32))[0]


def on_device(events_in, w_in, w_out, kv_list, counts, grad_out):
    size = lax.axis_size("seq")
    nblk = kv_list.shape[0]
    place = lax.axis_index("seq")
    core = (place % 2).astype(jnp.int32)[None]
    pairs = range(0, size, 2)
    live = jnp.arange(BLK, dtype=jnp.int32)[None, :] < counts[:, None]
    shown = jnp.where(live.reshape(-1)[:, None], events_in, jnp.zeros((), BF16))
    x_near = send(shown, [(i, i + 1) for i in range(size - 1)])
    x_even = send(shown, [(i, i + 2) for i in range(0, size - 2, 2)])
    x_odd = send(x_near, [(i, i + 1) for i in pairs])
    local = jnp.arange(nblk, dtype=jnp.int32)
    index = jnp.concatenate(
        [kv_list + (BACK - place) * nblk, (local + BACK * nblk)[:, None]], axis=1
    )
    index = jnp.clip(index, 0, (BACK + 1) * nblk - 1)

    kv, slope_own, normed_own, w_kv_t = project_kv_own(counts, events_in, w_in)
    acts, slopes = project_uq(tie(events_in, w_kv_t), w_in)
    dy = back_out(tie(grad_out, acts), w_out)
    x_odd = send(tie(x_near, dy), [(i, i + 1) for i in pairs])
    kv, slope_near, normed_near = project_kv_window(
        "project_kv_near", kv_near_kernel, 1, [x_near], w_kv_t, tie(kv, dy)
    )
    kv, slope_far, normed_far = project_kv_window(
        "project_kv_far", kv_far_kernel, 0, [x_even, x_odd], w_kv_t, kv
    )
    w, g, y, y_t, dpu, do, do_t, q_t = attend(index, acts, slopes, kv, dy)
    ups = list(range(1, size.bit_length() - 1))
    sum_early = Halving(*early(core, size, y_t, grad_out, normed_own, dpu), size, ups)
    events_out = events(events_in, tie(y, sum_early.keep), w_out)
    sent = sum_early.step(events_out)
    normed = (normed_far, normed_near, normed_own)
    dpq, dpt = attend_back(
        tie(index, sent), w, g, kv, do, do_t, q_t, slopes, (slope_far, slope_near, slope_own)
    )
    sent = sum_early.step(dpq)
    first = Halving(*late(core, size, 0, 3, normed, tie(dpq, sent), dpt), size, ups)
    second = late(core, size, 3, 3, normed, tie(dpq, first.keep), dpt)
    sent = first.step(second[0])
    second = Halving(tie(second[0], sent), second[1], size, ups[1:] + ups[:1])
    far, near = grad_normed_window(w_in, tie(dpt, second.keep))
    to_even = [(i + 1, i) for i in pairs]
    near_odd = send(near, to_even)
    far_odd = send(far, to_even)
    far_even = send(far, [(i + 2, i) for i in range(0, size - 2, 2)])
    sent = second.step(near)
    early_sent = sum_early.step(sent)
    own = grad_normed_own(w_in, tie(dpu, early_sent), dpq, dpt)
    joined = (near.astype(F32) + tie(far_odd, early_sent).astype(F32)).astype(BF16)
    joined = send(joined, [(i, i - 1) for i in range(2, size, 2)])
    grad_x = last(own, near_odd, far_even, joined, events_in, grad_out)
    total = sum_early.finish()
    grad_w_in = jnp.concatenate([total[:, WIDE:], first.finish(), second.finish()], axis=1)
    return (events_out, grad_x, grad_w_in, total[:, :WIDE])


def solution(mesh):
    rows = P(("grp", "seq"), None)
    return jax.shard_map(
        on_device,
        mesh=mesh,
        in_specs=(rows, P(), P(), rows, P(("grp", "seq")), rows),
        out_specs=(rows, rows, rows, rows),
        check_vma=False,
    )
```

```python
import jax
import jax.numpy as jnp
from jax import lax
from jax.experimental import pallas as pl
from jax.experimental.pallas import tpu as pltpu
from jax.sharding import PartitionSpec as P

HEADS = 16
HD = 64
BLK = 128
WIDE = 1024
BACK = 2
EPS = 1e-05
F32 = jnp.float32
BF16 = jnp.bfloat16
VMEM_LIMIT = 60 * 1024 * 1024


def nn(left, right):
    return lax.dot_general(left, right, (((1,), (0,)), ((), ())), preferred_element_type=F32)


def nt(left, right):
    return lax.dot_general(left, right, (((1,), (1,)), ((), ())), preferred_element_type=F32)


def params(*kinds):
    return pltpu.CompilerParams(dimension_semantics=kinds or None, vmem_limit_bytes=VMEM_LIMIT)


def cost(micros):
    return pl.CostEstimate(flops=int(micros * 1e9), transcendentals=0, bytes_accessed=1 << 20)


def tie(value, *others):
    return lax.optimization_barrier((value, *others))[0]


def whole(shape):
    zeros = (0,) * len(shape)
    return pl.BlockSpec(shape, lambda *_: zeros, pipeline_mode=pl.Buffered(1))


def sds(shape, dtype):
    return jax.ShapeDtypeStruct(shape, dtype)


def norm_parts(rows):
    mean = jnp.mean(rows, axis=-1, keepdims=True)
    cent = rows - mean
    var = jnp.mean(cent * cent, axis=-1, keepdims=True)
    return cent, lax.rsqrt(var + EPS)


def normed_of(x):
    cent, rstd = norm_parts(x.astype(F32))
    return (cent * rstd).astype(BF16)


def halved(bf):
    return bf * jnp.asarray(0.5, BF16)


def silu_both(half):
    t = jnp.tanh(half)
    p = 1.0 + t
    act = half * p
    return act, p + act * (1.0 - t)


def uq_kernel(x_ref, w_ref, acts_ref, slope_ref, normed_ref):
    step = pl.program_id(0)

    @pl.when(step == 0)
    def _():
        normed_ref[...] = halved(normed_of(x_ref[...]))

    scale = jnp.where(step >= 2, HD ** (-0.5) * 0.5, 1.0).astype(F32)
    act, slope = silu_both(nn(normed_ref[...], w_ref[...]))
    acts_ref[...] = (act * scale).astype(BF16)
    slope_ref[...] = slope.astype(BF16)


def project_uq(x, w_in):
    rows = x.shape[0]
    out = pl.BlockSpec((rows, 512), lambda j: (0, j))
    return pl.pallas_call(
        uq_kernel,
        grid=(4,),
        in_specs=[whole(x.shape), pl.BlockSpec((WIDE, 512), lambda j: (0, j + 2 * (j // 2)))],
        out_specs=[out, out],
        out_shape=[sds((rows, 2 * WIDE), BF16)] * 2,
        scratch_shapes=[pltpu.VMEM((rows, WIDE), BF16)],
        compiler_params=params("arbitrary"),
        name="project_uq",
        cost_estimate=cost(8),
    )(x, w_in)


def kv_tile(w_t, normed_t_ref, kv_ref, slope_ref, counts_ref):
    act, slope = silu_both(0.5 * nn(w_t, normed_t_ref[...]))
    slope_ref[...] = slope.astype(BF16)
    lane = lax.broadcasted_iota(jnp.int32, (1, BLK), 1)
    for place in range(act.shape[1] // BLK):
        part = act[:, place * BLK : (place + 1) * BLK]
        if counts_ref is not None:
            part = jnp.where(lane < counts_ref[place], part, 0.0)
        kv_ref[place] = part.astype(BF16)


def kv_own_kernel(counts_ref, x_ref, w_ref, kv_ref, slope_ref, normed_t_ref, w_t_ref):
    @pl.when(pl.program_id(0) == 0)
    def _():
        normed_t_ref[...] = normed_of(x_ref[...]).T

    w_t_ref[...] = w_ref[...].T
    kv_tile(w_t_ref[...], normed_t_ref, kv_ref, slope_ref, counts_ref)


def kv_near_kernel(x_ref, w_ref, _kv, _slope, _normed, kv_ref, slope_ref, normed_t_ref):
    @pl.when(pl.program_id(0) == 0)
    def _():
        normed_t_ref[...] = normed_of(x_ref[...]).T

    kv_tile(w_ref[...], normed_t_ref, kv_ref, slope_ref, None)


def kv_far_kernel(
    x_even_ref, x_odd_ref, w_ref, _kv, _slope, _normed, kv_ref, slope_ref, normed_t_ref
):
    @pl.when(pl.program_id(0) == 0)
    def _():
        far = x_odd_ref[...].astype(F32) + x_even_ref[...].astype(F32)
        normed_t_ref[...] = normed_of(far).T

    kv_tile(w_ref[...], normed_t_ref, kv_ref, slope_ref, None)


def project_kv_own(counts, x, w_in):
    rows = x.shape[0]
    nblk = rows // BLK
    return pl.pallas_call(
        kv_own_kernel,
        grid_spec=pltpu.PrefetchScalarGridSpec(
            num_scalar_prefetch=1,
            grid=(4,),
            in_specs=[
                whole(x.shape),
                pl.BlockSpec((WIDE, 512), lambda j, _: (0, j + 2 + 2 * (j // 2))),
            ],
            out_specs=[
                pl.BlockSpec((nblk, 512, BLK), lambda j, _: (BACK, j, 0)),
                pl.BlockSpec((512, rows), lambda j, _: (j, BACK)),
                pl.BlockSpec((WIDE, rows), lambda j, _: (0, BACK)),
                pl.BlockSpec((512, WIDE), lambda j, _: (j, 0)),
            ],
        ),
        out_shape=[
            sds(((BACK + 1) * nblk, 2 * WIDE, BLK), BF16),
            sds((2 * WIDE, (BACK + 1) * rows), BF16),
            sds((WIDE, (BACK + 1) * rows), BF16),
            sds((2 * WIDE, WIDE), BF16),
        ],
        compiler_params=params("arbitrary"),
        name="project_kv_own",
        cost_estimate=cost(10),
    )(counts, x, w_in)


def project_kv_window(name, kernel, group, xs, w_kv_t, arrays):
    rows = xs[0].shape[0]
    nblk = rows // BLK
    return pl.pallas_call(
        kernel,
        grid=(4,),
        in_specs=[whole(x.shape) for x in xs]
        + [pl.BlockSpec((512, WIDE), lambda j: (j, 0))]
        + [pl.BlockSpec(memory_space=pl.ANY)] * 3,
        out_specs=[
            pl.BlockSpec((nblk, 512, BLK), lambda j: (group, j, 0)),
            pl.BlockSpec((512, rows), lambda j: (j, group)),
            pl.BlockSpec((WIDE, rows), lambda j: (0, group)),
        ],
        out_shape=[sds(a.shape, BF16) for a in arrays],
        input_output_aliases={len(xs) + 1 + i: i for i in range(3)},
        compiler_params=params("arbitrary"),
        name=name,
        cost_estimate=cost(7),
    )(*xs, w_kv_t, *arrays)


def dy_kernel(g_ref, w_ref, dy_ref):
    dy_ref[...] = nt(g_ref[...], w_ref[...])


def back_out(grad_out, w_out):
    rows = grad_out.shape[0]
    return pl.pallas_call(
        dy_kernel,
        grid=(2,),
        in_specs=[whole(grad_out.shape), pl.BlockSpec((512, WIDE), lambda j: (j, 0))],
        out_specs=pl.BlockSpec((rows, 512), lambda j: (0, j)),
        out_shape=sds((rows, WIDE), F32),
        compiler_params=params("arbitrary"),
        name="back_out",
        cost_estimate=cost(4),
    )(grad_out, w_out)


def duo_of(ref, idx_ref, blk, duo, rows):
    return jnp.concatenate([ref[idx_ref[blk, 2 * duo + i], rows, :] for i in range(2)], axis=1)


def diagonal(quad_rows):
    left = lax.broadcasted_iota(jnp.int32, (BLK, BLK), 1) < HD
    pairs = []
    for pair in range(2):
        lanes = slice(pair * BLK, pair * BLK + BLK)
        one = quad_rows[2 * pair * BLK : (2 * pair + 1) * BLK, lanes]
        two = quad_rows[(2 * pair + 1) * BLK : (2 * pair + 2) * BLK, lanes]
        pairs.append(jnp.where(left, one, two))
    return jnp.concatenate(pairs, axis=1)


def fwd_kernel(
    idx_ref, q_ref, v_ref, k_ref, u_ref, uslope_ref, dy_ref,
    w_ref, g_ref, qt_ref, y_ref, yt_ref, dpu_ref, do_ref, dot_ref, attn_ref,
):
    quad = pl.program_id(0)
    blk = pl.program_id(1)
    row = lax.broadcasted_iota(jnp.int32, (BLK, BLK), 0)
    col = lax.broadcasted_iota(jnp.int32, (BLK, BLK), 1)
    keep = jnp.concatenate([jnp.full((BLK, BLK), True), col <= row], axis=1)
    qt_ref[...] = q_ref[...].T
    total = None
    for duo in range(2):
        ws = []
        for head in range(4):
            rows = slice(head * HD, head * HD + HD)
            half = nn(q_ref[:, rows], duo_of(k_ref, idx_ref, blk, duo, rows))
            w, g = silu_both(half)
            if duo == 1:
                w = jnp.where(keep, w, 0.0)
                g = jnp.where(keep, g, 0.0)
            w = w.astype(BF16)
            ws.append(w)
            w_ref[0, head, :, duo * 256 : duo * 256 + 256] = w
            g_ref[0, head, :, duo * 256 : duo * 256 + 256] = g.astype(BF16)
        vals = duo_of(v_ref, idx_ref, blk, duo, slice(None))
        part = nt(jnp.concatenate(ws, axis=0), vals)
        total = part if total is None else total + part
    attn_ref[quad, blk] = diagonal(total) * (1.0 / BLK)

    @pl.when(quad == pl.num_programs(0) - 1)
    def _():
        attn = jnp.concatenate([attn_ref[i, blk] for i in range(4)], axis=1)
        cent, rstd = norm_parts(attn)
        z = cent * rstd
        u = u_ref[...].astype(F32)
        dy = dy_ref[...].astype(F32)
        y = (z * u).astype(BF16)
        y_ref[...] = y
        yt_ref[...] = y.T
        dpu_ref[...] = (dy * (0.5 * z) * uslope_ref[...].astype(F32)).astype(BF16)
        dz = dy * u
        dattn = rstd * (
            dz - jnp.mean(dz, axis=-1, keepdims=True) - z * jnp.mean(dz * z, axis=-1, keepdims=True)
        )
        dattn = dattn.astype(BF16)
        do_ref[...] = dattn
        dot_ref[...] = dattn.T


def attend(idx, acts, slopes, kv, dy):
    rows = dy.shape[0]
    nblk = rows // BLK
    places = kv.shape[0]
    final = HEADS // 4 - 1

    def at_end(i, b):
        return jnp.where(i == final, b, 0)

    rowblk = pl.BlockSpec((BLK, WIDE), lambda i, b, _: (at_end(i, b), 0))
    colblk = pl.BlockSpec((WIDE, BLK), lambda i, b, _: (0, at_end(i, b)))
    scores = pl.BlockSpec((1, 4, BLK, 4 * BLK), lambda i, b, _: (b, i, 0, 0))
    return pl.pallas_call(
        fwd_kernel,
        grid_spec=pltpu.PrefetchScalarGridSpec(
            num_scalar_prefetch=1,
            grid=(HEADS // 4, nblk),
            in_specs=[
                pl.BlockSpec((BLK, 256), lambda i, b, _: (b, 4 + i)),
                pl.BlockSpec((places, 256, BLK), lambda i, b, _: (0, i, 0)),
                pl.BlockSpec((places, 256, BLK), lambda i, b, _: (0, 4 + i, 0)),
                rowblk,
                rowblk,
                rowblk,
            ],
            out_specs=[
                scores, scores, pl.BlockSpec((256, BLK), lambda i, b, _: (i, b)),
                rowblk, colblk, rowblk, rowblk, colblk,
            ],
            scratch_shapes=[pltpu.VMEM((HEADS // 4, nblk, BLK, 256), F32)],
        ),
        out_shape=[
            sds((nblk, HEADS, BLK, 4 * BLK), BF16),
            sds((nblk, HEADS, BLK, 4 * BLK), BF16),
            sds((WIDE, rows), BF16),
            sds((rows, WIDE), BF16),
            sds((WIDE, rows), BF16),
            sds((rows, WIDE), BF16),
            sds((rows, WIDE), BF16),
            sds((WIDE, rows), BF16),
        ],
        compiler_params=params("arbitrary", "arbitrary"),
        name="attend",
        cost_estimate=cost(14),
    )(idx, acts, kv, kv, acts, slopes, dy)


def put_split(core_ref, val, mine_ref, theirs_ref, group=0):
    _, pieces, height, cols = mine_ref.shape
    split = val.astype(BF16).reshape(pieces, 2, height, cols)

    @pl.when(core_ref[0] == 0)
    def _():
        mine_ref[group] = split[:, 0]
        theirs_ref[group] = split[:, 1]

    @pl.when(core_ref[0] != 0)
    def _():
        mine_ref[group] = split[:, 1]
        theirs_ref[group] = split[:, 0]


def early_kernel(core_ref, yt_ref, grad_ref, nt_ref, dpu_ref, mine_ref, theirs_ref):
    step = pl.program_id(0)

    @pl.when(step < 2)
    def _():
        put_split(core_ref, nn(yt_ref[...], grad_ref[...]), mine_ref, theirs_ref)

    @pl.when(step >= 2)
    def _():
        put_split(core_ref, nn(nt_ref[...], dpu_ref[...]), mine_ref, theirs_ref)


def early(core, size, yt, grad_out, normed_t, dpu):
    rows = grad_out.shape[0]
    first = pl.BlockSpec((rows, 512), lambda j, _: (0, jnp.minimum(j, 1)))
    second = pl.BlockSpec((rows, 512), lambda j, _: (0, jnp.maximum(j - 2, 0)))
    out = pl.BlockSpec((1, size // 2, WIDE // size, 512), lambda j, _: (j // 2, 0, 0, j % 2))
    shape = sds((2, size // 2, WIDE // size, WIDE), BF16)
    return pl.pallas_call(
        early_kernel,
        grid_spec=pltpu.PrefetchScalarGridSpec(
            num_scalar_prefetch=1,
            grid=(4,),
            in_specs=[
                whole(yt.shape),
                first,
                pl.BlockSpec((WIDE, rows), lambda j, _: (0, BACK), pipeline_mode=pl.Buffered(1)),
                second,
            ],
            out_specs=[out, out],
        ),
        out_shape=[shape, shape],
        compiler_params=params("arbitrary"),
        name="early_grads",
        cost_estimate=cost(7),
    )(core, yt, grad_out, normed_t, dpu)


def events_kernel(x_ref, y_ref, wo_ref, ev_ref):
    ev_ref[...] = (x_ref[...].astype(F32) + nn(y_ref[...], wo_ref[...])).astype(BF16)


def events(x, y, w_out):
    rows = x.shape[0]
    tile = pl.BlockSpec((rows, 512), lambda j: (0, j))
    return pl.pallas_call(
        events_kernel,
        grid=(2,),
        in_specs=[tile, whole(y.shape), pl.BlockSpec((WIDE, 512), lambda j: (0, j))],
        out_specs=tile,
        out_shape=sds((rows, WIDE), BF16),
        compiler_params=params("arbitrary"),
        name="events_out",
        cost_estimate=cost(4),
    )(x, y, w_out)


def bwd_kernel(*refs, first):
    (idx_ref, core_ref, w_ref, g_ref, v_ref, k_ref, do_ref, dot_ref, qt_ref, qslope_ref) = refs[:10]
    (vslope_ref, kslope_ref, normed_ref, wv_ref, wk_ref) = refs[10:15]
    rest = refs[15:]
    if first:
        part_ref = rest[5]
        rest = rest[:5] + rest[6:]
    else:
        part_ref, far_ref, near_ref = rest[0], rest[6], rest[7]
        rest = rest[1:6] + rest[8:]
    (mine_ref, theirs_ref, dpq_ref, dvt_ref, dkt_ref) = rest[:5]
    (dva_ref, dka_ref, dvb_ref, dkb_ref, sum_ref) = rest[5:]
    step = pl.program_id(0)
    blk = pl.program_id(1)
    rows = dpq_ref.shape[0]

    @pl.when(blk == 0)
    def _():
        dva_ref[...] = jnp.zeros_like(dva_ref)
        dka_ref[...] = jnp.zeros_like(dka_ref)

    total = None
    for duo in range(2):
        span = slice(duo * 256, duo * 256 + 256)
        dss = []
        for head in range(4):
            cols = slice(head * HD, head * HD + HD)
            dw = nn(do_ref[:, cols], duo_of(v_ref, idx_ref, blk, duo, cols))
            ds = (dw * g_ref[0, head, :, span].astype(F32)).astype(BF16)
            dss.append(ds)
            dk = nn(qt_ref[cols, :], ds)
            dv = nn(dot_ref[cols, :], w_ref[0, head, :, span])
            for side in range(2):
                place = idx_ref[blk, 2 * duo + side]
                lanes = slice(side * BLK, side * BLK + BLK)
                dva_ref[place, cols, :] += dv[:, lanes]
                dka_ref[place, cols, :] += dk[:, lanes]
        part = nt(jnp.concatenate(dss, axis=0), duo_of(k_ref, idx_ref, blk, duo, slice(None)))
        total = part if total is None else total + part
    dq = diagonal(total) * (HD ** (-0.5) / (4 * BLK))
    dpq_ref[pl.ds(pl.multiple_of(blk * BLK, BLK), BLK), :] = (
        dq * qslope_ref[...].astype(F32)
    ).astype(BF16)

    @pl.when(blk == pl.num_programs(1) - 1)
    def _():
        for place in range(dva_ref.shape[0]):
            lanes = slice(place * BLK, place * BLK + BLK)
            for acc_ref, slope_ref, out_ref in (
                (dva_ref, vslope_ref, dvb_ref),
                (dka_ref, kslope_ref, dkb_ref),
            ):
                out_ref[:, lanes] = (
                    acc_ref[place] * (0.5 / BLK) * slope_ref[:, lanes].astype(F32)
                ).astype(BF16)
        dvt_ref[...] = dvb_ref[:, BACK * rows :]
        dkt_ref[...] = dkb_ref[:, BACK * rows :]
        put_split(core_ref, nt(normed_ref[...], dvb_ref[...]), mine_ref, theirs_ref, 0)
        put_split(
            core_ref, nn(normed_ref[:, BACK * rows :], dpq_ref[...]), mine_ref, theirs_ref, 1
        )
        put_split(core_ref, nt(normed_ref[...], dkb_ref[...]), mine_ref, theirs_ref, 2)
        for at in range(BACK):
            lanes = slice(at * rows, at * rows + rows)
            add = nn(wv_ref[...], dvb_ref[:, lanes]) + nn(wk_ref[...], dkb_ref[:, lanes])

            @pl.when(step == 0)
            def _():
                sum_ref[at] = add if first else part_ref[at].astype(F32) + add

            @pl.when(step != 0)
            def _():
                done = (sum_ref[at] + add).astype(BF16)
                if first:
                    part_ref[at] = done
                else:
                    (far_ref, near_ref)[at][...] = done


def attend_back(start, idx, core, size, w, g, kv, do, do_t, q_t, slopes, kv_slopes, normed, w_in, part):
    rows = do.shape[0]
    nblk = rows // BLK
    places = kv.shape[0]
    first = part is None
    heads = pl.BlockSpec((1, 4, BLK, 4 * BLK), lambda i, b, *_: (b, start + i, 0, 0))
    tall = (BACK + 1) * rows
    wide = pl.BlockSpec((3, size // 2, WIDE // size, 256), lambda i, b, *_: (0, 0, 0, i))
    cols = pl.BlockSpec((256, rows), lambda i, b, *_: (i, 0))
    in_specs = [
        heads,
        heads,
        pl.BlockSpec((places, 256, BLK), lambda i, b, *_: (0, start + i, 0)),
        pl.BlockSpec((places, 256, BLK), lambda i, b, *_: (0, 4 + start + i, 0)),
        pl.BlockSpec((BLK, 256), lambda i, b, *_: (b, start + i)),
        pl.BlockSpec((256, BLK), lambda i, b, *_: (start + i, b)),
        pl.BlockSpec((256, BLK), lambda i, b, *_: (start + i, b)),
        pl.BlockSpec((BLK, 256), lambda i, b, *_: (b, 4 + start + i)),
        pl.BlockSpec((256, tall), lambda i, b, *_: (start + i, 0)),
        pl.BlockSpec((256, tall), lambda i, b, *_: (4 + start + i, 0)),
        whole(normed.shape),
        pl.BlockSpec((WIDE, 256), lambda i, b, *_: (0, 4 + start + i)),
        pl.BlockSpec((WIDE, 256), lambda i, b, *_: (0, 12 + start + i)),
    ]
    args = [idx, core, w, g, kv, kv, do, do_t, q_t, slopes, kv_slopes, kv_slopes, normed, w_in, w_in]
    chunk = sds((3, size // 2, WIDE // size, 512), BF16)
    out_specs = [wide, wide, pl.BlockSpec((rows, 256), lambda i, b, *_: (0, i)), cols, cols]
    out_shape = [chunk, chunk, sds((rows, 512), BF16), sds((512, rows), BF16), sds((512, rows), BF16)]
    if first:
        out_specs.append(whole((BACK, WIDE, rows)))
        out_shape.append(sds((BACK, WIDE, rows), BF16))
    else:
        in_specs.append(whole(part.shape))
        args.append(part)
        out_specs += [whole((WIDE, rows))] * 2
        out_shape += [sds((WIDE, rows), BF16)] * 2
    return pl.pallas_call(
        lambda *refs: bwd_kernel(*refs, first=first),
        grid_spec=pltpu.PrefetchScalarGridSpec(
            num_scalar_prefetch=2,
            grid=(2, nblk),
            in_specs=in_specs,
            out_specs=out_specs,
            scratch_shapes=[
                pltpu.VMEM((places, 256, BLK), F32),
                pltpu.VMEM((places, 256, BLK), F32),
                pltpu.VMEM((256, tall), BF16),
                pltpu.VMEM((256, tall), BF16),
                pltpu.VMEM((BACK, WIDE, rows), F32),
            ],
        ),
        out_shape=out_shape,
        compiler_params=params("arbitrary", "arbitrary"),
        name="attend_back_%d" % start,
        cost_estimate=cost(24),
    )(*args)


def dn_u_kernel(w_ref, dpu_ref, own_ref):
    own_ref[...] = nt(w_ref[...], dpu_ref[...])


def grad_normed_u(w_in, dpu):
    rows = dpu.shape[0]
    return pl.pallas_call(
        dn_u_kernel,
        grid=(2,),
        in_specs=[pl.BlockSpec((WIDE // 2, WIDE), lambda j: (j, 0)), whole(dpu.shape)],
        out_specs=pl.BlockSpec((WIDE // 2, rows), lambda j: (j, 0)),
        out_shape=sds((WIDE, rows), F32),
        compiler_params=params("arbitrary"),
        name="grad_normed_u",
        cost_estimate=cost(4),
    )(w_in, dpu)


def dn_own_kernel(w_ref, u_ref, qa_ref, qb_ref, va_ref, vb_ref, ka_ref, kb_ref, own_ref):
    step = pl.program_id(0)
    half = WIDE // 2
    left, right = w_ref[:, :half], w_ref[:, half:]

    @pl.when(step == 0)
    def _():
        own_ref[...] = u_ref[...] + nn(left, va_ref[...]) + nn(right, vb_ref[...])

    @pl.when(step == 1)
    def _():
        own_ref[...] += nt(left, qa_ref[...]) + nt(right, qb_ref[...])

    @pl.when(step == 2)
    def _():
        own_ref[...] += nn(left, ka_ref[...]) + nn(right, kb_ref[...])


def grad_normed_own(w_in, from_u, *halves):
    return pl.pallas_call(
        dn_own_kernel,
        grid=(3,),
        in_specs=[pl.BlockSpec((WIDE, WIDE), lambda j: (0, j + 1)), whole(from_u.shape)]
        + [whole(a.shape) for a in halves],
        out_specs=whole(from_u.shape),
        out_shape=sds(from_u.shape, F32),
        compiler_params=params("arbitrary"),
        name="grad_normed_own",
        cost_estimate=cost(8),
    )(w_in, from_u, *halves)


def last_kernel(own_ref, a_ref, b_ref, c_ref, x_ref, grad_ref, out_ref):
    dn_t = own_ref[...] + a_ref[...].astype(F32) + b_ref[...].astype(F32) + c_ref[...].astype(F32)
    dn = dn_t.T
    cent, rstd = norm_parts(x_ref[...].astype(F32))
    z = cent * rstd
    dx = rstd * (
        dn - jnp.mean(dn, axis=-1, keepdims=True) - z * jnp.mean(dn * z, axis=-1, keepdims=True)
    )
    out_ref[...] = (grad_ref[...].astype(F32) + dx).astype(BF16)


def last(own, one, two, three, x, grad_out):
    rows = x.shape[0]
    colblk = pl.BlockSpec((WIDE, BLK), lambda b: (0, b))
    rowblk = pl.BlockSpec((BLK, WIDE), lambda b: (b, 0))
    return pl.pallas_call(
        last_kernel,
        grid=(rows // BLK,),
        in_specs=[colblk, colblk, colblk, colblk, rowblk, rowblk],
        out_specs=rowblk,
        out_shape=sds((rows, WIDE), BF16),
        compiler_params=params("arbitrary"),
        name="grad_x",
        cost_estimate=cost(6),
    )(own, one, two, three, x, grad_out)


def send(array, pairs):
    return lax.ppermute(array, "seq", pairs)


class Halving:
    def __init__(self, mine, theirs, size, bits):
        self.size, self.bits, self.at = size, bits, 0
        self.left = list(range(1, size.bit_length() - 1))
        self.keep, self.got = mine, self.swap(theirs, 0)

    def swap(self, array, bit):
        return send(array, [(i, i ^ (1 << bit)) for i in range(self.size)])

    def step(self, *after):
        bit = self.bits[self.at]
        inner = 1 << self.left.index(bit)
        self.at += 1
        groups, count, height, cols = self.keep.shape
        shape = (groups, count // (2 * inner), 2, inner * height, cols)
        keep, got = self.keep.reshape(shape), self.got.reshape(shape)
        if after:
            got = tie(got, *after)
        side = (lax.axis_index("seq") >> bit) & 1

        def added(which):
            parts = [lax.dynamic_index_in_dim(a, which, 2, keepdims=False) for a in (keep, got)]
            total = parts[0].astype(F32) + parts[1].astype(F32)
            return total.astype(BF16).reshape(groups, count // 2, height, cols)

        moving = added(1 - side)
        self.keep, self.got = added(side), self.swap(moving, bit)
        self.left.remove(bit)
        return moving

    def parts(self):
        while self.at < len(self.bits):
            self.step()
        return self.keep, self.got


def finish_kernel(ek_ref, eg_ref, ak_ref, ag_ref, bk_ref, bg_ref, win_ref, wout_ref):
    def total(keep_ref, got_ref, group):
        return keep_ref[group, 0].astype(F32) + got_ref[group, 0].astype(F32)

    wout_ref[...] = total(ek_ref, eg_ref, 0)
    win_ref[:, :WIDE] = total(ek_ref, eg_ref, 1)
    for group in range(3):
        at = (group + 1) * WIDE
        win_ref[:, at : at + 512] = total(ak_ref, ag_ref, group)
        win_ref[:, at + 512 : at + WIDE] = total(bk_ref, bg_ref, group)


def finish(*sums):
    args = [a for pair in sums for a in pair]
    height = args[0].shape[2]
    return pl.pallas_call(
        finish_kernel,
        in_specs=[pl.BlockSpec(memory_space=pltpu.VMEM)] * 6,
        out_specs=[pl.BlockSpec(memory_space=pltpu.VMEM)] * 2,
        out_shape=[sds((height, 4 * WIDE), F32), sds((height, WIDE), F32)],
        compiler_params=params(),
        name="finish_sums",
        cost_estimate=cost(2),
    )(*args)


def on_device(events_in, w_in, w_out, kv_list, counts, grad_out):
    size = lax.axis_size("seq")
    nblk = kv_list.shape[0]
    place = lax.axis_index("seq")
    core = (place % 2).astype(jnp.int32)[None]
    pairs = range(0, size, 2)
    live = jnp.arange(BLK, dtype=jnp.int32)[None, :] < counts[:, None]
    shown = jnp.where(live.reshape(-1)[:, None], events_in, jnp.zeros((), BF16))
    x_near = send(shown, [(i, i + 1) for i in range(size - 1)])
    x_even = send(shown, [(i, i + 2) for i in range(0, size - 2, 2)])
    x_odd = send(x_near, [(i, i + 1) for i in pairs])
    local = jnp.arange(nblk, dtype=jnp.int32)
    index = jnp.concatenate(
        [kv_list + (BACK - place) * nblk, (local + BACK * nblk)[:, None]], axis=1
    )
    index = jnp.clip(index, 0, (BACK + 1) * nblk - 1)

    kv, kv_slopes, normed, w_kv_t = project_kv_own(counts, events_in, w_in)
    acts, slopes = project_uq(tie(events_in, w_kv_t), w_in)
    dy = back_out(tie(grad_out, acts), w_out)
    x_odd = send(tie(x_near, dy), [(i, i + 1) for i in pairs])
    arrays = (tie(kv, dy), kv_slopes, normed)
    arrays = project_kv_window("project_kv_near", kv_near_kernel, 1, [x_near], w_kv_t, arrays)
    arrays = project_kv_window("project_kv_far", kv_far_kernel, 0, [x_even, x_odd], w_kv_t, arrays)
    kv, kv_slopes, normed = arrays
    w, g, q_t, y, y_t, dpu, do, do_t = attend(index, acts, slopes, kv, dy)
    ups = list(range(1, size.bit_length() - 1))
    sum_early = Halving(*early(core, size, y_t, grad_out, normed, dpu), size, ups)
    events_out = events(events_in, tie(y, sum_early.keep), w_out)
    sent = sum_early.step(events_out)

    def backward(start, token, part):
        return attend_back(
            start, token, core, size, w, g, kv, do, do_t, q_t, slopes, kv_slopes, normed, w_in, part
        )

    mine, theirs, qa, va, ka, part = backward(0, tie(index, sent), None)
    sent = sum_early.step(qa)
    first = Halving(mine, tie(theirs, sent), size, ups)
    from_u = grad_normed_u(w_in, tie(dpu, first.keep, sent))
    sent = first.step(from_u)
    mine, theirs, qb, vb, kb, far, near = backward(2, tie(index, sent), part)
    to_even = [(i + 1, i) for i in pairs]
    far, near, mine, theirs, sum_early.got, first.got = lax.optimization_barrier(
        (far, near, mine, theirs, sum_early.got, first.got)
    )
    far_odd = send(far, to_even)
    far_even = send(far, [(i + 2, i) for i in range(0, size - 2, 2)])
    near_odd = send(near, to_even)
    second = Halving(mine, theirs, size, ups[1:] + ups[:1])
    joined = (near.astype(F32) + far_odd.astype(F32)).astype(BF16)
    sent = second.step(joined)
    back = send(joined, [(i, i - 1) for i in range(2, size, 2)])
    early_sent = sum_early.step(sent)
    first_sent = first.step(early_sent)
    own = grad_normed_own(w_in, tie(from_u, first_sent), qa, qb, va, vb, ka, kb)
    grad_x = last(own, near_odd, far_even, back, events_in, grad_out)
    grad_w_in, grad_w_out = finish(sum_early.parts(), first.parts(), second.parts())
    return (events_out, grad_x, grad_w_in, grad_w_out)


def solution(mesh):
    rows = P(("grp", "seq"), None)
    return jax.shard_map(
        on_device,
        mesh=mesh,
        in_specs=(rows, P(), P(), rows, P(("grp", "seq")), rows),
        out_specs=(rows, rows, rows, rows),
        check_vma=False,
    )
```

```python
import jax
import jax.numpy as jnp
from jax import lax
from jax.experimental import pallas as pl
from jax.experimental.pallas import tpu as pltpu
from jax.sharding import PartitionSpec as P

HEADS = 16
HD = 64
BLK = 128
WIDE = 1024
BACK = 2
EPS = 1e-05
F32 = jnp.float32
BF16 = jnp.bfloat16
MIB = 1024 * 1024


def nn(left, right):
    return lax.dot_general(left, right, (((1,), (0,)), ((), ())), preferred_element_type=F32)


def nt(left, right):
    return lax.dot_general(left, right, (((1,), (1,)), ((), ())), preferred_element_type=F32)


def params(mib):
    return pltpu.CompilerParams(dimension_semantics=("arbitrary",), vmem_limit_bytes=mib * MIB)


def cost(micros):
    return pl.CostEstimate(flops=int(micros * 1e9), transcendentals=0, bytes_accessed=1 << 20)


def tie(value, *others):
    return lax.optimization_barrier((value, *others))[0]


def whole(shape):
    zeros = (0,) * len(shape)
    return pl.BlockSpec(shape, lambda *_: zeros, pipeline_mode=pl.Buffered(1))


def sds(shape, dtype):
    return jax.ShapeDtypeStruct(shape, dtype)


def norm_parts(rows):
    mean = jnp.mean(rows, axis=-1, keepdims=True)
    cent = rows - mean
    var = jnp.mean(cent * cent, axis=-1, keepdims=True)
    return cent, lax.rsqrt(var + EPS)


def normed_of(x):
    cent, rstd = norm_parts(x.astype(F32))
    return (cent * rstd).astype(BF16)


def halved(bf):
    return bf * jnp.asarray(0.5, BF16)


def silu_both(half):
    t = jnp.tanh(half)
    p = 1.0 + t
    act = half * p
    return act, p + act * (1.0 - t)


def kv_tile(w_t, normed_t, kv_ref, slope_ref, counts_ref):
    act, slope = silu_both(0.5 * nn(w_t, normed_t))
    slope_ref[...] = slope.astype(BF16)
    lane = lax.broadcasted_iota(jnp.int32, (1, BLK), 1)
    for place in range(act.shape[1] // BLK):
        part = act[:, place * BLK : (place + 1) * BLK]
        if counts_ref is not None:
            part = jnp.where(lane < counts_ref[place], part, 0.0)
        kv_ref[place] = part.astype(BF16)


def own_kernel(
    counts_ref, x_ref, grad_ref, w_ref, wo_ref,
    kv_ref, kvslope_ref, normed_t_ref, w_t_ref, acts_ref, slope_ref, dy_ref, normed_ref,
):
    step = pl.program_id(0)

    @pl.when(step == 0)
    def _():
        normed = normed_of(x_ref[...])
        normed_ref[...] = halved(normed)
        normed_t_ref[...] = normed.T

    @pl.when(step < 4)
    def _():
        w_t_ref[...] = w_ref[...].T
        kv_tile(w_t_ref[...], normed_t_ref[...], kv_ref, kvslope_ref, counts_ref)

    @pl.when(jnp.logical_and(step >= 4, step < 8))
    def _():
        scale = jnp.where(step >= 6, HD ** (-0.5) * 0.5, 1.0).astype(F32)
        act, slope = silu_both(nn(normed_ref[...], w_ref[...]))
        acts_ref[...] = (act * scale).astype(BF16)
        slope_ref[...] = slope.astype(BF16)

    @pl.when(step >= 8)
    def _():
        dy_ref[...] = nt(grad_ref[...], wo_ref[...])


def project_own(counts, x, grad_out, w_in, w_out):
    rows = x.shape[0]
    nblk = rows // BLK

    def w_at(j, _):
        early_tile = j + 2 + 2 * (j // 2)
        later = jnp.minimum(j, 7) - 4
        return (0, jnp.where(j < 4, early_tile, later + 2 * (later // 2)))

    def up_to(last, start=0):
        return lambda j: jnp.clip(j - start, 0, last)

    kv_at, uq_at, dy_at = up_to(3), up_to(3, 4), up_to(1, 8)
    uq = pl.BlockSpec((rows, 512), lambda j, _: (0, uq_at(j)))
    return pl.pallas_call(
        own_kernel,
        grid_spec=pltpu.PrefetchScalarGridSpec(
            num_scalar_prefetch=1,
            grid=(10,),
            in_specs=[
                whole(x.shape),
                whole(grad_out.shape),
                pl.BlockSpec((WIDE, 512), w_at),
                pl.BlockSpec((512, WIDE), lambda j, _: (dy_at(j), 0)),
            ],
            out_specs=[
                pl.BlockSpec((nblk, 512, BLK), lambda j, _: (BACK, kv_at(j), 0)),
                pl.BlockSpec((512, rows), lambda j, _: (kv_at(j), BACK)),
                pl.BlockSpec((WIDE, rows), lambda j, _: (0, BACK)),
                pl.BlockSpec((512, WIDE), lambda j, _: (kv_at(j), 0)),
                uq,
                uq,
                pl.BlockSpec((rows, 512), lambda j, _: (0, dy_at(j))),
            ],
            scratch_shapes=[pltpu.VMEM((rows, WIDE), BF16)],
        ),
        out_shape=[
            sds(((BACK + 1) * nblk, 2 * WIDE, BLK), BF16),
            sds((2 * WIDE, (BACK + 1) * rows), BF16),
            sds((WIDE, (BACK + 1) * rows), BF16),
            sds((2 * WIDE, WIDE), BF16),
            sds((rows, 2 * WIDE), BF16),
            sds((rows, 2 * WIDE), BF16),
            sds((rows, WIDE), F32),
        ],
        compiler_params=params(32),
        name="project_own",
        cost_estimate=cost(13),
    )(counts, x, grad_out, w_in, w_out)


def window_kernel(
    x_even_ref, x_odd_ref, x_near_ref, w_ref, _kv, _slope, _normed,
    kv_ref, slope_ref, normed_t_ref,
):
    rows = x_near_ref.shape[0]

    @pl.when(pl.program_id(0) == 0)
    def _():
        far = x_odd_ref[...].astype(F32) + x_even_ref[...].astype(F32)
        normed_t_ref[:, :rows] = normed_of(far).T
        normed_t_ref[:, rows:] = normed_of(x_near_ref[...]).T

    kv_tile(w_ref[...], normed_t_ref[...], kv_ref, slope_ref, None)


def project_window(xs, w_kv_t, arrays):
    rows = xs[0].shape[0]
    nblk = rows // BLK
    return pl.pallas_call(
        window_kernel,
        grid=(4,),
        in_specs=[whole(x.shape) for x in xs]
        + [pl.BlockSpec((512, WIDE), lambda j: (j, 0))]
        + [pl.BlockSpec(memory_space=pl.ANY)] * 3,
        out_specs=[
            pl.BlockSpec((BACK * nblk, 512, BLK), lambda j: (0, j, 0)),
            pl.BlockSpec((512, BACK * rows), lambda j: (j, 0)),
            pl.BlockSpec((WIDE, BACK * rows), lambda j: (0, 0)),
        ],
        out_shape=[sds(a.shape, BF16) for a in arrays],
        input_output_aliases={len(xs) + 1 + i: i for i in range(3)},
        compiler_params=params(32),
        name="project_window",
        cost_estimate=cost(10),
    )(*xs, w_kv_t, *arrays)


def duo_of(ref, idx_ref, blk, duo, rows):
    return jnp.concatenate([ref[idx_ref[blk, 2 * duo + i], rows, :] for i in range(2)], axis=1)


def diagonal(quad_rows):
    left = lax.broadcasted_iota(jnp.int32, (BLK, BLK), 1) < HD
    pairs = []
    for pair in range(2):
        lanes = slice(pair * BLK, pair * BLK + BLK)
        one = quad_rows[2 * pair * BLK : (2 * pair + 1) * BLK, lanes]
        two = quad_rows[(2 * pair + 1) * BLK : (2 * pair + 2) * BLK, lanes]
        pairs.append(jnp.where(left, one, two))
    return jnp.concatenate(pairs, axis=1)


def put_split(core_ref, val, mine_ref, theirs_ref, group, cols):
    _, pieces, height, _ = mine_ref.shape
    split = val.astype(BF16).reshape(pieces, 2, height, val.shape[1])
    even, odd = split[:, 0], split[:, 1]
    first = core_ref[0] == 0
    mine_ref[group, :, :, cols] = jnp.where(first, even, odd)
    theirs_ref[group, :, :, cols] = jnp.where(first, odd, even)


def fwd_kernel(
    idx_ref, core_ref, q_ref, v_ref, k_ref, u_ref, uslope_ref, dy_ref, grad_ref, normed_ref,
    w_ref, g_ref, qt_ref, y_ref, dpu_ref, do_ref, dot_ref, mine_ref, theirs_ref,
    attn_ref, yt_ref,
):
    quad = pl.program_id(0)
    rows = y_ref.shape[0]
    row = lax.broadcasted_iota(jnp.int32, (BLK, BLK), 0)
    col = lax.broadcasted_iota(jnp.int32, (BLK, BLK), 1)
    keep = jnp.concatenate([jnp.full((BLK, BLK), True), col <= row], axis=1)
    qt_ref[...] = q_ref[...].T

    def one_block(blk, carry):
        block = pl.ds(pl.multiple_of(blk * BLK, BLK), BLK)
        total = None
        for duo in range(2):
            ws = []
            for head in range(4):
                cols = slice(head * HD, head * HD + HD)
                half = nn(q_ref[block, cols], duo_of(k_ref, idx_ref, blk, duo, cols))
                w, g = silu_both(half)
                if duo == 1:
                    w = jnp.where(keep, w, 0.0)
                    g = jnp.where(keep, g, 0.0)
                w = w.astype(BF16)
                ws.append(w)
                w_ref[blk, head, :, duo * 256 : duo * 256 + 256] = w
                g_ref[blk, head, :, duo * 256 : duo * 256 + 256] = g.astype(BF16)
            vals = duo_of(v_ref, idx_ref, blk, duo, slice(None))
            part = nt(jnp.concatenate(ws, axis=0), vals)
            total = part if total is None else total + part
        attn_ref[quad, block, :] = diagonal(total) * (1.0 / BLK)
        return carry

    lax.fori_loop(0, rows // BLK, one_block, 0)

    @pl.when(quad == pl.num_programs(0) - 1)
    def _():
        def finish_block(blk, carry):
            block = pl.ds(pl.multiple_of(blk * BLK, BLK), BLK)
            attn = jnp.concatenate([attn_ref[i, block, :] for i in range(4)], axis=1)
            cent, rstd = norm_parts(attn)
            z = cent * rstd
            u = u_ref[block, :].astype(F32)
            dy = dy_ref[block, :]
            y = (z * u).astype(BF16)
            y_ref[block, :] = y
            yt_ref[:, block] = y.T
            dpu_ref[block, :] = (dy * (0.5 * z) * uslope_ref[block, :].astype(F32)).astype(BF16)
            dz = dy * u
            shift = jnp.mean(dz, axis=-1, keepdims=True)
            dattn = rstd * (dz - shift - z * jnp.mean(dz * z, axis=-1, keepdims=True))
            dattn = dattn.astype(BF16)
            do_ref[block, :] = dattn
            dot_ref[:, block] = dattn.T
            return carry

        lax.fori_loop(0, rows // BLK, finish_block, 0)
        for group, (left_ref, right_ref) in enumerate(((yt_ref, grad_ref), (normed_ref, dpu_ref))):
            for tile in range(2):
                cols = slice(tile * 512, tile * 512 + 512)
                val = nn(left_ref[...], right_ref[:, cols])
                put_split(core_ref, val, mine_ref, theirs_ref, group, cols)


def attend(idx, core, size, acts, slopes, kv, dy, grad_out, normed):
    rows = dy.shape[0]
    nblk = rows // BLK
    places = kv.shape[0]
    scores = pl.BlockSpec((nblk, 4, BLK, 4 * BLK), lambda i, *_: (0, i, 0, 0))
    left = pl.BlockSpec((rows, WIDE), lambda *_: (0, 0), pipeline_mode=pl.Buffered(1))
    chunk = (2, size // 2, WIDE // size, WIDE)
    return pl.pallas_call(
        fwd_kernel,
        grid_spec=pltpu.PrefetchScalarGridSpec(
            num_scalar_prefetch=2,
            grid=(HEADS // 4,),
            in_specs=[
                pl.BlockSpec((rows, 256), lambda i, *_: (0, 4 + i)),
                pl.BlockSpec((places, 256, BLK), lambda i, *_: (0, i, 0)),
                pl.BlockSpec((places, 256, BLK), lambda i, *_: (0, 4 + i, 0)),
                left,
                left,
                left,
                left,
                pl.BlockSpec((WIDE, rows), lambda *_: (0, BACK), pipeline_mode=pl.Buffered(1)),
            ],
            out_specs=[
                scores,
                scores,
                pl.BlockSpec((256, rows), lambda i, *_: (i, 0)),
                left,
                left,
                left,
                whole((WIDE, rows)),
                whole(chunk),
                whole(chunk),
            ],
            scratch_shapes=[
                pltpu.VMEM((HEADS // 4, rows, 256), F32),
                pltpu.VMEM((WIDE, rows), BF16),
            ],
        ),
        out_shape=[
            sds((nblk, HEADS, BLK, 4 * BLK), BF16),
            sds((nblk, HEADS, BLK, 4 * BLK), BF16),
            sds((WIDE, rows), BF16),
            sds((rows, WIDE), BF16),
            sds((rows, WIDE), BF16),
            sds((rows, WIDE), BF16),
            sds((WIDE, rows), BF16),
            sds(chunk, BF16),
            sds(chunk, BF16),
        ],
        compiler_params=params(44),
        name="attend",
        cost_estimate=cost(18),
    )(idx, core, acts, kv, kv, acts, slopes, dy, grad_out, normed)


def events_kernel(x_ref, y_ref, wo_ref, ev_ref):
    ev_ref[...] = (x_ref[...].astype(F32) + nn(y_ref[...], wo_ref[...])).astype(BF16)


def events(x, y, w_out):
    rows = x.shape[0]
    tile = pl.BlockSpec((rows, 512), lambda j: (0, j))
    return pl.pallas_call(
        events_kernel,
        grid=(2,),
        in_specs=[tile, whole(y.shape), pl.BlockSpec((WIDE, 512), lambda j: (0, j))],
        out_specs=tile,
        out_shape=sds((rows, WIDE), BF16),
        compiler_params=params(24),
        name="events_out",
        cost_estimate=cost(4),
    )(x, y, w_out)


def bwd_kernel(*refs, first):
    (idx_ref, core_ref, w_ref, g_ref, v_ref, k_ref, do_ref, dot_ref, qt_ref, qslope_ref) = refs[:10]
    (vslope_ref, kslope_ref, normed_ref, wv_ref, wk_ref) = refs[10:15]
    rest = refs[15:]
    if first:
        part_ref = rest[5]
        rest = rest[:5] + rest[6:]
    else:
        part_ref, far_ref, near_ref = rest[0], rest[6], rest[7]
        rest = rest[1:6] + rest[8:]
    (mine_ref, theirs_ref, dpq_ref, dvt_ref, dkt_ref) = rest[:5]
    (dva_ref, dka_ref, dvb_ref, dkb_ref, sum_ref) = rest[5:]
    step = pl.program_id(0)
    rows = dpq_ref.shape[0]
    dva_ref[...] = jnp.zeros_like(dva_ref)
    dka_ref[...] = jnp.zeros_like(dka_ref)

    @pl.when(step == 0)
    def _():
        sum_ref[...] = jnp.zeros_like(sum_ref) if first else part_ref[...].astype(F32)

    def one_block(blk, carry):
        at = pl.multiple_of(blk * BLK, BLK)
        block = pl.ds(at, BLK)
        total = None
        for duo in range(2):
            span = slice(duo * 256, duo * 256 + 256)
            dss = []
            for head in range(4):
                cols = slice(head * HD, head * HD + HD)
                dw = nn(do_ref[block, cols], duo_of(v_ref, idx_ref, blk, duo, cols))
                ds = (dw * g_ref[blk, head, :, span].astype(F32)).astype(BF16)
                dss.append(ds)
                dk = nn(qt_ref[cols, block], ds)
                dv = nn(dot_ref[cols, block], w_ref[blk, head, :, span])
                for side in range(2):
                    place = idx_ref[blk, 2 * duo + side]
                    lanes = slice(side * BLK, side * BLK + BLK)
                    dva_ref[place, cols, :] += dv[:, lanes]
                    dka_ref[place, cols, :] += dk[:, lanes]
            part = nt(jnp.concatenate(dss, axis=0), duo_of(k_ref, idx_ref, blk, duo, slice(None)))
            total = part if total is None else total + part
        dq = diagonal(total) * (HD ** (-0.5) / (4 * BLK))
        dpq_ref[block, :] = (dq * qslope_ref[block, :].astype(F32)).astype(BF16)
        return carry

    lax.fori_loop(0, rows // BLK, one_block, 0)
    for place in range(dva_ref.shape[0]):
        lanes = slice(place * BLK, place * BLK + BLK)
        for acc_ref, slope_ref, out_ref in (
            (dva_ref, vslope_ref, dvb_ref),
            (dka_ref, kslope_ref, dkb_ref),
        ):
            out_ref[:, lanes] = (
                acc_ref[place] * (0.5 / BLK) * slope_ref[:, lanes].astype(F32)
            ).astype(BF16)
    dvt_ref[...] = dvb_ref[:, BACK * rows :]
    dkt_ref[...] = dkb_ref[:, BACK * rows :]
    put_split(core_ref, nt(normed_ref[...], dvb_ref[...]), mine_ref, theirs_ref, 0, slice(None))
    put_split(
        core_ref, nn(normed_ref[:, BACK * rows :], dpq_ref[...]), mine_ref, theirs_ref, 1, slice(None)
    )
    put_split(core_ref, nt(normed_ref[...], dkb_ref[...]), mine_ref, theirs_ref, 2, slice(None))
    for at in range(BACK):
        lanes = slice(at * rows, at * rows + rows)
        left = jnp.concatenate([wv_ref[...], wk_ref[...]], axis=1)
        right = jnp.concatenate([dvb_ref[:, lanes], dkb_ref[:, lanes]], axis=0)
        sum_ref[at] += nn(left, right)

    @pl.when(step == pl.num_programs(0) - 1)
    def _():
        for at in range(BACK):
            done = sum_ref[at].astype(BF16)
            if first:
                part_ref[at] = done
            else:
                (far_ref, near_ref)[at][...] = done


def attend_back(start, idx, core, size, w, g, kv, do, do_t, q_t, slopes, kv_slopes, normed, w_in, part):
    rows = do.shape[0]
    nblk = rows // BLK
    places = kv.shape[0]
    first = part is None
    heads = pl.BlockSpec((nblk, 4, BLK, 4 * BLK), lambda i, *_: (0, start + i, 0, 0))
    tall = (BACK + 1) * rows
    wide = pl.BlockSpec((3, size // 2, WIDE // size, 256), lambda i, *_: (0, 0, 0, i))
    cols = pl.BlockSpec((256, rows), lambda i, *_: (i, 0))
    in_specs = [
        heads,
        heads,
        pl.BlockSpec((places, 256, BLK), lambda i, *_: (0, start + i, 0)),
        pl.BlockSpec((places, 256, BLK), lambda i, *_: (0, 4 + start + i, 0)),
        pl.BlockSpec((rows, 256), lambda i, *_: (0, start + i)),
        pl.BlockSpec((256, rows), lambda i, *_: (start + i, 0)),
        pl.BlockSpec((256, rows), lambda i, *_: (start + i, 0)),
        pl.BlockSpec((rows, 256), lambda i, *_: (0, 4 + start + i)),
        pl.BlockSpec((256, tall), lambda i, *_: (start + i, 0)),
        pl.BlockSpec((256, tall), lambda i, *_: (4 + start + i, 0)),
        whole(normed.shape),
        pl.BlockSpec((WIDE, 256), lambda i, *_: (0, 4 + start + i)),
        pl.BlockSpec((WIDE, 256), lambda i, *_: (0, 12 + start + i)),
    ]
    args = [idx, core, w, g, kv, kv, do, do_t, q_t, slopes, kv_slopes, kv_slopes, normed, w_in, w_in]
    chunk = sds((3, size // 2, WIDE // size, 512), BF16)
    out_specs = [wide, wide, pl.BlockSpec((rows, 256), lambda i, *_: (0, i)), cols, cols]
    out_shape = [chunk, chunk, sds((rows, 512), BF16), sds((512, rows), BF16), sds((512, rows), BF16)]
    if first:
        out_specs.append(whole((BACK, WIDE, rows)))
        out_shape.append(sds((BACK, WIDE, rows), BF16))
    else:
        in_specs.append(whole(part.shape))
        args.append(part)
        out_specs += [whole((WIDE, rows))] * 2
        out_shape += [sds((WIDE, rows), BF16)] * 2
    return pl.pallas_call(
        lambda *refs: bwd_kernel(*refs, first=first),
        grid_spec=pltpu.PrefetchScalarGridSpec(
            num_scalar_prefetch=2,
            grid=(2,),
            in_specs=in_specs,
            out_specs=out_specs,
            scratch_shapes=[
                pltpu.VMEM((places, 256, BLK), F32),
                pltpu.VMEM((places, 256, BLK), F32),
                pltpu.VMEM((256, tall), BF16),
                pltpu.VMEM((256, tall), BF16),
                pltpu.VMEM((BACK, WIDE, rows), F32),
            ],
        ),
        out_shape=out_shape,
        compiler_params=params(44),
        name="attend_back_%d" % start,
        cost_estimate=cost(24),
    )(*args)


def dn_u_kernel(w_ref, dpu_ref, own_ref):
    own_ref[...] = nt(w_ref[...], dpu_ref[...])


def grad_normed_u(w_in, dpu):
    rows = dpu.shape[0]
    return pl.pallas_call(
        dn_u_kernel,
        grid=(2,),
        in_specs=[pl.BlockSpec((WIDE // 2, WIDE), lambda j: (j, 0)), whole(dpu.shape)],
        out_specs=pl.BlockSpec((WIDE // 2, rows), lambda j: (j, 0)),
        out_shape=sds((WIDE, rows), F32),
        compiler_params=params(24),
        name="grad_normed_u",
        cost_estimate=cost(4),
    )(w_in, dpu)


def dn_own_kernel(w_ref, u_ref, qa_ref, qb_ref, va_ref, vb_ref, ka_ref, kb_ref, own_ref):
    step = pl.program_id(0)
    half = WIDE // 2
    left, right = w_ref[:, :half], w_ref[:, half:]

    @pl.when(step == 0)
    def _():
        own_ref[...] = u_ref[...] + nn(left, va_ref[...]) + nn(right, vb_ref[...])

    @pl.when(step == 1)
    def _():
        own_ref[...] += nt(left, qa_ref[...]) + nt(right, qb_ref[...])

    @pl.when(step == 2)
    def _():
        own_ref[...] += nn(left, ka_ref[...]) + nn(right, kb_ref[...])


def grad_normed_own(w_in, from_u, *halves):
    return pl.pallas_call(
        dn_own_kernel,
        grid=(3,),
        in_specs=[pl.BlockSpec((WIDE, WIDE), lambda j: (0, j + 1)), whole(from_u.shape)]
        + [whole(a.shape) for a in halves],
        out_specs=whole(from_u.shape),
        out_shape=sds(from_u.shape, F32),
        compiler_params=params(24),
        name="grad_normed_own",
        cost_estimate=cost(8),
    )(w_in, from_u, *halves)


def last_kernel(own_ref, a_ref, b_ref, c_ref, x_ref, grad_ref, out_ref):
    dn_t = own_ref[...] + a_ref[...].astype(F32) + b_ref[...].astype(F32) + c_ref[...].astype(F32)
    dn = dn_t.T
    cent, rstd = norm_parts(x_ref[...].astype(F32))
    z = cent * rstd
    dx = rstd * (
        dn - jnp.mean(dn, axis=-1, keepdims=True) - z * jnp.mean(dn * z, axis=-1, keepdims=True)
    )
    out_ref[...] = (grad_ref[...].astype(F32) + dx).astype(BF16)


def last(own, one, two, three, x, grad_out):
    rows = x.shape[0]
    colblk = pl.BlockSpec((WIDE, BLK), lambda b: (0, b))
    rowblk = pl.BlockSpec((BLK, WIDE), lambda b: (b, 0))
    return pl.pallas_call(
        last_kernel,
        grid=(rows // BLK,),
        in_specs=[colblk, colblk, colblk, colblk, rowblk, rowblk],
        out_specs=rowblk,
        out_shape=sds((rows, WIDE), BF16),
        compiler_params=params(24),
        name="grad_x",
        cost_estimate=cost(6),
    )(own, one, two, three, x, grad_out)


def send(array, pairs):
    return lax.ppermute(array, "seq", pairs)


class Halving:
    def __init__(self, mine, theirs, size, bits):
        self.size, self.bits, self.at = size, bits, 0
        self.left = list(range(1, size.bit_length() - 1))
        self.keep, self.got = mine, self.swap(theirs, 0)

    def swap(self, array, bit):
        return send(array, [(i, i ^ (1 << bit)) for i in range(self.size)])

    def step(self, *after):
        bit = self.bits[self.at]
        inner = 1 << self.left.index(bit)
        self.at += 1
        groups, count, height, cols = self.keep.shape
        shape = (groups, count // (2 * inner), 2, inner * height, cols)
        keep, got = self.keep.reshape(shape), self.got.reshape(shape)
        if after:
            got = tie(got, *after)
        side = (lax.axis_index("seq") >> bit) & 1

        def added(which):
            parts = [lax.dynamic_index_in_dim(a, which, 2, keepdims=False) for a in (keep, got)]
            total = parts[0].astype(F32) + parts[1].astype(F32)
            return total.astype(BF16).reshape(groups, count // 2, height, cols)

        moving = added(1 - side)
        self.keep, self.got = added(side), self.swap(moving, bit)
        self.left.remove(bit)
        return moving

    def parts(self):
        while self.at < len(self.bits):
            self.step()
        return self.keep, self.got


def finish_kernel(ek_ref, eg_ref, ak_ref, ag_ref, bk_ref, bg_ref, win_ref, wout_ref):
    def total(keep_ref, got_ref, group):
        return keep_ref[group, 0].astype(F32) + got_ref[group, 0].astype(F32)

    wout_ref[...] = total(ek_ref, eg_ref, 0)
    win_ref[:, :WIDE] = total(ek_ref, eg_ref, 1)
    for group in range(3):
        at = (group + 1) * WIDE
        win_ref[:, at : at + 512] = total(ak_ref, ag_ref, group)
        win_ref[:, at + 512 : at + WIDE] = total(bk_ref, bg_ref, group)


def finish(*sums):
    args = [a for pair in sums for a in pair]
    height = args[0].shape[2]
    return pl.pallas_call(
        finish_kernel,
        in_specs=[pl.BlockSpec(memory_space=pltpu.VMEM)] * 6,
        out_specs=[pl.BlockSpec(memory_space=pltpu.VMEM)] * 2,
        out_shape=[sds((height, 4 * WIDE), F32), sds((height, WIDE), F32)],
        compiler_params=pltpu.CompilerParams(vmem_limit_bytes=8 * MIB),
        name="finish_sums",
        cost_estimate=cost(2),
    )(*args)


def on_device(events_in, w_in, w_out, kv_list, counts, grad_out):
    size = lax.axis_size("seq")
    nblk = kv_list.shape[0]
    place = lax.axis_index("seq")
    core = (place % 2).astype(jnp.int32)[None]
    pairs = range(0, size, 2)
    live = jnp.arange(BLK, dtype=jnp.int32)[None, :] < counts[:, None]
    shown = jnp.where(live.reshape(-1)[:, None], events_in, jnp.zeros((), BF16))
    x_near = send(shown, [(i, i + 1) for i in range(size - 1)])
    x_even = send(shown, [(i, i + 2) for i in range(0, size - 2, 2)])
    x_odd = send(x_near, [(i, i + 1) for i in pairs])
    local = jnp.arange(nblk, dtype=jnp.int32)
    index = jnp.concatenate(
        [kv_list + (BACK - place) * nblk, (local + BACK * nblk)[:, None]], axis=1
    )
    index = jnp.clip(index, 0, (BACK + 1) * nblk - 1)

    kv, kv_slopes, normed, w_kv_t, acts, slopes, dy = project_own(
        counts, events_in, grad_out, w_in, w_out
    )
    x_odd = send(tie(x_near, dy), [(i, i + 1) for i in pairs])
    kv, kv_slopes, normed = project_window(
        [x_even, x_odd, x_near], w_kv_t, (kv, kv_slopes, normed)
    )
    w, g, q_t, y, dpu, do, do_t, mine, theirs = attend(
        index, core, size, acts, slopes, kv, dy, grad_out, normed
    )
    ups = list(range(1, size.bit_length() - 1))
    sum_early = Halving(mine, theirs, size, ups)
    from_u = grad_normed_u(w_in, tie(dpu, mine))
    sent = sum_early.step(from_u)

    def backward(start, token, part):
        return attend_back(
            start, token, core, size, w, g, kv, do, do_t, q_t, slopes, kv_slopes, normed, w_in, part
        )

    mine, theirs, qa, va, ka, part = backward(0, tie(index, sent), None)
    sent = sum_early.step(qa)
    first = Halving(mine, tie(theirs, sent), size, ups)
    events_out = events(events_in, tie(y, first.keep, sent), w_out)
    sent = first.step(events_out)
    mine, theirs, qb, vb, kb, far, near = backward(2, tie(index, sent), part)
    to_even = [(i + 1, i) for i in pairs]
    far, near, mine, theirs, sum_early.got, first.got = lax.optimization_barrier(
        (far, near, mine, theirs, sum_early.got, first.got)
    )
    far_odd = send(far, to_even)
    far_even = send(far, [(i + 2, i) for i in range(0, size - 2, 2)])
    near_odd = send(near, to_even)
    second = Halving(mine, theirs, size, ups[1:] + ups[:1])
    joined = (near.astype(F32) + far_odd.astype(F32)).astype(BF16)
    sent = second.step(joined)
    back = send(joined, [(i, i - 1) for i in range(2, size, 2)])
    early_sent = sum_early.step(sent)
    first_sent = first.step(early_sent)
    own = grad_normed_own(w_in, tie(from_u, first_sent), qa, qb, va, vb, ka, kb)
    grad_x = last(own, near_odd, far_even, back, events_in, grad_out)
    grad_w_in, grad_w_out = finish(sum_early.parts(), first.parts(), second.parts())
    return (events_out, grad_x, grad_w_in, grad_w_out)


def solution(mesh):
    rows = P(("grp", "seq"), None)
    return jax.shard_map(
        on_device,
        mesh=mesh,
        in_specs=(rows, P(), P(), rows, P(("grp", "seq")), rows),
        out_specs=(rows, rows, rows, rows),
        check_vma=False,
    )
```

```python
import jax
import jax.numpy as jnp
from jax import lax
from jax.experimental import pallas as pl
from jax.experimental.pallas import tpu as pltpu
from jax.sharding import PartitionSpec as P

HEADS = 16
HD = 64
BLK = 128
WIDE = 1024
BACK = 2
EPS = 1e-05
F32 = jnp.float32
BF16 = jnp.bfloat16
MIB = 1024 * 1024


def nn(left, right):
    return lax.dot_general(left, right, (((1,), (0,)), ((), ())), preferred_element_type=F32)


def nt(left, right):
    return lax.dot_general(left, right, (((1,), (1,)), ((), ())), preferred_element_type=F32)


def params(mib):
    return pltpu.CompilerParams(dimension_semantics=("arbitrary",), vmem_limit_bytes=mib * MIB)


def cost(micros):
    return pl.CostEstimate(flops=int(micros * 1e9), transcendentals=0, bytes_accessed=1 << 20)


def tie(value, *others):
    return lax.optimization_barrier((value, *others))[0]


def whole(shape):
    zeros = (0,) * len(shape)
    return pl.BlockSpec(shape, lambda *_: zeros, pipeline_mode=pl.Buffered(1))


def sds(shape, dtype):
    return jax.ShapeDtypeStruct(shape, dtype)


def norm_parts(rows):
    mean = jnp.mean(rows, axis=-1, keepdims=True)
    cent = rows - mean
    var = jnp.mean(cent * cent, axis=-1, keepdims=True)
    return cent, lax.rsqrt(var + EPS)


def normed_of(x):
    cent, rstd = norm_parts(x.astype(F32))
    return (cent * rstd).astype(BF16)


def halved(bf):
    return bf * jnp.asarray(0.5, BF16)


def silu_both(half):
    t = jnp.tanh(half)
    p = 1.0 + t
    act = half * p
    return act, p + act * (1.0 - t)


def kv_tile(w_t, normed_t, kv_ref, slope_ref, counts_ref):
    act, slope = silu_both(0.5 * nn(w_t, normed_t))
    slope_ref[...] = slope.astype(BF16)
    lane = lax.broadcasted_iota(jnp.int32, (1, BLK), 1)
    for place in range(act.shape[1] // BLK):
        part = act[:, place * BLK : (place + 1) * BLK]
        if counts_ref is not None:
            part = jnp.where(lane < counts_ref[place], part, 0.0)
        kv_ref[place] = part.astype(BF16)


def own_kernel(
    counts_ref, x_ref, grad_ref, w_ref, wo_ref,
    kv_ref, kvslope_ref, normed_t_ref, w_t_ref, acts_ref, slope_ref, dy_ref, normed_ref,
):
    step = pl.program_id(0)

    @pl.when(step == 0)
    def _():
        normed = normed_of(x_ref[...])
        normed_ref[...] = halved(normed)
        normed_t_ref[...] = normed.T

    @pl.when(step < 4)
    def _():
        w_t_ref[...] = w_ref[...].T
        kv_tile(w_t_ref[...], normed_t_ref[...], kv_ref, kvslope_ref, counts_ref)

    @pl.when(jnp.logical_and(step >= 4, step < 8))
    def _():
        scale = jnp.where(step >= 6, HD ** (-0.5) * 0.5, 1.0).astype(F32)
        act, slope = silu_both(nn(normed_ref[...], w_ref[...]))
        acts_ref[...] = (act * scale).astype(BF16)
        slope_ref[...] = slope.astype(BF16)

    @pl.when(step >= 8)
    def _():
        dy_ref[...] = nt(grad_ref[...], wo_ref[...])


def project_own(counts, x, grad_out, w_in, w_out):
    rows = x.shape[0]
    nblk = rows // BLK

    def w_at(j, _):
        early_tile = j + 2 + 2 * (j // 2)
        later = jnp.minimum(j, 7) - 4
        return (0, jnp.where(j < 4, early_tile, later + 2 * (later // 2)))

    def up_to(last, start=0):
        return lambda j: jnp.clip(j - start, 0, last)

    kv_at, uq_at, dy_at = up_to(3), up_to(3, 4), up_to(1, 8)
    uq = pl.BlockSpec((rows, 512), lambda j, _: (0, uq_at(j)))
    return pl.pallas_call(
        own_kernel,
        grid_spec=pltpu.PrefetchScalarGridSpec(
            num_scalar_prefetch=1,
            grid=(10,),
            in_specs=[
                whole(x.shape),
                whole(grad_out.shape),
                pl.BlockSpec((WIDE, 512), w_at),
                pl.BlockSpec((512, WIDE), lambda j, _: (dy_at(j), 0)),
            ],
            out_specs=[
                pl.BlockSpec((nblk, 512, BLK), lambda j, _: (BACK, kv_at(j), 0)),
                pl.BlockSpec((512, rows), lambda j, _: (kv_at(j), BACK)),
                pl.BlockSpec((WIDE, rows), lambda j, _: (0, BACK)),
                pl.BlockSpec((512, WIDE), lambda j, _: (kv_at(j), 0)),
                uq,
                uq,
                pl.BlockSpec((rows, 512), lambda j, _: (0, dy_at(j))),
            ],
            scratch_shapes=[pltpu.VMEM((rows, WIDE), BF16)],
        ),
        out_shape=[
            sds(((BACK + 1) * nblk, 2 * WIDE, BLK), BF16),
            sds((2 * WIDE, (BACK + 1) * rows), BF16),
            sds((WIDE, (BACK + 1) * rows), BF16),
            sds((2 * WIDE, WIDE), BF16),
            sds((rows, 2 * WIDE), BF16),
            sds((rows, 2 * WIDE), BF16),
            sds((rows, WIDE), F32),
        ],
        compiler_params=params(60),
        name="project_own",
        cost_estimate=cost(13),
    )(counts, x, grad_out, w_in, w_out)


def window_kernel(
    x_even_ref, x_odd_ref, x_near_ref, w_ref, _kv, _slope, _normed,
    kv_ref, slope_ref, normed_t_ref,
):
    rows = x_near_ref.shape[0]

    @pl.when(pl.program_id(0) == 0)
    def _():
        far = x_odd_ref[...].astype(F32) + x_even_ref[...].astype(F32)
        normed_t_ref[:, :rows] = normed_of(far).T
        normed_t_ref[:, rows:] = normed_of(x_near_ref[...]).T

    kv_tile(w_ref[...], normed_t_ref[...], kv_ref, slope_ref, None)


def project_window(xs, w_kv_t, arrays):
    rows = xs[0].shape[0]
    nblk = rows // BLK
    return pl.pallas_call(
        window_kernel,
        grid=(4,),
        in_specs=[whole(x.shape) for x in xs]
        + [pl.BlockSpec((512, WIDE), lambda j: (j, 0))]
        + [pl.BlockSpec(memory_space=pl.ANY)] * 3,
        out_specs=[
            pl.BlockSpec((BACK * nblk, 512, BLK), lambda j: (0, j, 0)),
            pl.BlockSpec((512, BACK * rows), lambda j: (j, 0)),
            pl.BlockSpec((WIDE, BACK * rows), lambda j: (0, 0)),
        ],
        out_shape=[sds(a.shape, BF16) for a in arrays],
        input_output_aliases={len(xs) + 1 + i: i for i in range(3)},
        compiler_params=params(60),
        name="project_window",
        cost_estimate=cost(10),
    )(*xs, w_kv_t, *arrays)


def duo_of(ref, idx_ref, blk, duo, rows):
    return jnp.concatenate([ref[idx_ref[blk, 2 * duo + i], rows, :] for i in range(2)], axis=1)


def diagonal(quad_rows):
    left = lax.broadcasted_iota(jnp.int32, (BLK, BLK), 1) < HD
    pairs = []
    for pair in range(2):
        lanes = slice(pair * BLK, pair * BLK + BLK)
        one = quad_rows[2 * pair * BLK : (2 * pair + 1) * BLK, lanes]
        two = quad_rows[(2 * pair + 1) * BLK : (2 * pair + 2) * BLK, lanes]
        pairs.append(jnp.where(left, one, two))
    return jnp.concatenate(pairs, axis=1)


def put_split(core_ref, val, mine_ref, theirs_ref, group, cols):
    _, pieces, height, _ = mine_ref.shape
    split = val.astype(BF16).reshape(pieces, 2, height, val.shape[1])
    even, odd = split[:, 0], split[:, 1]
    first = core_ref[0] == 0
    mine_ref[group, :, :, cols] = jnp.where(first, even, odd)
    theirs_ref[group, :, :, cols] = jnp.where(first, odd, even)


def fwd_kernel(
    idx_ref, core_ref, q_ref, v_ref, k_ref, u_ref, uslope_ref, dy_ref, grad_ref, normed_ref,
    w_ref, g_ref, qt_ref, y_ref, dpu_ref, do_ref, dot_ref, mine_ref, theirs_ref,
    attn_ref, yt_ref,
):
    quad = pl.program_id(0)
    rows = y_ref.shape[0]
    row = lax.broadcasted_iota(jnp.int32, (BLK, BLK), 0)
    col = lax.broadcasted_iota(jnp.int32, (BLK, BLK), 1)
    keep = jnp.concatenate([jnp.full((BLK, BLK), True), col <= row], axis=1)
    qt_ref[...] = q_ref[...].T

    def one_block(blk, carry):
        block = pl.ds(pl.multiple_of(blk * BLK, BLK), BLK)
        total = None
        for duo in range(2):
            ws = []
            for head in range(4):
                cols = slice(head * HD, head * HD + HD)
                half = nn(q_ref[block, cols], duo_of(k_ref, idx_ref, blk, duo, cols))
                w, g = silu_both(half)
                if duo == 1:
                    w = jnp.where(keep, w, 0.0)
                    g = jnp.where(keep, g, 0.0)
                w = w.astype(BF16)
                ws.append(w)
                w_ref[blk, head, :, duo * 256 : duo * 256 + 256] = w
                g_ref[blk, head, :, duo * 256 : duo * 256 + 256] = g.astype(BF16)
            vals = duo_of(v_ref, idx_ref, blk, duo, slice(None))
            part = nt(jnp.concatenate(ws, axis=0), vals)
            total = part if total is None else total + part
        attn_ref[quad, block, :] = diagonal(total) * (1.0 / BLK)
        return carry

    lax.fori_loop(0, rows // BLK, one_block, 0)

    @pl.when(quad == pl.num_programs(0) - 1)
    def _():
        def finish_block(blk, carry):
            block = pl.ds(pl.multiple_of(blk * BLK, BLK), BLK)
            attn = jnp.concatenate([attn_ref[i, block, :] for i in range(4)], axis=1)
            cent, rstd = norm_parts(attn)
            z = cent * rstd
            u = u_ref[block, :].astype(F32)
            dy = dy_ref[block, :]
            y = (z * u).astype(BF16)
            y_ref[block, :] = y
            yt_ref[:, block] = y.T
            dpu_ref[block, :] = (dy * (0.5 * z) * uslope_ref[block, :].astype(F32)).astype(BF16)
            dz = dy * u
            shift = jnp.mean(dz, axis=-1, keepdims=True)
            dattn = rstd * (dz - shift - z * jnp.mean(dz * z, axis=-1, keepdims=True))
            dattn = dattn.astype(BF16)
            do_ref[block, :] = dattn
            dot_ref[:, block] = dattn.T
            return carry

        lax.fori_loop(0, rows // BLK, finish_block, 0)
        for group, (left_ref, right_ref) in enumerate(((yt_ref, grad_ref), (normed_ref, dpu_ref))):
            for tile in range(2):
                cols = slice(tile * 512, tile * 512 + 512)
                val = nn(left_ref[...], right_ref[:, cols])
                put_split(core_ref, val, mine_ref, theirs_ref, group, cols)


def attend(idx, core, size, acts, slopes, kv, dy, grad_out, normed):
    rows = dy.shape[0]
    nblk = rows // BLK
    places = kv.shape[0]
    scores = pl.BlockSpec((nblk, 4, BLK, 4 * BLK), lambda i, *_: (0, i, 0, 0))
    left = pl.BlockSpec((rows, WIDE), lambda *_: (0, 0), pipeline_mode=pl.Buffered(1))
    chunk = (2, size // 2, WIDE // size, WIDE)
    return pl.pallas_call(
        fwd_kernel,
        grid_spec=pltpu.PrefetchScalarGridSpec(
            num_scalar_prefetch=2,
            grid=(HEADS // 4,),
            in_specs=[
                pl.BlockSpec((rows, 256), lambda i, *_: (0, 4 + i)),
                pl.BlockSpec((places, 256, BLK), lambda i, *_: (0, i, 0)),
                pl.BlockSpec((places, 256, BLK), lambda i, *_: (0, 4 + i, 0)),
                left,
                left,
                left,
                left,
                pl.BlockSpec((WIDE, rows), lambda *_: (0, BACK), pipeline_mode=pl.Buffered(1)),
            ],
            out_specs=[
                scores,
                scores,
                pl.BlockSpec((256, rows), lambda i, *_: (i, 0)),
                left,
                left,
                left,
                whole((WIDE, rows)),
                whole(chunk),
                whole(chunk),
            ],
            scratch_shapes=[
                pltpu.VMEM((HEADS // 4, rows, 256), F32),
                pltpu.VMEM((WIDE, rows), BF16),
            ],
        ),
        out_shape=[
            sds((nblk, HEADS, BLK, 4 * BLK), BF16),
            sds((nblk, HEADS, BLK, 4 * BLK), BF16),
            sds((WIDE, rows), BF16),
            sds((rows, WIDE), BF16),
            sds((rows, WIDE), BF16),
            sds((rows, WIDE), BF16),
            sds((WIDE, rows), BF16),
            sds(chunk, BF16),
            sds(chunk, BF16),
        ],
        compiler_params=params(60),
        name="attend",
        cost_estimate=cost(18),
    )(idx, core, acts, kv, kv, acts, slopes, dy, grad_out, normed)


def events_kernel(x_ref, y_ref, wo_ref, ev_ref):
    ev_ref[...] = (x_ref[...].astype(F32) + nn(y_ref[...], wo_ref[...])).astype(BF16)


def events(x, y, w_out):
    rows = x.shape[0]
    tile = pl.BlockSpec((rows, 512), lambda j: (0, j))
    return pl.pallas_call(
        events_kernel,
        grid=(2,),
        in_specs=[tile, whole(y.shape), pl.BlockSpec((WIDE, 512), lambda j: (0, j))],
        out_specs=tile,
        out_shape=sds((rows, WIDE), BF16),
        compiler_params=params(60),
        name="events_out",
        cost_estimate=cost(4),
    )(x, y, w_out)


def bwd_kernel(*refs, first):
    (idx_ref, core_ref, w_ref, g_ref, v_ref, k_ref, do_ref, dot_ref, qt_ref, qslope_ref) = refs[:10]
    (vslope_ref, kslope_ref, normed_ref, wv_ref, wk_ref) = refs[10:15]
    rest = refs[15:]
    if first:
        part_ref = rest[5]
        rest = rest[:5] + rest[6:]
    else:
        part_ref, far_ref, near_ref = rest[0], rest[6], rest[7]
        rest = rest[1:6] + rest[8:]
    (mine_ref, theirs_ref, dpq_ref, dvt_ref, dkt_ref) = rest[:5]
    (dva_ref, dka_ref, dvb_ref, dkb_ref, sum_ref) = rest[5:]
    step = pl.program_id(0)
    rows = dpq_ref.shape[0]
    dva_ref[...] = jnp.zeros_like(dva_ref)
    dka_ref[...] = jnp.zeros_like(dka_ref)

    @pl.when(step == 0)
    def _():
        sum_ref[...] = jnp.zeros_like(sum_ref) if first else part_ref[...].astype(F32)

    def one_block(blk, carry):
        at = pl.multiple_of(blk * BLK, BLK)
        block = pl.ds(at, BLK)
        total = None
        for duo in range(2):
            span = slice(duo * 256, duo * 256 + 256)
            dss = []
            for head in range(4):
                cols = slice(head * HD, head * HD + HD)
                dw = nn(do_ref[block, cols], duo_of(v_ref, idx_ref, blk, duo, cols))
                ds = (dw * g_ref[blk, head, :, span].astype(F32)).astype(BF16)
                dss.append(ds)
                dk = nn(qt_ref[cols, block], ds)
                dv = nn(dot_ref[cols, block], w_ref[blk, head, :, span])
                for side in range(2):
                    place = idx_ref[blk, 2 * duo + side]
                    lanes = slice(side * BLK, side * BLK + BLK)
                    dva_ref[place, cols, :] += dv[:, lanes]
                    dka_ref[place, cols, :] += dk[:, lanes]
            part = nt(jnp.concatenate(dss, axis=0), duo_of(k_ref, idx_ref, blk, duo, slice(None)))
            total = part if total is None else total + part
        dq = diagonal(total) * (HD ** (-0.5) / (4 * BLK))
        dpq_ref[block, :] = (dq * qslope_ref[block, :].astype(F32)).astype(BF16)
        return carry

    lax.fori_loop(0, rows // BLK, one_block, 0)
    for place in range(dva_ref.shape[0]):
        lanes = slice(place * BLK, place * BLK + BLK)
        for acc_ref, slope_ref, out_ref in (
            (dva_ref, vslope_ref, dvb_ref),
            (dka_ref, kslope_ref, dkb_ref),
        ):
            out_ref[:, lanes] = (
                acc_ref[place] * (0.5 / BLK) * slope_ref[:, lanes].astype(F32)
            ).astype(BF16)
    dvt_ref[...] = dvb_ref[:, BACK * rows :]
    dkt_ref[...] = dkb_ref[:, BACK * rows :]
    put_split(core_ref, nt(normed_ref[...], dvb_ref[...]), mine_ref, theirs_ref, 0, slice(None))
    put_split(
        core_ref, nn(normed_ref[:, BACK * rows :], dpq_ref[...]), mine_ref, theirs_ref, 1, slice(None)
    )
    put_split(core_ref, nt(normed_ref[...], dkb_ref[...]), mine_ref, theirs_ref, 2, slice(None))
    for at in range(BACK):
        lanes = slice(at * rows, at * rows + rows)
        left = jnp.concatenate([wv_ref[...], wk_ref[...]], axis=1)
        right = jnp.concatenate([dvb_ref[:, lanes], dkb_ref[:, lanes]], axis=0)
        sum_ref[at] += nn(left, right)

    @pl.when(step == pl.num_programs(0) - 1)
    def _():
        for at in range(BACK):
            done = sum_ref[at].astype(BF16)
            if first:
                part_ref[at] = done
            else:
                (far_ref, near_ref)[at][...] = done


def attend_back(start, idx, core, size, w, g, kv, do, do_t, q_t, slopes, kv_slopes, normed, w_in, part):
    rows = do.shape[0]
    nblk = rows // BLK
    places = kv.shape[0]
    first = part is None
    heads = pl.BlockSpec((nblk, 4, BLK, 4 * BLK), lambda i, *_: (0, start + i, 0, 0))
    tall = (BACK + 1) * rows
    wide = pl.BlockSpec((3, size // 2, WIDE // size, 256), lambda i, *_: (0, 0, 0, i))
    cols = pl.BlockSpec((256, rows), lambda i, *_: (i, 0))
    in_specs = [
        heads,
        heads,
        pl.BlockSpec((places, 256, BLK), lambda i, *_: (0, start + i, 0)),
        pl.BlockSpec((places, 256, BLK), lambda i, *_: (0, 4 + start + i, 0)),
        pl.BlockSpec((rows, 256), lambda i, *_: (0, start + i)),
        pl.BlockSpec((256, rows), lambda i, *_: (start + i, 0)),
        pl.BlockSpec((256, rows), lambda i, *_: (start + i, 0)),
        pl.BlockSpec((rows, 256), lambda i, *_: (0, 4 + start + i)),
        pl.BlockSpec((256, tall), lambda i, *_: (start + i, 0)),
        pl.BlockSpec((256, tall), lambda i, *_: (4 + start + i, 0)),
        whole(normed.shape),
        pl.BlockSpec((WIDE, 256), lambda i, *_: (0, 4 + start + i)),
        pl.BlockSpec((WIDE, 256), lambda i, *_: (0, 12 + start + i)),
    ]
    args = [idx, core, w, g, kv, kv, do, do_t, q_t, slopes, kv_slopes, kv_slopes, normed, w_in, w_in]
    chunk = sds((3, size // 2, WIDE // size, 512), BF16)
    out_specs = [wide, wide, pl.BlockSpec((rows, 256), lambda i, *_: (0, i)), cols, cols]
    out_shape = [chunk, chunk, sds((rows, 512), BF16), sds((512, rows), BF16), sds((512, rows), BF16)]
    if first:
        out_specs.append(whole((BACK, WIDE, rows)))
        out_shape.append(sds((BACK, WIDE, rows), BF16))
    else:
        in_specs.append(whole(part.shape))
        args.append(part)
        out_specs += [whole((WIDE, rows))] * 2
        out_shape += [sds((WIDE, rows), BF16)] * 2
    return pl.pallas_call(
        lambda *refs: bwd_kernel(*refs, first=first),
        grid_spec=pltpu.PrefetchScalarGridSpec(
            num_scalar_prefetch=2,
            grid=(2,),
            in_specs=in_specs,
            out_specs=out_specs,
            scratch_shapes=[
                pltpu.VMEM((places, 256, BLK), F32),
                pltpu.VMEM((places, 256, BLK), F32),
                pltpu.VMEM((256, tall), BF16),
                pltpu.VMEM((256, tall), BF16),
                pltpu.VMEM((BACK, WIDE, rows), F32),
            ],
        ),
        out_shape=out_shape,
        compiler_params=params(60),
        name="attend_back_%d" % start,
        cost_estimate=cost(24),
    )(*args)


def dn_u_kernel(w_ref, dpu_ref, own_ref):
    own_ref[...] = nt(w_ref[...], dpu_ref[...])


def grad_normed_u(w_in, dpu):
    rows = dpu.shape[0]
    return pl.pallas_call(
        dn_u_kernel,
        grid=(2,),
        in_specs=[pl.BlockSpec((WIDE // 2, WIDE), lambda j: (j, 0)), whole(dpu.shape)],
        out_specs=pl.BlockSpec((WIDE // 2, rows), lambda j: (j, 0)),
        out_shape=sds((WIDE, rows), F32),
        compiler_params=params(60),
        name="grad_normed_u",
        cost_estimate=cost(4),
    )(w_in, dpu)


def dn_own_kernel(w_ref, u_ref, qa_ref, qb_ref, va_ref, vb_ref, ka_ref, kb_ref, own_ref):
    step = pl.program_id(0)
    half = WIDE // 2
    left, right = w_ref[:, :half], w_ref[:, half:]

    @pl.when(step == 0)
    def _():
        own_ref[...] = u_ref[...] + nn(left, va_ref[...]) + nn(right, vb_ref[...])

    @pl.when(step == 1)
    def _():
        own_ref[...] += nt(left, qa_ref[...]) + nt(right, qb_ref[...])

    @pl.when(step == 2)
    def _():
        own_ref[...] += nn(left, ka_ref[...]) + nn(right, kb_ref[...])


def grad_normed_own(w_in, from_u, *halves):
    return pl.pallas_call(
        dn_own_kernel,
        grid=(3,),
        in_specs=[pl.BlockSpec((WIDE, WIDE), lambda j: (0, j + 1)), whole(from_u.shape)]
        + [whole(a.shape) for a in halves],
        out_specs=whole(from_u.shape),
        out_shape=sds(from_u.shape, F32),
        compiler_params=params(60),
        name="grad_normed_own",
        cost_estimate=cost(8),
    )(w_in, from_u, *halves)


def last_kernel(own_ref, a_ref, b_ref, c_ref, x_ref, grad_ref, out_ref):
    dn_t = own_ref[...] + a_ref[...].astype(F32) + b_ref[...].astype(F32) + c_ref[...].astype(F32)
    dn = dn_t.T
    cent, rstd = norm_parts(x_ref[...].astype(F32))
    z = cent * rstd
    dx = rstd * (
        dn - jnp.mean(dn, axis=-1, keepdims=True) - z * jnp.mean(dn * z, axis=-1, keepdims=True)
    )
    out_ref[...] = (grad_ref[...].astype(F32) + dx).astype(BF16)


def last(own, one, two, three, x, grad_out):
    rows = x.shape[0]
    colblk = pl.BlockSpec((WIDE, BLK), lambda b: (0, b))
    rowblk = pl.BlockSpec((BLK, WIDE), lambda b: (b, 0))
    return pl.pallas_call(
        last_kernel,
        grid=(rows // BLK,),
        in_specs=[colblk, colblk, colblk, colblk, rowblk, rowblk],
        out_specs=rowblk,
        out_shape=sds((rows, WIDE), BF16),
        compiler_params=params(60),
        name="grad_x",
        cost_estimate=cost(6),
    )(own, one, two, three, x, grad_out)


def send(array, pairs):
    return lax.ppermute(array, "seq", pairs)


class Halving:
    def __init__(self, mine, theirs, size, bits):
        self.size, self.bits, self.at = size, bits, 0
        self.left = list(range(1, size.bit_length() - 1))
        self.keep, self.got = mine, self.swap(theirs, 0)

    def swap(self, array, bit):
        return send(array, [(i, i ^ (1 << bit)) for i in range(self.size)])

    def step(self, *after):
        bit = self.bits[self.at]
        inner = 1 << self.left.index(bit)
        self.at += 1
        groups, count, height, cols = self.keep.shape
        shape = (groups, count // (2 * inner), 2, inner * height, cols)
        keep, got = self.keep.reshape(shape), self.got.reshape(shape)
        if after:
            got = tie(got, *after)
        side = (lax.axis_index("seq") >> bit) & 1

        def added(which):
            parts = [lax.dynamic_index_in_dim(a, which, 2, keepdims=False) for a in (keep, got)]
            total = parts[0].astype(F32) + parts[1].astype(F32)
            return total.astype(BF16).reshape(groups, count // 2, height, cols)

        moving = added(1 - side)
        self.keep, self.got = added(side), self.swap(moving, bit)
        self.left.remove(bit)
        return moving

    def parts(self):
        while self.at < len(self.bits):
            self.step()
        return self.keep, self.got


def finish_kernel(ek_ref, eg_ref, ak_ref, ag_ref, bk_ref, bg_ref, win_ref, wout_ref):
    def total(keep_ref, got_ref, group):
        return keep_ref[group, 0].astype(F32) + got_ref[group, 0].astype(F32)

    wout_ref[...] = total(ek_ref, eg_ref, 0)
    win_ref[:, :WIDE] = total(ek_ref, eg_ref, 1)
    for group in range(3):
        at = (group + 1) * WIDE
        win_ref[:, at : at + 512] = total(ak_ref, ag_ref, group)
        win_ref[:, at + 512 : at + WIDE] = total(bk_ref, bg_ref, group)


def finish(*sums):
    args = [a for pair in sums for a in pair]
    height = args[0].shape[2]
    return pl.pallas_call(
        finish_kernel,
        in_specs=[pl.BlockSpec(memory_space=pltpu.VMEM)] * 6,
        out_specs=[pl.BlockSpec(memory_space=pltpu.VMEM)] * 2,
        out_shape=[sds((height, 4 * WIDE), F32), sds((height, WIDE), F32)],
        compiler_params=pltpu.CompilerParams(vmem_limit_bytes=60 * MIB),
        name="finish_sums",
        cost_estimate=cost(2),
    )(*args)


def on_device(events_in, w_in, w_out, kv_list, counts, grad_out):
    size = lax.axis_size("seq")
    nblk = kv_list.shape[0]
    place = lax.axis_index("seq")
    core = (place % 2).astype(jnp.int32)[None]
    pairs = range(0, size, 2)
    live = jnp.arange(BLK, dtype=jnp.int32)[None, :] < counts[:, None]
    shown = jnp.where(live.reshape(-1)[:, None], events_in, jnp.zeros((), BF16))
    x_near = send(shown, [(i, i + 1) for i in range(size - 1)])
    x_even = send(shown, [(i, i + 2) for i in range(0, size - 2, 2)])
    x_odd = send(x_near, [(i, i + 1) for i in pairs])
    local = jnp.arange(nblk, dtype=jnp.int32)
    index = jnp.concatenate(
        [kv_list + (BACK - place) * nblk, (local + BACK * nblk)[:, None]], axis=1
    )
    index = jnp.clip(index, 0, (BACK + 1) * nblk - 1)

    kv, kv_slopes, normed, w_kv_t, acts, slopes, dy = project_own(
        counts, events_in, grad_out, w_in, w_out
    )
    x_odd = send(tie(x_near, dy), [(i, i + 1) for i in pairs])
    kv, kv_slopes, normed = project_window(
        [x_even, x_odd, x_near], w_kv_t, (kv, kv_slopes, normed)
    )
    w, g, q_t, y, dpu, do, do_t, mine, theirs = attend(
        index, core, size, acts, slopes, kv, dy, grad_out, normed
    )
    ups = list(range(1, size.bit_length() - 1))
    sum_early = Halving(mine, theirs, size, ups[1:] + ups[:1])
    from_u = grad_normed_u(w_in, tie(dpu, mine))
    sent = sum_early.step(from_u)

    def backward(start, token, part):
        return attend_back(
            start, token, core, size, w, g, kv, do, do_t, q_t, slopes, kv_slopes, normed, w_in, part
        )

    mine, theirs, qa, va, ka, part = backward(0, tie(index, sent), None)
    sent = sum_early.step(qa)
    first = Halving(mine, tie(theirs, sent), size, ups)
    events_out = events(events_in, tie(y, first.keep, sent), w_out)
    sent = first.step(events_out)
    mine, theirs, qb, vb, kb, far, near = backward(2, tie(index, sent), part)
    to_even = [(i + 1, i) for i in pairs]
    far, near, mine, theirs, sum_early.got, first.got = lax.optimization_barrier(
        (far, near, mine, theirs, sum_early.got, first.got)
    )
    far_odd = send(far, to_even)
    second = Halving(mine, theirs, size, ups)
    sent = first.step(sum_early.step(second.keep))
    sent = second.step(sent)
    joined = (tie(near, sent).astype(F32) + far_odd.astype(F32)).astype(BF16)
    back = send(joined, [(i, i - 1) for i in range(2, size, 2)])
    far_even = send(tie(far, sent), [(i + 2, i) for i in range(0, size - 2, 2)])
    near_odd = send(tie(near, sent), to_even)
    own = grad_normed_own(w_in, tie(from_u, joined), qa, qb, va, vb, ka, kb)
    own, first.got, second.got = lax.optimization_barrier((own, first.got, second.got))
    grad_x = last(own, near_odd, far_even, back, events_in, grad_out)
    grad_w_in, grad_w_out = finish(sum_early.parts(), first.parts(), second.parts())
    return (events_out, grad_x, grad_w_in, grad_w_out)


def solution(mesh):
    rows = P(("grp", "seq"), None)
    return jax.shard_map(
        on_device,
        mesh=mesh,
        in_specs=(rows, P(), P(), rows, P(("grp", "seq")), rows),
        out_specs=(rows, rows, rows, rows),
        check_vma=False,
    )
```

```python
import jax
import jax.numpy as jnp
from jax import lax
from jax.experimental import pallas as pl
from jax.experimental.pallas import tpu as pltpu
from jax.sharding import PartitionSpec as P

HEADS = 16
HD = 64
BLK = 128
WIDE = 1024
BACK = 2
EPS = 1e-05
F32 = jnp.float32
BF16 = jnp.bfloat16
MIB = 1024 * 1024


def nn(left, right):
    return lax.dot_general(left, right, (((1,), (0,)), ((), ())), preferred_element_type=F32)


def nt(left, right):
    return lax.dot_general(left, right, (((1,), (1,)), ((), ())), preferred_element_type=F32)


def params(mib):
    return pltpu.CompilerParams(dimension_semantics=("arbitrary",), vmem_limit_bytes=mib * MIB)


def cost(micros):
    return pl.CostEstimate(flops=int(micros * 1e9), transcendentals=0, bytes_accessed=1 << 20)


def tie(value, *others):
    return lax.optimization_barrier((value, *others))[0]


def whole(shape):
    zeros = (0,) * len(shape)
    return pl.BlockSpec(shape, lambda *_: zeros, pipeline_mode=pl.Buffered(1))


def sds(shape, dtype):
    return jax.ShapeDtypeStruct(shape, dtype)


def norm_parts(rows):
    mean = jnp.mean(rows, axis=-1, keepdims=True)
    cent = rows - mean
    var = jnp.mean(cent * cent, axis=-1, keepdims=True)
    return cent, lax.rsqrt(var + EPS)


def normed_of(x):
    cent, rstd = norm_parts(x.astype(F32))
    return (cent * rstd).astype(BF16)


def halved(bf):
    return bf * jnp.asarray(0.5, BF16)


def silu_both(half):
    t = jnp.tanh(half)
    p = 1.0 + t
    act = half * p
    return act, p + act * (1.0 - t)


def kv_tile(w_t, normed_t, kv_ref, slope_ref, counts_ref):
    act, slope = silu_both(0.5 * nn(w_t, normed_t))
    slope_ref[...] = slope.astype(BF16)
    lane = lax.broadcasted_iota(jnp.int32, (1, BLK), 1)
    for place in range(act.shape[1] // BLK):
        part = act[:, place * BLK : (place + 1) * BLK]
        if counts_ref is not None:
            part = jnp.where(lane < counts_ref[place], part, 0.0)
        kv_ref[place] = part.astype(BF16)


def own_kernel(
    counts_ref, x_ref, grad_ref, w_ref, wo_ref,
    kv_ref, kvslope_ref, normed_t_ref, w_t_ref, acts_ref, slope_ref, dy_ref, normed_ref,
):
    step = pl.program_id(0)

    @pl.when(step == 0)
    def _():
        normed = normed_of(x_ref[...])
        normed_ref[...] = halved(normed)
        normed_t_ref[...] = normed.T

    @pl.when(step < 4)
    def _():
        w_t_ref[...] = w_ref[...].T
        kv_tile(w_t_ref[...], normed_t_ref[...], kv_ref, kvslope_ref, counts_ref)

    @pl.when(jnp.logical_and(step >= 4, step < 8))
    def _():
        scale = jnp.where(step >= 6, HD ** (-0.5) * 0.5, 1.0).astype(F32)
        act, slope = silu_both(nn(normed_ref[...], w_ref[...]))
        acts_ref[...] = (act * scale).astype(BF16)
        slope_ref[...] = slope.astype(BF16)

    @pl.when(step >= 8)
    def _():
        dy_ref[...] = nt(grad_ref[...], wo_ref[...])


def project_own(counts, x, grad_out, w_in, w_out):
    rows = x.shape[0]
    nblk = rows // BLK

    def w_at(j, _):
        early_tile = j + 2 + 2 * (j // 2)
        later = jnp.minimum(j, 7) - 4
        return (0, jnp.where(j < 4, early_tile, later + 2 * (later // 2)))

    def up_to(last, start=0):
        return lambda j: jnp.clip(j - start, 0, last)

    kv_at, uq_at, dy_at = up_to(3), up_to(3, 4), up_to(1, 8)
    uq = pl.BlockSpec((rows, 512), lambda j, _: (0, uq_at(j)))
    return pl.pallas_call(
        own_kernel,
        grid_spec=pltpu.PrefetchScalarGridSpec(
            num_scalar_prefetch=1,
            grid=(10,),
            in_specs=[
                whole(x.shape),
                whole(grad_out.shape),
                pl.BlockSpec((WIDE, 512), w_at),
                pl.BlockSpec((512, WIDE), lambda j, _: (dy_at(j), 0)),
            ],
            out_specs=[
                pl.BlockSpec((nblk, 512, BLK), lambda j, _: (BACK, kv_at(j), 0)),
                pl.BlockSpec((512, rows), lambda j, _: (kv_at(j), BACK)),
                pl.BlockSpec((WIDE, rows), lambda j, _: (0, BACK)),
                pl.BlockSpec((512, WIDE), lambda j, _: (kv_at(j), 0)),
                uq,
                uq,
                pl.BlockSpec((rows, 512), lambda j, _: (0, dy_at(j))),
            ],
            scratch_shapes=[pltpu.VMEM((rows, WIDE), BF16)],
        ),
        out_shape=[
            sds(((BACK + 1) * nblk, 2 * WIDE, BLK), BF16),
            sds((2 * WIDE, (BACK + 1) * rows), BF16),
            sds((WIDE, (BACK + 1) * rows), BF16),
            sds((2 * WIDE, WIDE), BF16),
            sds((rows, 2 * WIDE), BF16),
            sds((rows, 2 * WIDE), BF16),
            sds((rows, WIDE), F32),
        ],
        compiler_params=params(60),
        name="project_own",
        cost_estimate=cost(13),
    )(counts, x, grad_out, w_in, w_out)


def window_kernel(
    x_even_ref, x_odd_ref, x_near_ref, w_ref, _kv, _slope, _normed,
    kv_ref, slope_ref, normed_t_ref,
):
    rows = x_near_ref.shape[0]

    @pl.when(pl.program_id(0) == 0)
    def _():
        far = x_odd_ref[...].astype(F32) + x_even_ref[...].astype(F32)
        normed_t_ref[:, :rows] = normed_of(far).T
        normed_t_ref[:, rows:] = normed_of(x_near_ref[...]).T

    kv_tile(w_ref[...], normed_t_ref[...], kv_ref, slope_ref, None)


def project_window(xs, w_kv_t, arrays):
    rows = xs[0].shape[0]
    nblk = rows // BLK
    return pl.pallas_call(
        window_kernel,
        grid=(4,),
        in_specs=[whole(x.shape) for x in xs]
        + [pl.BlockSpec((512, WIDE), lambda j: (j, 0))]
        + [pl.BlockSpec(memory_space=pl.ANY)] * 3,
        out_specs=[
            pl.BlockSpec((BACK * nblk, 512, BLK), lambda j: (0, j, 0)),
            pl.BlockSpec((512, BACK * rows), lambda j: (j, 0)),
            pl.BlockSpec((WIDE, BACK * rows), lambda j: (0, 0)),
        ],
        out_shape=[sds(a.shape, BF16) for a in arrays],
        input_output_aliases={len(xs) + 1 + i: i for i in range(3)},
        compiler_params=params(60),
        name="project_window",
        cost_estimate=cost(10),
    )(*xs, w_kv_t, *arrays)


def duo_of(ref, idx_ref, blk, duo, rows):
    return jnp.concatenate([ref[idx_ref[blk, 2 * duo + i], rows, :] for i in range(2)], axis=1)


def diagonal(quad_rows):
    left = lax.broadcasted_iota(jnp.int32, (BLK, BLK), 1) < HD
    pairs = []
    for pair in range(2):
        lanes = slice(pair * BLK, pair * BLK + BLK)
        one = quad_rows[2 * pair * BLK : (2 * pair + 1) * BLK, lanes]
        two = quad_rows[(2 * pair + 1) * BLK : (2 * pair + 2) * BLK, lanes]
        pairs.append(jnp.where(left, one, two))
    return jnp.concatenate(pairs, axis=1)


def put_split(core_ref, val, mine_ref, theirs_ref, group, cols):
    _, pieces, height, _ = mine_ref.shape
    split = val.astype(BF16).reshape(pieces, 2, height, val.shape[1])
    even, odd = split[:, 0], split[:, 1]
    first = core_ref[0] == 0
    mine_ref[group, :, :, cols] = jnp.where(first, even, odd)
    theirs_ref[group, :, :, cols] = jnp.where(first, odd, even)


def fwd_kernel(
    idx_ref, core_ref, q_ref, v_ref, k_ref, u_ref, uslope_ref, dy_ref, grad_ref, normed_ref,
    w_ref, g_ref, qt_ref, y_ref, dpu_ref, do_ref, dot_ref, mine_ref, theirs_ref,
    attn_ref, yt_ref,
):
    quad = pl.program_id(0)
    rows = y_ref.shape[0]
    row = lax.broadcasted_iota(jnp.int32, (BLK, BLK), 0)
    col = lax.broadcasted_iota(jnp.int32, (BLK, BLK), 1)
    keep = jnp.concatenate([jnp.full((BLK, BLK), True), col <= row], axis=1)
    qt_ref[...] = q_ref[...].T

    def one_block(blk, carry):
        block = pl.ds(pl.multiple_of(blk * BLK, BLK), BLK)
        total = None
        for duo in range(2):
            ws = []
            for head in range(4):
                cols = slice(head * HD, head * HD + HD)
                half = nn(q_ref[block, cols], duo_of(k_ref, idx_ref, blk, duo, cols))
                w, g = silu_both(half)
                if duo == 1:
                    w = jnp.where(keep, w, 0.0)
                    g = jnp.where(keep, g, 0.0)
                w = w.astype(BF16)
                ws.append(w)
                w_ref[blk, head, :, duo * 256 : duo * 256 + 256] = w
                g_ref[blk, head, :, duo * 256 : duo * 256 + 256] = g.astype(BF16)
            vals = duo_of(v_ref, idx_ref, blk, duo, slice(None))
            part = nt(jnp.concatenate(ws, axis=0), vals)
            total = part if total is None else total + part
        attn_ref[quad, block, :] = diagonal(total) * (1.0 / BLK)
        return carry

    lax.fori_loop(0, rows // BLK, one_block, 0)

    @pl.when(quad == pl.num_programs(0) - 1)
    def _():
        def finish_block(blk, carry):
            block = pl.ds(pl.multiple_of(blk * BLK, BLK), BLK)
            attn = jnp.concatenate([attn_ref[i, block, :] for i in range(4)], axis=1)
            cent, rstd = norm_parts(attn)
            z = cent * rstd
            u = u_ref[block, :].astype(F32)
            dy = dy_ref[block, :]
            y = (z * u).astype(BF16)
            y_ref[block, :] = y
            yt_ref[:, block] = y.T
            dpu_ref[block, :] = (dy * (0.5 * z) * uslope_ref[block, :].astype(F32)).astype(BF16)
            dz = dy * u
            shift = jnp.mean(dz, axis=-1, keepdims=True)
            dattn = rstd * (dz - shift - z * jnp.mean(dz * z, axis=-1, keepdims=True))
            dattn = dattn.astype(BF16)
            do_ref[block, :] = dattn
            dot_ref[:, block] = dattn.T
            return carry

        lax.fori_loop(0, rows // BLK, finish_block, 0)
        for group, (left_ref, right_ref) in enumerate(((yt_ref, grad_ref), (normed_ref, dpu_ref))):
            for tile in range(2):
                cols = slice(tile * 512, tile * 512 + 512)
                val = nn(left_ref[...], right_ref[:, cols])
                put_split(core_ref, val, mine_ref, theirs_ref, group, cols)


def attend(idx, core, size, acts, slopes, kv, dy, grad_out, normed):
    rows = dy.shape[0]
    nblk = rows // BLK
    places = kv.shape[0]
    scores = pl.BlockSpec((nblk, 4, BLK, 4 * BLK), lambda i, *_: (0, i, 0, 0))
    left = pl.BlockSpec((rows, WIDE), lambda *_: (0, 0), pipeline_mode=pl.Buffered(1))
    chunk = (2, size // 2, WIDE // size, WIDE)
    return pl.pallas_call(
        fwd_kernel,
        grid_spec=pltpu.PrefetchScalarGridSpec(
            num_scalar_prefetch=2,
            grid=(HEADS // 4,),
            in_specs=[
                pl.BlockSpec((rows, 256), lambda i, *_: (0, 4 + i)),
                pl.BlockSpec((places, 256, BLK), lambda i, *_: (0, i, 0)),
                pl.BlockSpec((places, 256, BLK), lambda i, *_: (0, 4 + i, 0)),
                left,
                left,
                left,
                left,
                pl.BlockSpec((WIDE, rows), lambda *_: (0, BACK), pipeline_mode=pl.Buffered(1)),
            ],
            out_specs=[
                scores,
                scores,
                pl.BlockSpec((256, rows), lambda i, *_: (i, 0)),
                left,
                left,
                left,
                whole((WIDE, rows)),
                whole(chunk),
                whole(chunk),
            ],
            scratch_shapes=[
                pltpu.VMEM((HEADS // 4, rows, 256), F32),
                pltpu.VMEM((WIDE, rows), BF16),
            ],
        ),
        out_shape=[
            sds((nblk, HEADS, BLK, 4 * BLK), BF16),
            sds((nblk, HEADS, BLK, 4 * BLK), BF16),
            sds((WIDE, rows), BF16),
            sds((rows, WIDE), BF16),
            sds((rows, WIDE), BF16),
            sds((rows, WIDE), BF16),
            sds((WIDE, rows), BF16),
            sds(chunk, BF16),
            sds(chunk, BF16),
        ],
        compiler_params=params(60),
        name="attend",
        cost_estimate=cost(18),
    )(idx, core, acts, kv, kv, acts, slopes, dy, grad_out, normed)


def events_kernel(x_ref, y_ref, wo_ref, ev_ref):
    ev_ref[...] = (x_ref[...].astype(F32) + nn(y_ref[...], wo_ref[...])).astype(BF16)


def events(x, y, w_out):
    rows = x.shape[0]
    tile = pl.BlockSpec((rows, 512), lambda j: (0, j))
    return pl.pallas_call(
        events_kernel,
        grid=(2,),
        in_specs=[tile, whole(y.shape), pl.BlockSpec((WIDE, 512), lambda j: (0, j))],
        out_specs=tile,
        out_shape=sds((rows, WIDE), BF16),
        compiler_params=params(60),
        name="events_out",
        cost_estimate=cost(4),
    )(x, y, w_out)


def bwd_kernel(*refs, first):
    (idx_ref, core_ref, w_ref, g_ref, v_ref, k_ref, do_ref, dot_ref, qt_ref, qslope_ref) = refs[:10]
    (vslope_ref, kslope_ref, normed_ref, wv_ref, wk_ref) = refs[10:15]
    rest = refs[15:]
    if first:
        part_ref = rest[5]
        rest = rest[:5] + rest[6:]
    else:
        part_ref, far_ref, near_ref = rest[0], rest[6], rest[7]
        rest = rest[1:6] + rest[8:]
    (mine_ref, theirs_ref, dpq_ref, dvt_ref, dkt_ref) = rest[:5]
    (dva_ref, dka_ref, dvb_ref, dkb_ref, sum_ref) = rest[5:]
    step = pl.program_id(0)
    rows = dpq_ref.shape[0]
    dva_ref[...] = jnp.zeros_like(dva_ref)
    dka_ref[...] = jnp.zeros_like(dka_ref)

    @pl.when(step == 0)
    def _():
        sum_ref[...] = jnp.zeros_like(sum_ref) if first else part_ref[...].astype(F32)

    def one_block(blk, carry):
        at = pl.multiple_of(blk * BLK, BLK)
        block = pl.ds(at, BLK)
        total = None
        for duo in range(2):
            span = slice(duo * 256, duo * 256 + 256)
            dss = []
            for head in range(4):
                cols = slice(head * HD, head * HD + HD)
                dw = nn(do_ref[block, cols], duo_of(v_ref, idx_ref, blk, duo, cols))
                ds = (dw * g_ref[blk, head, :, span].astype(F32)).astype(BF16)
                dss.append(ds)
                dk = nn(qt_ref[cols, block], ds)
                dv = nn(dot_ref[cols, block], w_ref[blk, head, :, span])
                for side in range(2):
                    place = idx_ref[blk, 2 * duo + side]
                    lanes = slice(side * BLK, side * BLK + BLK)
                    dva_ref[place, cols, :] += dv[:, lanes]
                    dka_ref[place, cols, :] += dk[:, lanes]
            part = nt(jnp.concatenate(dss, axis=0), duo_of(k_ref, idx_ref, blk, duo, slice(None)))
            total = part if total is None else total + part
        dq = diagonal(total) * (HD ** (-0.5) / (4 * BLK))
        dpq_ref[block, :] = (dq * qslope_ref[block, :].astype(F32)).astype(BF16)
        return carry

    lax.fori_loop(0, rows // BLK, one_block, 0)
    for place in range(dva_ref.shape[0]):
        lanes = slice(place * BLK, place * BLK + BLK)
        for acc_ref, slope_ref, out_ref in (
            (dva_ref, vslope_ref, dvb_ref),
            (dka_ref, kslope_ref, dkb_ref),
        ):
            out_ref[:, lanes] = (
                acc_ref[place] * (0.5 / BLK) * slope_ref[:, lanes].astype(F32)
            ).astype(BF16)
    dvt_ref[...] = dvb_ref[:, BACK * rows :]
    dkt_ref[...] = dkb_ref[:, BACK * rows :]
    put_split(core_ref, nt(normed_ref[...], dvb_ref[...]), mine_ref, theirs_ref, 0, slice(None))
    put_split(
        core_ref, nn(normed_ref[:, BACK * rows :], dpq_ref[...]), mine_ref, theirs_ref, 1, slice(None)
    )
    put_split(core_ref, nt(normed_ref[...], dkb_ref[...]), mine_ref, theirs_ref, 2, slice(None))
    for at in range(BACK):
        lanes = slice(at * rows, at * rows + rows)
        left = jnp.concatenate([wv_ref[...], wk_ref[...]], axis=1)
        right = jnp.concatenate([dvb_ref[:, lanes], dkb_ref[:, lanes]], axis=0)
        sum_ref[at] += nn(left, right)

    @pl.when(step == pl.num_programs(0) - 1)
    def _():
        for at in range(BACK):
            done = sum_ref[at].astype(BF16)
            if first:
                part_ref[at] = done
            else:
                (far_ref, near_ref)[at][...] = done


def attend_back(start, idx, core, size, w, g, kv, do, do_t, q_t, slopes, kv_slopes, normed, w_in, part):
    rows = do.shape[0]
    nblk = rows // BLK
    places = kv.shape[0]
    first = part is None
    heads = pl.BlockSpec((nblk, 4, BLK, 4 * BLK), lambda i, *_: (0, start + i, 0, 0))
    tall = (BACK + 1) * rows
    wide = pl.BlockSpec((3, size // 2, WIDE // size, 256), lambda i, *_: (0, 0, 0, i))
    cols = pl.BlockSpec((256, rows), lambda i, *_: (i, 0))
    in_specs = [
        heads,
        heads,
        pl.BlockSpec((places, 256, BLK), lambda i, *_: (0, start + i, 0)),
        pl.BlockSpec((places, 256, BLK), lambda i, *_: (0, 4 + start + i, 0)),
        pl.BlockSpec((rows, 256), lambda i, *_: (0, start + i)),
        pl.BlockSpec((256, rows), lambda i, *_: (start + i, 0)),
        pl.BlockSpec((256, rows), lambda i, *_: (start + i, 0)),
        pl.BlockSpec((rows, 256), lambda i, *_: (0, 4 + start + i)),
        pl.BlockSpec((256, tall), lambda i, *_: (start + i, 0)),
        pl.BlockSpec((256, tall), lambda i, *_: (4 + start + i, 0)),
        whole(normed.shape),
        pl.BlockSpec((WIDE, 256), lambda i, *_: (0, 4 + start + i)),
        pl.BlockSpec((WIDE, 256), lambda i, *_: (0, 12 + start + i)),
    ]
    args = [idx, core, w, g, kv, kv, do, do_t, q_t, slopes, kv_slopes, kv_slopes, normed, w_in, w_in]
    chunk = sds((3, size // 2, WIDE // size, 512), BF16)
    out_specs = [wide, wide, pl.BlockSpec((rows, 256), lambda i, *_: (0, i)), cols, cols]
    out_shape = [chunk, chunk, sds((rows, 512), BF16), sds((512, rows), BF16), sds((512, rows), BF16)]
    if first:
        out_specs.append(whole((BACK, WIDE, rows)))
        out_shape.append(sds((BACK, WIDE, rows), BF16))
    else:
        in_specs.append(whole(part.shape))
        args.append(part)
        out_specs += [whole((WIDE, rows))] * 2
        out_shape += [sds((WIDE, rows), BF16)] * 2
    return pl.pallas_call(
        lambda *refs: bwd_kernel(*refs, first=first),
        grid_spec=pltpu.PrefetchScalarGridSpec(
            num_scalar_prefetch=2,
            grid=(2,),
            in_specs=in_specs,
            out_specs=out_specs,
            scratch_shapes=[
                pltpu.VMEM((places, 256, BLK), F32),
                pltpu.VMEM((places, 256, BLK), F32),
                pltpu.VMEM((256, tall), BF16),
                pltpu.VMEM((256, tall), BF16),
                pltpu.VMEM((BACK, WIDE, rows), F32),
            ],
        ),
        out_shape=out_shape,
        compiler_params=params(60),
        name="attend_back_%d" % start,
        cost_estimate=cost(24),
    )(*args)


def dn_u_kernel(w_ref, dpu_ref, own_ref):
    own_ref[...] = nt(w_ref[...], dpu_ref[...])


def grad_normed_u(w_in, dpu):
    rows = dpu.shape[0]
    return pl.pallas_call(
        dn_u_kernel,
        grid=(2,),
        in_specs=[pl.BlockSpec((WIDE // 2, WIDE), lambda j: (j, 0)), whole(dpu.shape)],
        out_specs=pl.BlockSpec((WIDE // 2, rows), lambda j: (j, 0)),
        out_shape=sds((WIDE, rows), F32),
        compiler_params=params(60),
        name="grad_normed_u",
        cost_estimate=cost(4),
    )(w_in, dpu)


def dn_own_kernel(w_ref, u_ref, qa_ref, qb_ref, va_ref, vb_ref, ka_ref, kb_ref, own_ref):
    step = pl.program_id(0)
    half = WIDE // 2
    left, right = w_ref[:, :half], w_ref[:, half:]

    @pl.when(step == 0)
    def _():
        own_ref[...] = u_ref[...] + nn(left, va_ref[...]) + nn(right, vb_ref[...])

    @pl.when(step == 1)
    def _():
        own_ref[...] += nt(left, qa_ref[...]) + nt(right, qb_ref[...])

    @pl.when(step == 2)
    def _():
        own_ref[...] += nn(left, ka_ref[...]) + nn(right, kb_ref[...])


def grad_normed_own(w_in, from_u, *halves):
    return pl.pallas_call(
        dn_own_kernel,
        grid=(3,),
        in_specs=[pl.BlockSpec((WIDE, WIDE), lambda j: (0, j + 1)), whole(from_u.shape)]
        + [whole(a.shape) for a in halves],
        out_specs=whole(from_u.shape),
        out_shape=sds(from_u.shape, F32),
        compiler_params=params(60),
        name="grad_normed_own",
        cost_estimate=cost(8),
    )(w_in, from_u, *halves)


def last_kernel(own_ref, a_ref, b_ref, c_ref, x_ref, grad_ref, out_ref):
    dn_t = own_ref[...] + a_ref[...].astype(F32) + b_ref[...].astype(F32) + c_ref[...].astype(F32)
    dn = dn_t.T
    cent, rstd = norm_parts(x_ref[...].astype(F32))
    z = cent * rstd
    dx = rstd * (
        dn - jnp.mean(dn, axis=-1, keepdims=True) - z * jnp.mean(dn * z, axis=-1, keepdims=True)
    )
    out_ref[...] = (grad_ref[...].astype(F32) + dx).astype(BF16)


def last(own, one, two, three, x, grad_out):
    rows = x.shape[0]
    colblk = pl.BlockSpec((WIDE, BLK), lambda b: (0, b))
    rowblk = pl.BlockSpec((BLK, WIDE), lambda b: (b, 0))
    return pl.pallas_call(
        last_kernel,
        grid=(rows // BLK,),
        in_specs=[colblk, colblk, colblk, colblk, rowblk, rowblk],
        out_specs=rowblk,
        out_shape=sds((rows, WIDE), BF16),
        compiler_params=params(60),
        name="grad_x",
        cost_estimate=cost(6),
    )(own, one, two, three, x, grad_out)


def send(array, pairs):
    return lax.ppermute(array, "seq", pairs)


class Halving:
    def __init__(self, mine, theirs, size, bits):
        self.size, self.bits, self.at = size, bits, 0
        self.left = list(range(1, size.bit_length() - 1))
        self.keep, self.got = mine, self.swap(theirs, 0)

    def swap(self, array, bit):
        return send(array, [(i, i ^ (1 << bit)) for i in range(self.size)])

    def step(self, *after):
        bit = self.bits[self.at]
        inner = 1 << self.left.index(bit)
        self.at += 1
        groups, count, height, cols = self.keep.shape
        shape = (groups, count // (2 * inner), 2, inner * height, cols)
        keep, got = self.keep.reshape(shape), self.got.reshape(shape)
        if after:
            got = tie(got, *after)
        side = (lax.axis_index("seq") >> bit) & 1

        def added(which):
            parts = [lax.dynamic_index_in_dim(a, which, 2, keepdims=False) for a in (keep, got)]
            total = parts[0].astype(F32) + parts[1].astype(F32)
            return total.astype(BF16).reshape(groups, count // 2, height, cols)

        moving = added(1 - side)
        self.keep, self.got = added(side), self.swap(moving, bit)
        self.left.remove(bit)
        return moving

    def parts(self):
        while self.at < len(self.bits):
            self.step()
        return self.keep, self.got


def finish_kernel(ek_ref, eg_ref, ak_ref, ag_ref, bk_ref, bg_ref, win_ref, wout_ref):
    def total(keep_ref, got_ref, group):
        return keep_ref[group, 0].astype(F32) + got_ref[group, 0].astype(F32)

    wout_ref[...] = total(ek_ref, eg_ref, 0)
    win_ref[:, :WIDE] = total(ek_ref, eg_ref, 1)
    for group in range(3):
        at = (group + 1) * WIDE
        win_ref[:, at : at + 512] = total(ak_ref, ag_ref, group)
        win_ref[:, at + 512 : at + WIDE] = total(bk_ref, bg_ref, group)


def finish(*sums):
    args = [a for pair in sums for a in pair]
    height = args[0].shape[2]
    return pl.pallas_call(
        finish_kernel,
        in_specs=[pl.BlockSpec(memory_space=pltpu.VMEM)] * 6,
        out_specs=[pl.BlockSpec(memory_space=pltpu.VMEM)] * 2,
        out_shape=[sds((height, 4 * WIDE), F32), sds((height, WIDE), F32)],
        compiler_params=pltpu.CompilerParams(vmem_limit_bytes=60 * MIB),
        name="finish_sums",
        cost_estimate=cost(2),
    )(*args)


def on_device(events_in, w_in, w_out, kv_list, counts, grad_out):
    size = lax.axis_size("seq")
    nblk = kv_list.shape[0]
    place = lax.axis_index("seq")
    core = (place % 2).astype(jnp.int32)[None]
    pairs = range(0, size, 2)
    live = jnp.arange(BLK, dtype=jnp.int32)[None, :] < counts[:, None]
    shown = jnp.where(live.reshape(-1)[:, None], events_in, jnp.zeros((), BF16))
    x_near = send(shown, [(i, i + 1) for i in range(size - 1)])
    x_even = send(shown, [(i, i + 2) for i in range(0, size - 2, 2)])
    x_odd = send(x_near, [(i, i + 1) for i in pairs])
    local = jnp.arange(nblk, dtype=jnp.int32)
    index = jnp.concatenate(
        [kv_list + (BACK - place) * nblk, (local + BACK * nblk)[:, None]], axis=1
    )
    index = jnp.clip(index, 0, (BACK + 1) * nblk - 1)

    kv, kv_slopes, normed, w_kv_t, acts, slopes, dy = project_own(
        counts, events_in, grad_out, w_in, w_out
    )
    x_odd = send(tie(x_near, dy), [(i, i + 1) for i in pairs])
    kv, kv_slopes, normed = project_window(
        [x_even, x_odd, x_near], w_kv_t, (kv, kv_slopes, normed)
    )
    w, g, q_t, y, dpu, do, do_t, mine, theirs = attend(
        index, core, size, acts, slopes, kv, dy, grad_out, normed
    )
    ups = list(range(1, size.bit_length() - 1))
    sum_early = Halving(mine, theirs, size, ups[1:] + ups[:1])
    from_u = grad_normed_u(w_in, tie(dpu, mine))
    sent = sum_early.step(from_u)

    def backward(start, token, part):
        return attend_back(
            start, token, core, size, w, g, kv, do, do_t, q_t, slopes, kv_slopes, normed, w_in, part
        )

    mine, theirs, qa, va, ka, part = backward(0, tie(index, sent), None)
    sent = sum_early.step(qa)
    first = Halving(mine, tie(theirs, sent), size, ups)
    events_out = events(events_in, tie(y, first.keep, sent), w_out)
    sent = first.step(events_out)
    mine, theirs, qb, vb, kb, far, near = backward(2, tie(index, sent), part)
    to_even = [(i + 1, i) for i in pairs]
    far, near, mine, theirs, sum_early.got, first.got = lax.optimization_barrier(
        (far, near, mine, theirs, sum_early.got, first.got)
    )
    far_odd = send(far, to_even)
    second = Halving(mine, theirs, size, ups)
    sent = first.step(sum_early.step(second.keep))
    sent = second.step(sent)
    joined = (tie(near, sent).astype(F32) + far_odd.astype(F32)).astype(BF16)
    own = grad_normed_own(w_in, tie(from_u, joined), qa, qb, va, vb, ka, kb)
    own, sum_early.got, first.got, second.got = lax.optimization_barrier(
        (own, sum_early.got, first.got, second.got)
    )
    sent = second.step()
    back = send(tie(joined, sent), [(i, i - 1) for i in range(2, size, 2)])
    far_even = send(tie(far, sent), [(i + 2, i) for i in range(0, size - 2, 2)])
    near_odd = send(tie(near, sent), to_even)
    grad_x = last(own, near_odd, far_even, back, events_in, grad_out)
    grad_w_in, grad_w_out = finish(sum_early.parts(), first.parts(), second.parts())
    return (events_out, grad_x, grad_w_in, grad_w_out)


def solution(mesh):
    rows = P(("grp", "seq"), None)
    return jax.shard_map(
        on_device,
        mesh=mesh,
        in_specs=(rows, P(), P(), rows, P(("grp", "seq")), rows),
        out_specs=(rows, rows, rows, rows),
        check_vma=False,
    )
```

```python
import jax
import jax.numpy as jnp
from jax import lax
from jax.experimental import pallas as pl
from jax.experimental.pallas import tpu as pltpu
from jax.sharding import PartitionSpec as P

HEADS = 16
HD = 64
BLK = 128
WIDE = 1024
BACK = 2
EPS = 1e-05
F32 = jnp.float32
BF16 = jnp.bfloat16
MIB = 1024 * 1024


def nn(left, right):
    return lax.dot_general(left, right, (((1,), (0,)), ((), ())), preferred_element_type=F32)


def nt(left, right):
    return lax.dot_general(left, right, (((1,), (1,)), ((), ())), preferred_element_type=F32)


def params(mib):
    return pltpu.CompilerParams(dimension_semantics=("arbitrary",), vmem_limit_bytes=mib * MIB)


def cost(micros):
    return pl.CostEstimate(flops=int(micros * 1e9), transcendentals=0, bytes_accessed=1 << 20)


def tie(value, *others):
    return lax.optimization_barrier((value, *others))[0]


def whole(shape):
    zeros = (0,) * len(shape)
    return pl.BlockSpec(shape, lambda *_: zeros, pipeline_mode=pl.Buffered(1))


def sds(shape, dtype):
    return jax.ShapeDtypeStruct(shape, dtype)


def norm_parts(rows):
    mean = jnp.mean(rows, axis=-1, keepdims=True)
    cent = rows - mean
    var = jnp.mean(cent * cent, axis=-1, keepdims=True)
    return cent, lax.rsqrt(var + EPS)


def normed_of(x):
    cent, rstd = norm_parts(x.astype(F32))
    return (cent * rstd).astype(BF16)


def halved(bf):
    return bf * jnp.asarray(0.5, BF16)


def silu_both(half):
    t = jnp.tanh(half)
    p = 1.0 + t
    act = half * p
    return act, p + act * (1.0 - t)


def kv_tile(w_t, normed_t, kv_ref, slope_ref, counts_ref):
    act, slope = silu_both(0.5 * nn(w_t, normed_t))
    slope_ref[...] = slope.astype(BF16)
    lane = lax.broadcasted_iota(jnp.int32, (1, BLK), 1)
    for place in range(act.shape[1] // BLK):
        part = act[:, place * BLK : (place + 1) * BLK]
        if counts_ref is not None:
            part = jnp.where(lane < counts_ref[place], part, 0.0)
        kv_ref[place] = part.astype(BF16)


def own_kernel(
    counts_ref, x_ref, grad_ref, w_ref, wo_ref,
    kv_ref, kvslope_ref, normed_t_ref, w_t_ref, acts_ref, slope_ref, dy_ref, normed_ref,
):
    step = pl.program_id(0)

    @pl.when(step == 0)
    def _():
        normed = normed_of(x_ref[...])
        normed_ref[...] = halved(normed)
        normed_t_ref[...] = normed.T

    @pl.when(step < 4)
    def _():
        w_t_ref[...] = w_ref[...].T
        kv_tile(w_t_ref[...], normed_t_ref[...], kv_ref, kvslope_ref, counts_ref)

    @pl.when(jnp.logical_and(step >= 4, step < 8))
    def _():
        scale = jnp.where(step >= 6, HD ** (-0.5) * 0.5, 1.0).astype(F32)
        act, slope = silu_both(nn(normed_ref[...], w_ref[...]))
        acts_ref[...] = (act * scale).astype(BF16)
        slope_ref[...] = slope.astype(BF16)

    @pl.when(step >= 8)
    def _():
        dy_ref[...] = nt(grad_ref[...], wo_ref[...])


def project_own(counts, x, grad_out, w_in, w_out):
    rows = x.shape[0]
    nblk = rows // BLK

    def w_at(j, _):
        early_tile = j + 2 + 2 * (j // 2)
        later = jnp.minimum(j, 7) - 4
        return (0, jnp.where(j < 4, early_tile, later + 2 * (later // 2)))

    def up_to(last, start=0):
        return lambda j: jnp.clip(j - start, 0, last)

    kv_at, uq_at, dy_at = up_to(3), up_to(3, 4), up_to(1, 8)
    uq = pl.BlockSpec((rows, 512), lambda j, _: (0, uq_at(j)))
    return pl.pallas_call(
        own_kernel,
        grid_spec=pltpu.PrefetchScalarGridSpec(
            num_scalar_prefetch=1,
            grid=(10,),
            in_specs=[
                whole(x.shape),
                whole(grad_out.shape),
                pl.BlockSpec((WIDE, 512), w_at),
                pl.BlockSpec((512, WIDE), lambda j, _: (dy_at(j), 0)),
            ],
            out_specs=[
                pl.BlockSpec((nblk, 512, BLK), lambda j, _: (BACK, kv_at(j), 0)),
                pl.BlockSpec((512, rows), lambda j, _: (kv_at(j), BACK)),
                pl.BlockSpec((WIDE, rows), lambda j, _: (0, BACK)),
                pl.BlockSpec((512, WIDE), lambda j, _: (kv_at(j), 0)),
                uq,
                uq,
                pl.BlockSpec((rows, 512), lambda j, _: (0, dy_at(j))),
            ],
            scratch_shapes=[pltpu.VMEM((rows, WIDE), BF16)],
        ),
        out_shape=[
            sds(((BACK + 1) * nblk, 2 * WIDE, BLK), BF16),
            sds((2 * WIDE, (BACK + 1) * rows), BF16),
            sds((WIDE, (BACK + 1) * rows), BF16),
            sds((2 * WIDE, WIDE), BF16),
            sds((rows, 2 * WIDE), BF16),
            sds((rows, 2 * WIDE), BF16),
            sds((rows, WIDE), F32),
        ],
        compiler_params=params(60),
        name="project_own",
        cost_estimate=cost(13),
    )(counts, x, grad_out, w_in, w_out)


def window_kernel(
    x_even_ref, x_odd_ref, x_near_ref, w_ref, _kv, _slope, _normed,
    kv_ref, slope_ref, normed_t_ref,
):
    rows = x_near_ref.shape[0]

    @pl.when(pl.program_id(0) == 0)
    def _():
        far = x_odd_ref[...].astype(F32) + x_even_ref[...].astype(F32)
        normed_t_ref[:, :rows] = normed_of(far).T
        normed_t_ref[:, rows:] = normed_of(x_near_ref[...]).T

    kv_tile(w_ref[...], normed_t_ref[...], kv_ref, slope_ref, None)


def project_window(xs, w_kv_t, arrays):
    rows = xs[0].shape[0]
    nblk = rows // BLK
    return pl.pallas_call(
        window_kernel,
        grid=(4,),
        in_specs=[whole(x.shape) for x in xs]
        + [pl.BlockSpec((512, WIDE), lambda j: (j, 0))]
        + [pl.BlockSpec(memory_space=pl.ANY)] * 3,
        out_specs=[
            pl.BlockSpec((BACK * nblk, 512, BLK), lambda j: (0, j, 0)),
            pl.BlockSpec((512, BACK * rows), lambda j: (j, 0)),
            pl.BlockSpec((WIDE, BACK * rows), lambda j: (0, 0)),
        ],
        out_shape=[sds(a.shape, BF16) for a in arrays],
        input_output_aliases={len(xs) + 1 + i: i for i in range(3)},
        compiler_params=params(60),
        name="project_window",
        cost_estimate=cost(10),
    )(*xs, w_kv_t, *arrays)


def duo_of(ref, idx_ref, blk, duo, rows):
    return jnp.concatenate([ref[idx_ref[blk, 2 * duo + i], rows, :] for i in range(2)], axis=1)


def diagonal(quad_rows):
    left = lax.broadcasted_iota(jnp.int32, (BLK, BLK), 1) < HD
    pairs = []
    for pair in range(2):
        lanes = slice(pair * BLK, pair * BLK + BLK)
        one = quad_rows[2 * pair * BLK : (2 * pair + 1) * BLK, lanes]
        two = quad_rows[(2 * pair + 1) * BLK : (2 * pair + 2) * BLK, lanes]
        pairs.append(jnp.where(left, one, two))
    return jnp.concatenate(pairs, axis=1)


def put_split(core_ref, val, mine_ref, theirs_ref, group, cols):
    _, pieces, height, _ = mine_ref.shape
    split = val.astype(BF16).reshape(pieces, 2, height, val.shape[1])
    even, odd = split[:, 0], split[:, 1]
    first = core_ref[0] == 0
    mine_ref[group, :, :, cols] = jnp.where(first, even, odd)
    theirs_ref[group, :, :, cols] = jnp.where(first, odd, even)


def fwd_kernel(
    idx_ref, core_ref, q_ref, kv_ref, u_ref, uslope_ref, dy_ref, grad_ref, normed_ref,
    w_ref, g_ref, qt_ref, y_ref, dpu_ref, do_ref, dot_ref, mine_ref, theirs_ref,
    attn_ref, yt_ref, dpu_all_ref,
):
    blk = pl.program_id(0)
    row = lax.broadcasted_iota(jnp.int32, (BLK, BLK), 0)
    col = lax.broadcasted_iota(jnp.int32, (BLK, BLK), 1)
    keep = jnp.concatenate([jnp.full((BLK, BLK), True), col <= row], axis=1)
    qt_ref[...] = q_ref[...].T
    for quad in range(HEADS // 4):
        at = quad * 256
        total = None
        for duo in range(2):
            span = slice(duo * 256, duo * 256 + 256)
            ws = []
            for head in range(4 * quad, 4 * quad + 4):
                cols = slice(head * HD, head * HD + HD)
                keys = duo_of(kv_ref, idx_ref, blk, duo, slice(WIDE + head * HD, WIDE + head * HD + HD))
                w, g = silu_both(nn(q_ref[:, cols], keys))
                if duo == 1:
                    w = jnp.where(keep, w, 0.0)
                    g = jnp.where(keep, g, 0.0)
                w = w.astype(BF16)
                ws.append(w)
                w_ref[0, head, :, span] = w
                g_ref[0, head, :, span] = g.astype(BF16)
            vals = duo_of(kv_ref, idx_ref, blk, duo, slice(at, at + 256))
            part = nt(jnp.concatenate(ws, axis=0), vals)
            total = part if total is None else total + part
        attn_ref[:, at : at + 256] = diagonal(total) * (1.0 / BLK)
    cent, rstd = norm_parts(attn_ref[...])
    z = cent * rstd
    u = u_ref[...].astype(F32)
    dy = dy_ref[...]
    y = (z * u).astype(BF16)
    y_ref[...] = y
    here = pl.ds(pl.multiple_of(blk * BLK, BLK), BLK)
    yt_ref[:, here] = y.T
    dpu = (dy * (0.5 * z) * uslope_ref[...].astype(F32)).astype(BF16)
    dpu_ref[...] = dpu
    dpu_all_ref[here, :] = dpu
    dz = dy * u
    shift = jnp.mean(dz, axis=-1, keepdims=True)
    dattn = rstd * (dz - shift - z * jnp.mean(dz * z, axis=-1, keepdims=True))
    dattn = dattn.astype(BF16)
    do_ref[...] = dattn
    dot_ref[...] = dattn.T

    @pl.when(blk == pl.num_programs(0) - 1)
    def _():
        for group, (left_ref, right_ref) in enumerate(
            ((yt_ref, grad_ref), (normed_ref, dpu_all_ref))
        ):
            for tile in range(2):
                cols = slice(tile * 512, tile * 512 + 512)
                val = nn(left_ref[...], right_ref[:, cols])
                put_split(core_ref, val, mine_ref, theirs_ref, group, cols)


def attend(idx, core, size, acts, slopes, kv, dy, grad_out, normed):
    rows = dy.shape[0]
    nblk = rows // BLK
    scores = pl.BlockSpec((1, HEADS, BLK, 4 * BLK), lambda b, *_: (b, 0, 0, 0))
    rowblk = pl.BlockSpec((BLK, WIDE), lambda b, *_: (b, 0))
    colblk = pl.BlockSpec((WIDE, BLK), lambda b, *_: (0, b))
    chunk = (2, size // 2, WIDE // size, WIDE)
    return pl.pallas_call(
        fwd_kernel,
        grid_spec=pltpu.PrefetchScalarGridSpec(
            num_scalar_prefetch=2,
            grid=(nblk,),
            in_specs=[
                pl.BlockSpec((BLK, WIDE), lambda b, *_: (b, 1)),
                whole(kv.shape),
                rowblk,
                rowblk,
                rowblk,
                whole(grad_out.shape),
                pl.BlockSpec((WIDE, rows), lambda *_: (0, BACK), pipeline_mode=pl.Buffered(1)),
            ],
            out_specs=[
                scores, scores, colblk, rowblk, rowblk, rowblk, colblk, whole(chunk), whole(chunk)
            ],
            scratch_shapes=[
                pltpu.VMEM((BLK, WIDE), F32),
                pltpu.VMEM((WIDE, rows), BF16),
                pltpu.VMEM((rows, WIDE), BF16),
            ],
        ),
        out_shape=[
            sds((nblk, HEADS, BLK, 4 * BLK), BF16),
            sds((nblk, HEADS, BLK, 4 * BLK), BF16),
            sds((WIDE, rows), BF16),
            sds((rows, WIDE), BF16),
            sds((rows, WIDE), BF16),
            sds((rows, WIDE), BF16),
            sds((WIDE, rows), BF16),
            sds(chunk, BF16),
            sds(chunk, BF16),
        ],
        compiler_params=params(60),
        name="attend",
        cost_estimate=cost(18),
    )(idx, core, acts, kv, acts, slopes, dy, grad_out, normed)


def events_kernel(x_ref, y_ref, wo_ref, ev_ref):
    ev_ref[...] = (x_ref[...].astype(F32) + nn(y_ref[...], wo_ref[...])).astype(BF16)


def events(x, y, w_out):
    rows = x.shape[0]
    tile = pl.BlockSpec((rows, 512), lambda j: (0, j))
    return pl.pallas_call(
        events_kernel,
        grid=(2,),
        in_specs=[tile, whole(y.shape), pl.BlockSpec((WIDE, 512), lambda j: (0, j))],
        out_specs=tile,
        out_shape=sds((rows, WIDE), BF16),
        compiler_params=params(60),
        name="events_out",
        cost_estimate=cost(4),
    )(x, y, w_out)


def bwd_kernel(*refs, first):
    (idx_ref, core_ref, w_ref, g_ref, v_ref, k_ref, do_ref, dot_ref, qt_ref, qslope_ref) = refs[:10]
    (vslope_ref, kslope_ref, normed_ref, wv_ref, wk_ref) = refs[10:15]
    rest = refs[15:]
    if first:
        part_ref = rest[5]
        rest = rest[:5] + rest[6:]
    else:
        part_ref, far_ref, near_ref = rest[0], rest[6], rest[7]
        rest = rest[1:6] + rest[8:]
    (mine_ref, theirs_ref, dpq_ref, dvt_ref, dkt_ref) = rest[:5]
    (dva_ref, dka_ref, dvb_ref, dkb_ref, sum_ref) = rest[5:]
    step = pl.program_id(0)
    rows = dpq_ref.shape[0]
    dva_ref[...] = jnp.zeros_like(dva_ref)
    dka_ref[...] = jnp.zeros_like(dka_ref)

    @pl.when(step == 0)
    def _():
        sum_ref[...] = jnp.zeros_like(sum_ref) if first else part_ref[...].astype(F32)

    def one_block(blk, carry):
        at = pl.multiple_of(blk * BLK, BLK)
        block = pl.ds(at, BLK)
        total = None
        for duo in range(2):
            span = slice(duo * 256, duo * 256 + 256)
            dss = []
            for head in range(4):
                cols = slice(head * HD, head * HD + HD)
                dw = nn(do_ref[block, cols], duo_of(v_ref, idx_ref, blk, duo, cols))
                ds = (dw * g_ref[blk, head, :, span].astype(F32)).astype(BF16)
                dss.append(ds)
                dk = nn(qt_ref[cols, block], ds)
                dv = nn(dot_ref[cols, block], w_ref[blk, head, :, span])
                for side in range(2):
                    place = idx_ref[blk, 2 * duo + side]
                    lanes = slice(side * BLK, side * BLK + BLK)
                    dva_ref[place, cols, :] += dv[:, lanes]
                    dka_ref[place, cols, :] += dk[:, lanes]
            part = nt(jnp.concatenate(dss, axis=0), duo_of(k_ref, idx_ref, blk, duo, slice(None)))
            total = part if total is None else total + part
        dq = diagonal(total) * (HD ** (-0.5) / (4 * BLK))
        dpq_ref[block, :] = (dq * qslope_ref[block, :].astype(F32)).astype(BF16)
        return carry

    lax.fori_loop(0, rows // BLK, one_block, 0)
    for place in range(dva_ref.shape[0]):
        lanes = slice(place * BLK, place * BLK + BLK)
        for acc_ref, slope_ref, out_ref in (
            (dva_ref, vslope_ref, dvb_ref),
            (dka_ref, kslope_ref, dkb_ref),
        ):
            out_ref[:, lanes] = (
                acc_ref[place] * (0.5 / BLK) * slope_ref[:, lanes].astype(F32)
            ).astype(BF16)
    dvt_ref[...] = dvb_ref[:, BACK * rows :]
    dkt_ref[...] = dkb_ref[:, BACK * rows :]
    put_split(core_ref, nt(normed_ref[...], dvb_ref[...]), mine_ref, theirs_ref, 0, slice(None))
    put_split(
        core_ref, nn(normed_ref[:, BACK * rows :], dpq_ref[...]), mine_ref, theirs_ref, 1, slice(None)
    )
    put_split(core_ref, nt(normed_ref[...], dkb_ref[...]), mine_ref, theirs_ref, 2, slice(None))
    for at in range(BACK):
        lanes = slice(at * rows, at * rows + rows)
        left = jnp.concatenate([wv_ref[...], wk_ref[...]], axis=1)
        right = jnp.concatenate([dvb_ref[:, lanes], dkb_ref[:, lanes]], axis=0)
        sum_ref[at] += nn(left, right)

    @pl.when(step == pl.num_programs(0) - 1)
    def _():
        for at in range(BACK):
            done = sum_ref[at].astype(BF16)
            if first:
                part_ref[at] = done
            else:
                (far_ref, near_ref)[at][...] = done


def attend_back(start, idx, core, size, w, g, kv, do, do_t, q_t, slopes, kv_slopes, normed, w_in, part):
    rows = do.shape[0]
    nblk = rows // BLK
    places = kv.shape[0]
    first = part is None
    heads = pl.BlockSpec((nblk, 4, BLK, 4 * BLK), lambda i, *_: (0, start + i, 0, 0))
    tall = (BACK + 1) * rows
    wide = pl.BlockSpec((3, size // 2, WIDE // size, 256), lambda i, *_: (0, 0, 0, i))
    cols = pl.BlockSpec((256, rows), lambda i, *_: (i, 0))
    in_specs = [
        heads,
        heads,
        pl.BlockSpec((places, 256, BLK), lambda i, *_: (0, start + i, 0)),
        pl.BlockSpec((places, 256, BLK), lambda i, *_: (0, 4 + start + i, 0)),
        pl.BlockSpec((rows, 256), lambda i, *_: (0, start + i)),
        pl.BlockSpec((256, rows), lambda i, *_: (start + i, 0)),
        pl.BlockSpec((256, rows), lambda i, *_: (start + i, 0)),
        pl.BlockSpec((rows, 256), lambda i, *_: (0, 4 + start + i)),
        pl.BlockSpec((256, tall), lambda i, *_: (start + i, 0)),
        pl.BlockSpec((256, tall), lambda i, *_: (4 + start + i, 0)),
        whole(normed.shape),
        pl.BlockSpec((WIDE, 256), lambda i, *_: (0, 4 + start + i)),
        pl.BlockSpec((WIDE, 256), lambda i, *_: (0, 12 + start + i)),
    ]
    args = [idx, core, w, g, kv, kv, do, do_t, q_t, slopes, kv_slopes, kv_slopes, normed, w_in, w_in]
    chunk = sds((3, size // 2, WIDE // size, 512), BF16)
    out_specs = [wide, wide, pl.BlockSpec((rows, 256), lambda i, *_: (0, i)), cols, cols]
    out_shape = [chunk, chunk, sds((rows, 512), BF16), sds((512, rows), BF16), sds((512, rows), BF16)]
    if first:
        out_specs.append(whole((BACK, WIDE, rows)))
        out_shape.append(sds((BACK, WIDE, rows), BF16))
    else:
        in_specs.append(whole(part.shape))
        args.append(part)
        out_specs += [whole((WIDE, rows))] * 2
        out_shape += [sds((WIDE, rows), BF16)] * 2
    return pl.pallas_call(
        lambda *refs: bwd_kernel(*refs, first=first),
        grid_spec=pltpu.PrefetchScalarGridSpec(
            num_scalar_prefetch=2,
            grid=(2,),
            in_specs=in_specs,
            out_specs=out_specs,
            scratch_shapes=[
                pltpu.VMEM((places, 256, BLK), F32),
                pltpu.VMEM((places, 256, BLK), F32),
                pltpu.VMEM((256, tall), BF16),
                pltpu.VMEM((256, tall), BF16),
                pltpu.VMEM((BACK, WIDE, rows), F32),
            ],
        ),
        out_shape=out_shape,
        compiler_params=params(60),
        name="attend_back_%d" % start,
        cost_estimate=cost(24),
    )(*args)


def dn_u_kernel(w_ref, dpu_ref, own_ref):
    own_ref[...] = nt(w_ref[...], dpu_ref[...])


def grad_normed_u(w_in, dpu):
    rows = dpu.shape[0]
    return pl.pallas_call(
        dn_u_kernel,
        grid=(2,),
        in_specs=[pl.BlockSpec((WIDE // 2, WIDE), lambda j: (j, 0)), whole(dpu.shape)],
        out_specs=pl.BlockSpec((WIDE // 2, rows), lambda j: (j, 0)),
        out_shape=sds((WIDE, rows), F32),
        compiler_params=params(60),
        name="grad_normed_u",
        cost_estimate=cost(4),
    )(w_in, dpu)


def dn_own_kernel(w_ref, u_ref, qa_ref, qb_ref, va_ref, vb_ref, ka_ref, kb_ref, own_ref):
    step = pl.program_id(0)
    half = WIDE // 2
    left, right = w_ref[:, :half], w_ref[:, half:]

    @pl.when(step == 0)
    def _():
        own_ref[...] = u_ref[...] + nn(left, va_ref[...]) + nn(right, vb_ref[...])

    @pl.when(step == 1)
    def _():
        own_ref[...] += nt(left, qa_ref[...]) + nt(right, qb_ref[...])

    @pl.when(step == 2)
    def _():
        own_ref[...] += nn(left, ka_ref[...]) + nn(right, kb_ref[...])


def grad_normed_own(w_in, from_u, *halves):
    return pl.pallas_call(
        dn_own_kernel,
        grid=(3,),
        in_specs=[pl.BlockSpec((WIDE, WIDE), lambda j: (0, j + 1)), whole(from_u.shape)]
        + [whole(a.shape) for a in halves],
        out_specs=whole(from_u.shape),
        out_shape=sds(from_u.shape, F32),
        compiler_params=params(60),
        name="grad_normed_own",
        cost_estimate=cost(8),
    )(w_in, from_u, *halves)


def last_kernel(own_ref, a_ref, b_ref, c_ref, x_ref, grad_ref, out_ref):
    dn_t = own_ref[...] + a_ref[...].astype(F32) + b_ref[...].astype(F32) + c_ref[...].astype(F32)
    dn = dn_t.T
    cent, rstd = norm_parts(x_ref[...].astype(F32))
    z = cent * rstd
    dx = rstd * (
        dn - jnp.mean(dn, axis=-1, keepdims=True) - z * jnp.mean(dn * z, axis=-1, keepdims=True)
    )
    out_ref[...] = (grad_ref[...].astype(F32) + dx).astype(BF16)


def last(own, one, two, three, x, grad_out):
    rows = x.shape[0]
    colblk = pl.BlockSpec((WIDE, BLK), lambda b: (0, b))
    rowblk = pl.BlockSpec((BLK, WIDE), lambda b: (b, 0))
    return pl.pallas_call(
        last_kernel,
        grid=(rows // BLK,),
        in_specs=[colblk, colblk, colblk, colblk, rowblk, rowblk],
        out_specs=rowblk,
        out_shape=sds((rows, WIDE), BF16),
        compiler_params=params(60),
        name="grad_x",
        cost_estimate=cost(6),
    )(own, one, two, three, x, grad_out)


def send(array, pairs):
    return lax.ppermute(array, "seq", pairs)


class Halving:
    def __init__(self, mine, theirs, size, bits):
        self.size, self.bits, self.at = size, bits, 0
        self.left = list(range(1, size.bit_length() - 1))
        self.keep, self.got = mine, self.swap(theirs, 0)

    def swap(self, array, bit):
        return send(array, [(i, i ^ (1 << bit)) for i in range(self.size)])

    def step(self, *after):
        bit = self.bits[self.at]
        inner = 1 << self.left.index(bit)
        self.at += 1
        groups, count, height, cols = self.keep.shape
        shape = (groups, count // (2 * inner), 2, inner * height, cols)
        keep, got = self.keep.reshape(shape), self.got.reshape(shape)
        if after:
            got = tie(got, *after)
        side = (lax.axis_index("seq") >> bit) & 1

        def added(which):
            parts = [lax.dynamic_index_in_dim(a, which, 2, keepdims=False) for a in (keep, got)]
            total = parts[0].astype(F32) + parts[1].astype(F32)
            return total.astype(BF16).reshape(groups, count // 2, height, cols)

        moving = added(1 - side)
        self.keep, self.got = added(side), self.swap(moving, bit)
        self.left.remove(bit)
        return moving

    def parts(self):
        while self.at < len(self.bits):
            self.step()
        return self.keep, self.got


def finish_kernel(ek_ref, eg_ref, ak_ref, ag_ref, bk_ref, bg_ref, win_ref, wout_ref):
    def total(keep_ref, got_ref, group):
        return keep_ref[group, 0].astype(F32) + got_ref[group, 0].astype(F32)

    wout_ref[...] = total(ek_ref, eg_ref, 0)
    win_ref[:, :WIDE] = total(ek_ref, eg_ref, 1)
    for group in range(3):
        at = (group + 1) * WIDE
        win_ref[:, at : at + 512] = total(ak_ref, ag_ref, group)
        win_ref[:, at + 512 : at + WIDE] = total(bk_ref, bg_ref, group)


def finish(*sums):
    args = [a for pair in sums for a in pair]
    height = args[0].shape[2]
    return pl.pallas_call(
        finish_kernel,
        in_specs=[pl.BlockSpec(memory_space=pltpu.VMEM)] * 6,
        out_specs=[pl.BlockSpec(memory_space=pltpu.VMEM)] * 2,
        out_shape=[sds((height, 4 * WIDE), F32), sds((height, WIDE), F32)],
        compiler_params=pltpu.CompilerParams(vmem_limit_bytes=60 * MIB),
        name="finish_sums",
        cost_estimate=cost(2),
    )(*args)


def on_device(events_in, w_in, w_out, kv_list, counts, grad_out):
    size = lax.axis_size("seq")
    nblk = kv_list.shape[0]
    place = lax.axis_index("seq")
    core = (place % 2).astype(jnp.int32)[None]
    pairs = range(0, size, 2)
    live = jnp.arange(BLK, dtype=jnp.int32)[None, :] < counts[:, None]
    shown = jnp.where(live.reshape(-1)[:, None], events_in, jnp.zeros((), BF16))
    x_near = send(shown, [(i, i + 1) for i in range(size - 1)])
    x_even = send(shown, [(i, i + 2) for i in range(0, size - 2, 2)])
    x_odd = send(x_near, [(i, i + 1) for i in pairs])
    local = jnp.arange(nblk, dtype=jnp.int32)
    index = jnp.concatenate(
        [kv_list + (BACK - place) * nblk, (local + BACK * nblk)[:, None]], axis=1
    )
    index = jnp.clip(index, 0, (BACK + 1) * nblk - 1)

    kv, kv_slopes, normed, w_kv_t, acts, slopes, dy = project_own(
        counts, events_in, grad_out, w_in, w_out
    )
    x_odd = send(tie(x_near, dy), [(i, i + 1) for i in pairs])
    kv, kv_slopes, normed = project_window(
        [x_even, x_odd, x_near], w_kv_t, (kv, kv_slopes, normed)
    )
    w, g, q_t, y, dpu, do, do_t, mine, theirs = attend(
        index, core, size, acts, slopes, kv, dy, grad_out, normed
    )
    ups = list(range(1, size.bit_length() - 1))
    sum_early = Halving(mine, theirs, size, ups[1:] + ups[:1])
    from_u = grad_normed_u(w_in, tie(dpu, mine))
    sent = sum_early.step(from_u)

    def backward(start, token, part):
        return attend_back(
            start, token, core, size, w, g, kv, do, do_t, q_t, slopes, kv_slopes, normed, w_in, part
        )

    mine, theirs, qa, va, ka, part = backward(0, tie(index, sent), None)
    sent = sum_early.step(qa)
    first = Halving(mine, tie(theirs, sent), size, ups)
    events_out = events(events_in, tie(y, first.keep, sent), w_out)
    sent = first.step(events_out)
    mine, theirs, qb, vb, kb, far, near = backward(2, tie(index, sent), part)
    to_even = [(i + 1, i) for i in pairs]
    far, near, mine, theirs, sum_early.got, first.got = lax.optimization_barrier(
        (far, near, mine, theirs, sum_early.got, first.got)
    )
    far_odd = send(far, to_even)
    second = Halving(mine, theirs, size, ups)
    sent = first.step(sum_early.step(second.keep))
    sent = second.step(sent)
    joined = (tie(near, sent).astype(F32) + far_odd.astype(F32)).astype(BF16)
    back = send(joined, [(i, i - 1) for i in range(2, size, 2)])
    far_even = send(tie(far, sent), [(i + 2, i) for i in range(0, size - 2, 2)])
    near_odd = send(tie(near, sent), to_even)
    own = grad_normed_own(w_in, tie(from_u, joined), qa, qb, va, vb, ka, kb)
    own, first.got, sum_early.got = lax.optimization_barrier((own, first.got, sum_early.got))
    sent = first.step()
    second.got = tie(second.got, sent)
    grad_x = last(own, near_odd, far_even, back, events_in, grad_out)
    grad_w_in, grad_w_out = finish(sum_early.parts(), first.parts(), second.parts())
    return (events_out, grad_x, grad_w_in, grad_w_out)


def solution(mesh):
    rows = P(("grp", "seq"), None)
    return jax.shard_map(
        on_device,
        mesh=mesh,
        in_specs=(rows, P(), P(), rows, P(("grp", "seq")), rows),
        out_specs=(rows, rows, rows, rows),
        check_vma=False,
    )
```

```python
import jax
import jax.numpy as jnp
from jax import lax
from jax.experimental import pallas as pl
from jax.experimental.pallas import tpu as pltpu
from jax.sharding import PartitionSpec as P

HEADS = 16
HD = 64
BLK = 128
WIDE = 1024
BACK = 2
EPS = 1e-05
F32 = jnp.float32
BF16 = jnp.bfloat16
MIB = 1024 * 1024


def nn(left, right):
    return lax.dot_general(left, right, (((1,), (0,)), ((), ())), preferred_element_type=F32)


def nt(left, right):
    return lax.dot_general(left, right, (((1,), (1,)), ((), ())), preferred_element_type=F32)


def params(mib):
    return pltpu.CompilerParams(dimension_semantics=("arbitrary",), vmem_limit_bytes=mib * MIB)


def cost(micros):
    return pl.CostEstimate(flops=int(micros * 1e9), transcendentals=0, bytes_accessed=1 << 20)


def tie(value, *others):
    return lax.optimization_barrier((value, *others))[0]


def whole(shape):
    zeros = (0,) * len(shape)
    return pl.BlockSpec(shape, lambda *_: zeros, pipeline_mode=pl.Buffered(1))


def sds(shape, dtype):
    return jax.ShapeDtypeStruct(shape, dtype)


def norm_parts(rows):
    mean = jnp.mean(rows, axis=-1, keepdims=True)
    cent = rows - mean
    var = jnp.mean(cent * cent, axis=-1, keepdims=True)
    return cent, lax.rsqrt(var + EPS)


def normed_of(x):
    cent, rstd = norm_parts(x.astype(F32))
    return (cent * rstd).astype(BF16)


def halved(bf):
    return bf * jnp.asarray(0.5, BF16)


def silu_both(half):
    t = jnp.tanh(half)
    p = 1.0 + t
    act = half * p
    return act, p + act * (1.0 - t)


def kv_tile(w_t, normed_t, kv_ref, slope_ref, counts_ref):
    act, slope = silu_both(0.5 * nn(w_t, normed_t))
    slope_ref[...] = slope.astype(BF16)
    lane = lax.broadcasted_iota(jnp.int32, (1, BLK), 1)
    for place in range(act.shape[1] // BLK):
        part = act[:, place * BLK : (place + 1) * BLK]
        if counts_ref is not None:
            part = jnp.where(lane < counts_ref[place], part, 0.0)
        kv_ref[place] = part.astype(BF16)


def own_kernel(
    counts_ref, x_ref, grad_ref, w_ref, wo_ref,
    kv_ref, kvslope_ref, normed_t_ref, w_t_ref, acts_ref, slope_ref, dy_ref, normed_ref,
):
    step = pl.program_id(0)

    @pl.when(step == 0)
    def _():
        normed = normed_of(x_ref[...])
        normed_ref[...] = halved(normed)
        normed_t_ref[...] = normed.T

    @pl.when(step < 4)
    def _():
        w_t_ref[...] = w_ref[...].T
        kv_tile(w_t_ref[...], normed_t_ref[...], kv_ref, kvslope_ref, counts_ref)

    @pl.when(jnp.logical_and(step >= 4, step < 8))
    def _():
        scale = jnp.where(step >= 6, HD ** (-0.5) * 0.5, 1.0).astype(F32)
        act, slope = silu_both(nn(normed_ref[...], w_ref[...]))
        acts_ref[...] = (act * scale).astype(BF16)
        slope_ref[...] = slope.astype(BF16)

    @pl.when(step >= 8)
    def _():
        dy_ref[...] = nt(grad_ref[...], wo_ref[...])


def project_own(counts, x, grad_out, w_in, w_out):
    rows = x.shape[0]
    nblk = rows // BLK

    def w_at(j, _):
        early_tile = j + 2 + 2 * (j // 2)
        later = jnp.minimum(j, 7) - 4
        return (0, jnp.where(j < 4, early_tile, later + 2 * (later // 2)))

    def up_to(last, start=0):
        return lambda j: jnp.clip(j - start, 0, last)

    kv_at, uq_at, dy_at = up_to(3), up_to(3, 4), up_to(1, 8)
    uq = pl.BlockSpec((rows, 512), lambda j, _: (0, uq_at(j)))
    return pl.pallas_call(
        own_kernel,
        grid_spec=pltpu.PrefetchScalarGridSpec(
            num_scalar_prefetch=1,
            grid=(10,),
            in_specs=[
                whole(x.shape),
                whole(grad_out.shape),
                pl.BlockSpec((WIDE, 512), w_at),
                pl.BlockSpec((512, WIDE), lambda j, _: (dy_at(j), 0)),
            ],
            out_specs=[
                pl.BlockSpec((nblk, 512, BLK), lambda j, _: (BACK, kv_at(j), 0)),
                pl.BlockSpec((512, rows), lambda j, _: (kv_at(j), BACK)),
                pl.BlockSpec((WIDE, rows), lambda j, _: (0, BACK)),
                pl.BlockSpec((512, WIDE), lambda j, _: (kv_at(j), 0)),
                uq,
                uq,
                pl.BlockSpec((rows, 512), lambda j, _: (0, dy_at(j))),
            ],
            scratch_shapes=[pltpu.VMEM((rows, WIDE), BF16)],
        ),
        out_shape=[
            sds(((BACK + 1) * nblk, 2 * WIDE, BLK), BF16),
            sds((2 * WIDE, (BACK + 1) * rows), BF16),
            sds((WIDE, (BACK + 1) * rows), BF16),
            sds((2 * WIDE, WIDE), BF16),
            sds((rows, 2 * WIDE), BF16),
            sds((rows, 2 * WIDE), BF16),
            sds((rows, WIDE), F32),
        ],
        compiler_params=params(60),
        name="project_own",
        cost_estimate=cost(13),
    )(counts, x, grad_out, w_in, w_out)


def window_kernel(
    x_even_ref, x_odd_ref, x_near_ref, w_ref, _kv, _slope, _normed,
    kv_ref, slope_ref, normed_t_ref,
):
    rows = x_near_ref.shape[0]

    @pl.when(pl.program_id(0) == 0)
    def _():
        far = x_odd_ref[...].astype(F32) + x_even_ref[...].astype(F32)
        normed_t_ref[:, :rows] = normed_of(far).T
        normed_t_ref[:, rows:] = normed_of(x_near_ref[...]).T

    kv_tile(w_ref[...], normed_t_ref[...], kv_ref, slope_ref, None)


def project_window(xs, w_kv_t, arrays):
    rows = xs[0].shape[0]
    nblk = rows // BLK
    return pl.pallas_call(
        window_kernel,
        grid=(4,),
        in_specs=[whole(x.shape) for x in xs]
        + [pl.BlockSpec((512, WIDE), lambda j: (j, 0))]
        + [pl.BlockSpec(memory_space=pl.ANY)] * 3,
        out_specs=[
            pl.BlockSpec((BACK * nblk, 512, BLK), lambda j: (0, j, 0)),
            pl.BlockSpec((512, BACK * rows), lambda j: (j, 0)),
            pl.BlockSpec((WIDE, BACK * rows), lambda j: (0, 0)),
        ],
        out_shape=[sds(a.shape, BF16) for a in arrays],
        input_output_aliases={len(xs) + 1 + i: i for i in range(3)},
        compiler_params=params(60),
        name="project_window",
        cost_estimate=cost(10),
    )(*xs, w_kv_t, *arrays)


def duo_of(ref, idx_ref, blk, duo, rows):
    return jnp.concatenate([ref[idx_ref[blk, 2 * duo + i], rows, :] for i in range(2)], axis=1)


def diagonal(quad_rows):
    left = lax.broadcasted_iota(jnp.int32, (BLK, BLK), 1) < HD
    pairs = []
    for pair in range(2):
        lanes = slice(pair * BLK, pair * BLK + BLK)
        one = quad_rows[2 * pair * BLK : (2 * pair + 1) * BLK, lanes]
        two = quad_rows[(2 * pair + 1) * BLK : (2 * pair + 2) * BLK, lanes]
        pairs.append(jnp.where(left, one, two))
    return jnp.concatenate(pairs, axis=1)


def put_split(core_ref, val, mine_ref, theirs_ref, group, cols):
    _, pieces, height, _ = mine_ref.shape
    split = val.astype(BF16).reshape(pieces, 2, height, val.shape[1])
    even, odd = split[:, 0], split[:, 1]
    first = core_ref[0] == 0
    mine_ref[group, :, :, cols] = jnp.where(first, even, odd)
    theirs_ref[group, :, :, cols] = jnp.where(first, odd, even)


def fwd_kernel(
    idx_ref, core_ref, q_ref, kv_ref, u_ref, uslope_ref, dy_ref, grad_ref, normed_ref,
    w_ref, g_ref, qt_ref, y_ref, dpu_ref, do_ref, dot_ref, mine_ref, theirs_ref,
    attn_ref, yt_ref, dpu_all_ref,
):
    blk = pl.program_id(0)
    row = lax.broadcasted_iota(jnp.int32, (BLK, BLK), 0)
    col = lax.broadcasted_iota(jnp.int32, (BLK, BLK), 1)
    keep = jnp.concatenate([jnp.full((BLK, BLK), True), col <= row], axis=1)
    qt_ref[...] = q_ref[...].T
    for quad in range(HEADS // 4):
        at = quad * 256
        total = None
        for duo in range(2):
            span = slice(duo * 256, duo * 256 + 256)
            ws = []
            for head in range(4 * quad, 4 * quad + 4):
                cols = slice(head * HD, head * HD + HD)
                keys = duo_of(kv_ref, idx_ref, blk, duo, slice(WIDE + head * HD, WIDE + head * HD + HD))
                w, g = silu_both(nn(q_ref[:, cols], keys))
                if duo == 1:
                    w = jnp.where(keep, w, 0.0)
                    g = jnp.where(keep, g, 0.0)
                w = w.astype(BF16)
                ws.append(w)
                w_ref[0, head, :, span] = w
                g_ref[0, head, :, span] = g.astype(BF16)
            vals = duo_of(kv_ref, idx_ref, blk, duo, slice(at, at + 256))
            part = nt(jnp.concatenate(ws, axis=0), vals)
            total = part if total is None else total + part
        attn_ref[:, at : at + 256] = diagonal(total) * (1.0 / BLK)
    cent, rstd = norm_parts(attn_ref[...])
    z = cent * rstd
    u = u_ref[...].astype(F32)
    dy = dy_ref[...]
    y = (z * u).astype(BF16)
    y_ref[...] = y
    here = pl.ds(pl.multiple_of(blk * BLK, BLK), BLK)
    yt_ref[:, here] = y.T
    dpu = (dy * (0.5 * z) * uslope_ref[...].astype(F32)).astype(BF16)
    dpu_ref[...] = dpu
    dpu_all_ref[here, :] = dpu
    dz = dy * u
    shift = jnp.mean(dz, axis=-1, keepdims=True)
    dattn = rstd * (dz - shift - z * jnp.mean(dz * z, axis=-1, keepdims=True))
    dattn = dattn.astype(BF16)
    do_ref[...] = dattn
    dot_ref[...] = dattn.T

    @pl.when(blk == pl.num_programs(0) - 1)
    def _():
        for group, (left_ref, right_ref) in enumerate(
            ((yt_ref, grad_ref), (normed_ref, dpu_all_ref))
        ):
            for tile in range(2):
                cols = slice(tile * 512, tile * 512 + 512)
                val = nn(left_ref[...], right_ref[:, cols])
                put_split(core_ref, val, mine_ref, theirs_ref, group, cols)


def attend(idx, core, size, acts, slopes, kv, dy, grad_out, normed):
    rows = dy.shape[0]
    nblk = rows // BLK
    scores = pl.BlockSpec((1, HEADS, BLK, 4 * BLK), lambda b, *_: (b, 0, 0, 0))
    rowblk = pl.BlockSpec((BLK, WIDE), lambda b, *_: (b, 0))
    colblk = pl.BlockSpec((WIDE, BLK), lambda b, *_: (0, b))
    chunk = (2, size // 2, WIDE // size, WIDE)
    return pl.pallas_call(
        fwd_kernel,
        grid_spec=pltpu.PrefetchScalarGridSpec(
            num_scalar_prefetch=2,
            grid=(nblk,),
            in_specs=[
                pl.BlockSpec((BLK, WIDE), lambda b, *_: (b, 1)),
                whole(kv.shape),
                rowblk,
                rowblk,
                rowblk,
                whole(grad_out.shape),
                pl.BlockSpec((WIDE, rows), lambda *_: (0, BACK), pipeline_mode=pl.Buffered(1)),
            ],
            out_specs=[
                scores, scores, colblk, rowblk, rowblk, rowblk, colblk, whole(chunk), whole(chunk)
            ],
            scratch_shapes=[
                pltpu.VMEM((BLK, WIDE), F32),
                pltpu.VMEM((WIDE, rows), BF16),
                pltpu.VMEM((rows, WIDE), BF16),
            ],
        ),
        out_shape=[
            sds((nblk, HEADS, BLK, 4 * BLK), BF16),
            sds((nblk, HEADS, BLK, 4 * BLK), BF16),
            sds((WIDE, rows), BF16),
            sds((rows, WIDE), BF16),
            sds((rows, WIDE), BF16),
            sds((rows, WIDE), BF16),
            sds((WIDE, rows), BF16),
            sds(chunk, BF16),
            sds(chunk, BF16),
        ],
        compiler_params=params(60),
        name="attend",
        cost_estimate=cost(18),
    )(idx, core, acts, kv, acts, slopes, dy, grad_out, normed)


def events_kernel(x_ref, y_ref, wo_ref, ev_ref):
    ev_ref[...] = (x_ref[...].astype(F32) + nn(y_ref[...], wo_ref[...])).astype(BF16)


def events(x, y, w_out):
    rows = x.shape[0]
    tile = pl.BlockSpec((rows, 512), lambda j: (0, j))
    return pl.pallas_call(
        events_kernel,
        grid=(2,),
        in_specs=[tile, whole(y.shape), pl.BlockSpec((WIDE, 512), lambda j: (0, j))],
        out_specs=tile,
        out_shape=sds((rows, WIDE), BF16),
        compiler_params=params(60),
        name="events_out",
        cost_estimate=cost(4),
    )(x, y, w_out)


def bwd_kernel(*refs, first):
    (idx_ref, core_ref, w_ref, g_ref, v_ref, k_ref, do_ref, dot_ref, qt_ref, qslope_ref) = refs[:10]
    (vslope_ref, kslope_ref, normed_ref, wv_ref, wk_ref) = refs[10:15]
    rest = refs[15:]
    if first:
        part_ref = rest[5]
        rest = rest[:5] + rest[6:]
    else:
        part_ref, far_ref, near_ref = rest[0], rest[6], rest[7]
        rest = rest[1:6] + rest[8:]
    (mine_ref, theirs_ref, dpq_ref, dvt_ref, dkt_ref) = rest[:5]
    (dva_ref, dka_ref, dvb_ref, dkb_ref, sum_ref) = rest[5:]
    step = pl.program_id(0)
    rows = dpq_ref.shape[0]
    dva_ref[...] = jnp.zeros_like(dva_ref)
    dka_ref[...] = jnp.zeros_like(dka_ref)

    @pl.when(step == 0)
    def _():
        sum_ref[...] = jnp.zeros_like(sum_ref) if first else part_ref[...].astype(F32)

    def one_block(blk, carry):
        at = pl.multiple_of(blk * BLK, BLK)
        block = pl.ds(at, BLK)
        total = None
        for duo in range(2):
            span = slice(duo * 256, duo * 256 + 256)
            dss = []
            for head in range(4):
                cols = slice(head * HD, head * HD + HD)
                dw = nn(do_ref[block, cols], duo_of(v_ref, idx_ref, blk, duo, cols))
                ds = (dw * g_ref[blk, head, :, span].astype(F32)).astype(BF16)
                dss.append(ds)
                dk = nn(qt_ref[cols, block], ds)
                dv = nn(dot_ref[cols, block], w_ref[blk, head, :, span])
                for side in range(2):
                    place = idx_ref[blk, 2 * duo + side]
                    lanes = slice(side * BLK, side * BLK + BLK)
                    dva_ref[place, cols, :] += dv[:, lanes]
                    dka_ref[place, cols, :] += dk[:, lanes]
            part = nt(jnp.concatenate(dss, axis=0), duo_of(k_ref, idx_ref, blk, duo, slice(None)))
            total = part if total is None else total + part
        dq = diagonal(total) * (HD ** (-0.5) / (4 * BLK))
        dpq_ref[block, :] = (dq * qslope_ref[block, :].astype(F32)).astype(BF16)
        return carry

    lax.fori_loop(0, rows // BLK, one_block, 0)
    for place in range(dva_ref.shape[0]):
        lanes = slice(place * BLK, place * BLK + BLK)
        for acc_ref, slope_ref, out_ref in (
            (dva_ref, vslope_ref, dvb_ref),
            (dka_ref, kslope_ref, dkb_ref),
        ):
            out_ref[:, lanes] = (
                acc_ref[place] * (0.5 / BLK) * slope_ref[:, lanes].astype(F32)
            ).astype(BF16)
    dvt_ref[...] = dvb_ref[:, BACK * rows :]
    dkt_ref[...] = dkb_ref[:, BACK * rows :]
    put_split(core_ref, nt(normed_ref[...], dvb_ref[...]), mine_ref, theirs_ref, 0, slice(None))
    put_split(
        core_ref, nn(normed_ref[:, BACK * rows :], dpq_ref[...]), mine_ref, theirs_ref, 1, slice(None)
    )
    put_split(core_ref, nt(normed_ref[...], dkb_ref[...]), mine_ref, theirs_ref, 2, slice(None))
    for at in range(BACK):
        lanes = slice(at * rows, at * rows + rows)
        left = jnp.concatenate([wv_ref[...], wk_ref[...]], axis=1)
        right = jnp.concatenate([dvb_ref[:, lanes], dkb_ref[:, lanes]], axis=0)
        sum_ref[at] += nn(left, right)

    @pl.when(step == pl.num_programs(0) - 1)
    def _():
        for at in range(BACK):
            done = sum_ref[at].astype(BF16)
            if first:
                part_ref[at] = done
            else:
                (far_ref, near_ref)[at][...] = done


def attend_back(start, idx, core, size, w, g, kv, do, do_t, q_t, slopes, kv_slopes, normed, w_in, part):
    rows = do.shape[0]
    nblk = rows // BLK
    places = kv.shape[0]
    first = part is None
    heads = pl.BlockSpec((nblk, 4, BLK, 4 * BLK), lambda i, *_: (0, start + i, 0, 0))
    tall = (BACK + 1) * rows
    wide = pl.BlockSpec((3, size // 2, WIDE // size, 256), lambda i, *_: (0, 0, 0, i))
    cols = pl.BlockSpec((256, rows), lambda i, *_: (i, 0))
    in_specs = [
        heads,
        heads,
        pl.BlockSpec((places, 256, BLK), lambda i, *_: (0, start + i, 0)),
        pl.BlockSpec((places, 256, BLK), lambda i, *_: (0, 4 + start + i, 0)),
        pl.BlockSpec((rows, 256), lambda i, *_: (0, start + i)),
        pl.BlockSpec((256, rows), lambda i, *_: (start + i, 0)),
        pl.BlockSpec((256, rows), lambda i, *_: (start + i, 0)),
        pl.BlockSpec((rows, 256), lambda i, *_: (0, 4 + start + i)),
        pl.BlockSpec((256, tall), lambda i, *_: (start + i, 0)),
        pl.BlockSpec((256, tall), lambda i, *_: (4 + start + i, 0)),
        whole(normed.shape),
        pl.BlockSpec((WIDE, 256), lambda i, *_: (0, 4 + start + i)),
        pl.BlockSpec((WIDE, 256), lambda i, *_: (0, 12 + start + i)),
    ]
    args = [idx, core, w, g, kv, kv, do, do_t, q_t, slopes, kv_slopes, kv_slopes, normed, w_in, w_in]
    chunk = sds((3, size // 2, WIDE // size, 512), BF16)
    out_specs = [wide, wide, pl.BlockSpec((rows, 256), lambda i, *_: (0, i)), cols, cols]
    out_shape = [chunk, chunk, sds((rows, 512), BF16), sds((512, rows), BF16), sds((512, rows), BF16)]
    if first:
        out_specs.append(whole((BACK, WIDE, rows)))
        out_shape.append(sds((BACK, WIDE, rows), BF16))
    else:
        in_specs.append(whole(part.shape))
        args.append(part)
        out_specs += [whole((WIDE, rows))] * 2
        out_shape += [sds((WIDE, rows), BF16)] * 2
    return pl.pallas_call(
        lambda *refs: bwd_kernel(*refs, first=first),
        grid_spec=pltpu.PrefetchScalarGridSpec(
            num_scalar_prefetch=2,
            grid=(2,),
            in_specs=in_specs,
            out_specs=out_specs,
            scratch_shapes=[
                pltpu.VMEM((places, 256, BLK), F32),
                pltpu.VMEM((places, 256, BLK), F32),
                pltpu.VMEM((256, tall), BF16),
                pltpu.VMEM((256, tall), BF16),
                pltpu.VMEM((BACK, WIDE, rows), F32),
            ],
        ),
        out_shape=out_shape,
        compiler_params=params(60),
        name="attend_back_%d" % start,
        cost_estimate=cost(24),
    )(*args)


def dn_u_kernel(w_ref, dpu_ref, own_ref):
    own_ref[...] = nt(w_ref[...], dpu_ref[...])


def grad_normed_u(w_in, dpu):
    rows = dpu.shape[0]
    return pl.pallas_call(
        dn_u_kernel,
        grid=(2,),
        in_specs=[pl.BlockSpec((WIDE // 2, WIDE), lambda j: (j, 0)), whole(dpu.shape)],
        out_specs=pl.BlockSpec((WIDE // 2, rows), lambda j: (j, 0)),
        out_shape=sds((WIDE, rows), F32),
        compiler_params=params(60),
        name="grad_normed_u",
        cost_estimate=cost(4),
    )(w_in, dpu)


def dn_own_kernel(w_ref, u_ref, qa_ref, qb_ref, va_ref, vb_ref, ka_ref, kb_ref, own_ref):
    step = pl.program_id(0)
    half = WIDE // 2
    left, right = w_ref[:, :half], w_ref[:, half:]

    @pl.when(step == 0)
    def _():
        own_ref[...] = u_ref[...] + nn(left, va_ref[...]) + nn(right, vb_ref[...])

    @pl.when(step == 1)
    def _():
        own_ref[...] += nt(left, qa_ref[...]) + nt(right, qb_ref[...])

    @pl.when(step == 2)
    def _():
        own_ref[...] += nn(left, ka_ref[...]) + nn(right, kb_ref[...])


def grad_normed_own(w_in, from_u, *halves):
    return pl.pallas_call(
        dn_own_kernel,
        grid=(3,),
        in_specs=[pl.BlockSpec((WIDE, WIDE), lambda j: (0, j + 1)), whole(from_u.shape)]
        + [whole(a.shape) for a in halves],
        out_specs=whole(from_u.shape),
        out_shape=sds(from_u.shape, F32),
        compiler_params=params(60),
        name="grad_normed_own",
        cost_estimate=cost(8),
    )(w_in, from_u, *halves)


def last_kernel(own_ref, a_ref, b_ref, c_ref, x_ref, grad_ref, out_ref):
    dn_t = own_ref[...] + a_ref[...].astype(F32) + b_ref[...].astype(F32) + c_ref[...].astype(F32)
    dn = dn_t.T
    cent, rstd = norm_parts(x_ref[...].astype(F32))
    z = cent * rstd
    dx = rstd * (
        dn - jnp.mean(dn, axis=-1, keepdims=True) - z * jnp.mean(dn * z, axis=-1, keepdims=True)
    )
    out_ref[...] = (grad_ref[...].astype(F32) + dx).astype(BF16)


def last(own, one, two, three, x, grad_out):
    rows = x.shape[0]
    colblk = pl.BlockSpec((WIDE, BLK), lambda b: (0, b))
    rowblk = pl.BlockSpec((BLK, WIDE), lambda b: (b, 0))
    return pl.pallas_call(
        last_kernel,
        grid=(rows // BLK,),
        in_specs=[colblk, colblk, colblk, colblk, rowblk, rowblk],
        out_specs=rowblk,
        out_shape=sds((rows, WIDE), BF16),
        compiler_params=params(60),
        name="grad_x",
        cost_estimate=cost(6),
    )(own, one, two, three, x, grad_out)


def send(array, pairs):
    return lax.ppermute(array, "seq", pairs)


class Halving:
    def __init__(self, mine, theirs, size, bits):
        self.size, self.bits, self.at = size, bits, 0
        self.left = list(range(1, size.bit_length() - 1))
        self.keep, self.got = mine, self.swap(theirs, 0)

    def swap(self, array, bit):
        return send(array, [(i, i ^ (1 << bit)) for i in range(self.size)])

    def step(self, *after):
        bit = self.bits[self.at]
        inner = 1 << self.left.index(bit)
        self.at += 1
        groups, count, height, cols = self.keep.shape
        shape = (groups, count // (2 * inner), 2, inner * height, cols)
        keep, got = self.keep.reshape(shape), self.got.reshape(shape)
        if after:
            got = tie(got, *after)
        side = (lax.axis_index("seq") >> bit) & 1

        def added(which):
            parts = [lax.dynamic_index_in_dim(a, which, 2, keepdims=False) for a in (keep, got)]
            total = parts[0].astype(F32) + parts[1].astype(F32)
            return total.astype(BF16).reshape(groups, count // 2, height, cols)

        moving = added(1 - side)
        self.keep, self.got = added(side), self.swap(moving, bit)
        self.left.remove(bit)
        return moving

    def parts(self):
        while self.at < len(self.bits):
            self.step()
        return self.keep, self.got


def finish_kernel(ek_ref, eg_ref, ak_ref, ag_ref, bk_ref, bg_ref, win_ref, wout_ref):
    def total(keep_ref, got_ref, group):
        return keep_ref[group, 0].astype(F32) + got_ref[group, 0].astype(F32)

    wout_ref[...] = total(ek_ref, eg_ref, 0)
    win_ref[:, :WIDE] = total(ek_ref, eg_ref, 1)
    for group in range(3):
        at = (group + 1) * WIDE
        win_ref[:, at : at + 512] = total(ak_ref, ag_ref, group)
        win_ref[:, at + 512 : at + WIDE] = total(bk_ref, bg_ref, group)


def finish(*sums):
    args = [a for pair in sums for a in pair]
    height = args[0].shape[2]
    return pl.pallas_call(
        finish_kernel,
        in_specs=[pl.BlockSpec(memory_space=pltpu.VMEM)] * 6,
        out_specs=[pl.BlockSpec(memory_space=pltpu.VMEM)] * 2,
        out_shape=[sds((height, 4 * WIDE), F32), sds((height, WIDE), F32)],
        compiler_params=pltpu.CompilerParams(vmem_limit_bytes=60 * MIB),
        name="finish_sums",
        cost_estimate=cost(2),
    )(*args)


def on_device(events_in, w_in, w_out, kv_list, counts, grad_out):
    size = lax.axis_size("seq")
    nblk = kv_list.shape[0]
    place = lax.axis_index("seq")
    core = (place % 2).astype(jnp.int32)[None]
    pairs = range(0, size, 2)
    live = jnp.arange(BLK, dtype=jnp.int32)[None, :] < counts[:, None]
    shown = jnp.where(live.reshape(-1)[:, None], events_in, jnp.zeros((), BF16))
    x_near = send(shown, [(i, i + 1) for i in range(size - 1)])
    x_even = send(shown, [(i, i + 2) for i in range(0, size - 2, 2)])
    x_odd = send(x_near, [(i, i + 1) for i in pairs])
    local = jnp.arange(nblk, dtype=jnp.int32)
    index = jnp.concatenate(
        [kv_list + (BACK - place) * nblk, (local + BACK * nblk)[:, None]], axis=1
    )
    index = jnp.clip(index, 0, (BACK + 1) * nblk - 1)

    kv, kv_slopes, normed, w_kv_t, acts, slopes, dy = project_own(
        counts, events_in, grad_out, w_in, w_out
    )
    x_odd = send(tie(x_near, dy), [(i, i + 1) for i in pairs])
    kv, kv_slopes, normed = project_window(
        [x_even, x_odd, x_near], w_kv_t, (kv, kv_slopes, normed)
    )
    w, g, q_t, y, dpu, do, do_t, mine, theirs = attend(
        index, core, size, acts, slopes, kv, dy, grad_out, normed
    )
    ups = list(range(1, size.bit_length() - 1))
    sum_early = Halving(mine, theirs, size, ups[1:] + ups[:1])
    from_u = grad_normed_u(w_in, tie(dpu, mine))
    sent = sum_early.step(from_u)

    def backward(start, token, part):
        return attend_back(
            start, token, core, size, w, g, kv, do, do_t, q_t, slopes, kv_slopes, normed, w_in, part
        )

    mine, theirs, qa, va, ka, part = backward(0, tie(index, sent), None)
    sent = sum_early.step(qa)
    first = Halving(mine, tie(theirs, sent), size, ups)
    events_out = events(events_in, tie(y, first.keep, sent), w_out)
    sent = first.step(events_out)
    mine, theirs, qb, vb, kb, far, near = backward(2, tie(index, sent), part)
    to_even = [(i + 1, i) for i in pairs]
    far, near, mine, theirs, sum_early.got, first.got = lax.optimization_barrier(
        (far, near, mine, theirs, sum_early.got, first.got)
    )
    far_odd = send(far, to_even)
    second = Halving(mine, theirs, size, ups)
    sent = first.step(sum_early.step(second.keep))
    sent = second.step(sent)
    joined = (near.astype(F32) + far_odd.astype(F32)).astype(BF16)
    own = grad_normed_own(w_in, tie(from_u, sent), qa, qb, va, vb, ka, kb)
    joined, far, near, first.got, sum_early.got = lax.optimization_barrier(
        (joined, far, near, first.got, sum_early.got, own)
    )[:5]
    back = send(joined, [(i, i - 1) for i in range(2, size, 2)])
    far_even = send(far, [(i + 2, i) for i in range(0, size - 2, 2)])
    near_odd = send(near, to_even)
    first.step()
    second.got = tie(second.got, first.got)
    grad_x = last(own, near_odd, far_even, back, events_in, grad_out)
    grad_w_in, grad_w_out = finish(sum_early.parts(), first.parts(), second.parts())
    return (events_out, grad_x, grad_w_in, grad_w_out)


def solution(mesh):
    rows = P(("grp", "seq"), None)
    return jax.shard_map(
        on_device,
        mesh=mesh,
        in_specs=(rows, P(), P(), rows, P(("grp", "seq")), rows),
        out_specs=(rows, rows, rows, rows),
        check_vma=False,
    )
```

```python
import jax
import jax.numpy as jnp
from jax import lax
from jax.experimental import pallas as pl
from jax.experimental.pallas import tpu as pltpu
from jax.sharding import PartitionSpec as P

HEADS = 16
HD = 64
BLK = 128
WIDE = 1024
BACK = 2
EPS = 1e-05
F32 = jnp.float32
BF16 = jnp.bfloat16
MIB = 1024 * 1024


def nn(left, right):
    return lax.dot_general(left, right, (((1,), (0,)), ((), ())), preferred_element_type=F32)


def nt(left, right):
    return lax.dot_general(left, right, (((1,), (1,)), ((), ())), preferred_element_type=F32)


def params(mib):
    return pltpu.CompilerParams(dimension_semantics=("arbitrary",), vmem_limit_bytes=mib * MIB)


def cost(micros):
    return pl.CostEstimate(flops=int(micros * 1e9), transcendentals=0, bytes_accessed=1 << 20)


def tie(value, *others):
    return lax.optimization_barrier((value, *others))[0]


def whole(shape):
    zeros = (0,) * len(shape)
    return pl.BlockSpec(shape, lambda *_: zeros, pipeline_mode=pl.Buffered(1))


def sds(shape, dtype):
    return jax.ShapeDtypeStruct(shape, dtype)


def norm_parts(rows):
    mean = jnp.mean(rows, axis=-1, keepdims=True)
    cent = rows - mean
    var = jnp.mean(cent * cent, axis=-1, keepdims=True)
    return cent, lax.rsqrt(var + EPS)


def normed_of(x):
    cent, rstd = norm_parts(x.astype(F32))
    return (cent * rstd).astype(BF16)


def halved(bf):
    return bf * jnp.asarray(0.5, BF16)


def silu_both(half):
    t = jnp.tanh(half)
    p = 1.0 + t
    act = half * p
    return act, p + act * (1.0 - t)


def kv_tile(w_t, normed_t, kv_ref, slope_ref, counts_ref):
    act, slope = silu_both(0.5 * nn(w_t, normed_t))
    slope_ref[...] = slope.astype(BF16)
    lane = lax.broadcasted_iota(jnp.int32, (1, BLK), 1)
    for place in range(act.shape[1] // BLK):
        part = act[:, place * BLK : (place + 1) * BLK]
        if counts_ref is not None:
            part = jnp.where(lane < counts_ref[place], part, 0.0)
        kv_ref[place] = part.astype(BF16)


def own_kv_kernel(counts_ref, x_ref, w_ref, kv_ref, kvslope_ref, normed_t_ref, w_t_ref):
    @pl.when(pl.program_id(0) == 0)
    def _():
        normed_t_ref[...] = normed_of(x_ref[...]).T

    w_t_ref[...] = w_ref[...].T
    kv_tile(w_t_ref[...], normed_t_ref[...], kv_ref, kvslope_ref, counts_ref)


def project_own_kv(counts, x, w_in):
    rows = x.shape[0]
    nblk = rows // BLK
    return pl.pallas_call(
        own_kv_kernel,
        grid_spec=pltpu.PrefetchScalarGridSpec(
            num_scalar_prefetch=1,
            grid=(4,),
            in_specs=[
                whole(x.shape),
                pl.BlockSpec((WIDE, 512), lambda j, _: (0, j + 2 + 2 * (j // 2))),
            ],
            out_specs=[
                pl.BlockSpec((nblk, 512, BLK), lambda j, _: (BACK, j, 0)),
                pl.BlockSpec((512, rows), lambda j, _: (j, BACK)),
                pl.BlockSpec((WIDE, rows), lambda j, _: (0, BACK)),
                pl.BlockSpec((512, WIDE), lambda j, _: (j, 0)),
            ],
        ),
        out_shape=[
            sds(((BACK + 1) * nblk, 2 * WIDE, BLK), BF16),
            sds((2 * WIDE, (BACK + 1) * rows), BF16),
            sds((WIDE, (BACK + 1) * rows), BF16),
            sds((2 * WIDE, WIDE), BF16),
        ],
        compiler_params=params(60),
        name="project_own_kv",
        cost_estimate=cost(9),
    )(counts, x, w_in)


def own_uq_kernel(x_ref, grad_ref, w_ref, wo_ref, acts_ref, slope_ref, dy_ref, normed_ref):
    step = pl.program_id(0)

    @pl.when(step == 0)
    def _():
        normed_ref[...] = halved(normed_of(x_ref[...]))

    @pl.when(step < 4)
    def _():
        scale = jnp.where(step >= 2, HD ** (-0.5) * 0.5, 1.0).astype(F32)
        act, slope = silu_both(nn(normed_ref[...], w_ref[...]))
        acts_ref[...] = (act * scale).astype(BF16)
        slope_ref[...] = slope.astype(BF16)

    @pl.when(step >= 4)
    def _():
        dy_ref[...] = nt(grad_ref[...], wo_ref[...])


def project_own_uq(x, grad_out, w_in, w_out):
    rows = x.shape[0]

    def uq_at(j):
        return jnp.minimum(j, 3)

    def dy_at(j):
        return jnp.maximum(j - 4, 0)

    uq = pl.BlockSpec((rows, 512), lambda j: (0, uq_at(j)))
    return pl.pallas_call(
        own_uq_kernel,
        grid=(6,),
        in_specs=[
            whole(x.shape),
            whole(grad_out.shape),
            pl.BlockSpec((WIDE, 512), lambda j: (0, uq_at(j) + 2 * (uq_at(j) // 2))),
            pl.BlockSpec((512, WIDE), lambda j: (dy_at(j), 0)),
        ],
        out_specs=[uq, uq, pl.BlockSpec((rows, 512), lambda j: (0, dy_at(j)))],
        out_shape=[
            sds((rows, 2 * WIDE), BF16),
            sds((rows, 2 * WIDE), BF16),
            sds((rows, WIDE), F32),
        ],
        scratch_shapes=[pltpu.VMEM((rows, WIDE), BF16)],
        compiler_params=params(60),
        name="project_own_uq",
        cost_estimate=cost(10),
    )(x, grad_out, w_in, w_out)


def window_kernel(
    x_even_ref, x_odd_ref, x_near_ref, w_ref, _kv, _slope, _normed,
    kv_ref, slope_ref, normed_t_ref,
):
    rows = x_near_ref.shape[0]

    @pl.when(pl.program_id(0) == 0)
    def _():
        far = x_odd_ref[...].astype(F32) + x_even_ref[...].astype(F32)
        normed_t_ref[:, :rows] = normed_of(far).T
        normed_t_ref[:, rows:] = normed_of(x_near_ref[...]).T

    kv_tile(w_ref[...], normed_t_ref[...], kv_ref, slope_ref, None)


def project_window(xs, w_kv_t, arrays):
    rows = xs[0].shape[0]
    nblk = rows // BLK
    return pl.pallas_call(
        window_kernel,
        grid=(4,),
        in_specs=[whole(x.shape) for x in xs]
        + [pl.BlockSpec((512, WIDE), lambda j: (j, 0))]
        + [pl.BlockSpec(memory_space=pl.ANY)] * 3,
        out_specs=[
            pl.BlockSpec((BACK * nblk, 512, BLK), lambda j: (0, j, 0)),
            pl.BlockSpec((512, BACK * rows), lambda j: (j, 0)),
            pl.BlockSpec((WIDE, BACK * rows), lambda j: (0, 0)),
        ],
        out_shape=[sds(a.shape, BF16) for a in arrays],
        input_output_aliases={len(xs) + 1 + i: i for i in range(3)},
        compiler_params=params(60),
        name="project_window",
        cost_estimate=cost(10),
    )(*xs, w_kv_t, *arrays)


def duo_of(ref, idx_ref, blk, duo, rows):
    return jnp.concatenate([ref[idx_ref[blk, 2 * duo + i], rows, :] for i in range(2)], axis=1)


def diagonal(quad_rows):
    left = lax.broadcasted_iota(jnp.int32, (BLK, BLK), 1) < HD
    pairs = []
    for pair in range(2):
        lanes = slice(pair * BLK, pair * BLK + BLK)
        one = quad_rows[2 * pair * BLK : (2 * pair + 1) * BLK, lanes]
        two = quad_rows[(2 * pair + 1) * BLK : (2 * pair + 2) * BLK, lanes]
        pairs.append(jnp.where(left, one, two))
    return jnp.concatenate(pairs, axis=1)


def put_split(core_ref, val, mine_ref, theirs_ref, group, cols):
    _, pieces, height, _ = mine_ref.shape
    split = val.astype(BF16).reshape(pieces, 2, height, val.shape[1])
    even, odd = split[:, 0], split[:, 1]
    first = core_ref[0] == 0
    mine_ref[group, :, :, cols] = jnp.where(first, even, odd)
    theirs_ref[group, :, :, cols] = jnp.where(first, odd, even)


def fwd_kernel(
    idx_ref, core_ref, q_ref, kv_ref, u_ref, uslope_ref, dy_ref, grad_ref, normed_ref,
    w_ref, g_ref, qt_ref, y_ref, dpu_ref, do_ref, dot_ref, mine_ref, theirs_ref,
    attn_ref, yt_ref, dpu_all_ref,
):
    blk = pl.program_id(0)
    row = lax.broadcasted_iota(jnp.int32, (BLK, BLK), 0)
    col = lax.broadcasted_iota(jnp.int32, (BLK, BLK), 1)
    keep = jnp.concatenate([jnp.full((BLK, BLK), True), col <= row], axis=1)
    qt_ref[...] = q_ref[...].T
    for quad in range(HEADS // 4):
        at = quad * 256
        total = None
        for duo in range(2):
            span = slice(duo * 256, duo * 256 + 256)
            ws = []
            for head in range(4 * quad, 4 * quad + 4):
                cols = slice(head * HD, head * HD + HD)
                keys = duo_of(kv_ref, idx_ref, blk, duo, slice(WIDE + head * HD, WIDE + head * HD + HD))
                w, g = silu_both(nn(q_ref[:, cols], keys))
                if duo == 1:
                    w = jnp.where(keep, w, 0.0)
                    g = jnp.where(keep, g, 0.0)
                w = w.astype(BF16)
                ws.append(w)
                w_ref[0, head, :, span] = w
                g_ref[0, head, :, span] = g.astype(BF16)
            vals = duo_of(kv_ref, idx_ref, blk, duo, slice(at, at + 256))
            part = nt(jnp.concatenate(ws, axis=0), vals)
            total = part if total is None else total + part
        attn_ref[:, at : at + 256] = diagonal(total) * (1.0 / BLK)
    cent, rstd = norm_parts(attn_ref[...])
    z = cent * rstd
    u = u_ref[...].astype(F32)
    dy = dy_ref[...]
    y = (z * u).astype(BF16)
    y_ref[...] = y
    here = pl.ds(pl.multiple_of(blk * BLK, BLK), BLK)
    yt_ref[:, here] = y.T
    dpu = (dy * (0.5 * z) * uslope_ref[...].astype(F32)).astype(BF16)
    dpu_ref[...] = dpu
    dpu_all_ref[here, :] = dpu
    dz = dy * u
    shift = jnp.mean(dz, axis=-1, keepdims=True)
    dattn = rstd * (dz - shift - z * jnp.mean(dz * z, axis=-1, keepdims=True))
    dattn = dattn.astype(BF16)
    do_ref[...] = dattn
    dot_ref[...] = dattn.T

    @pl.when(blk == pl.num_programs(0) - 1)
    def _():
        for group, (left_ref, right_ref) in enumerate(
            ((yt_ref, grad_ref), (normed_ref, dpu_all_ref))
        ):
            for tile in range(2):
                cols = slice(tile * 512, tile * 512 + 512)
                val = nn(left_ref[...], right_ref[:, cols])
                put_split(core_ref, val, mine_ref, theirs_ref, group, cols)


def attend(idx, core, size, acts, slopes, kv, dy, grad_out, normed):
    rows = dy.shape[0]
    nblk = rows // BLK
    scores = pl.BlockSpec((1, HEADS, BLK, 4 * BLK), lambda b, *_: (b, 0, 0, 0))
    rowblk = pl.BlockSpec((BLK, WIDE), lambda b, *_: (b, 0))
    colblk = pl.BlockSpec((WIDE, BLK), lambda b, *_: (0, b))
    chunk = (2, size // 2, WIDE // size, WIDE)
    return pl.pallas_call(
        fwd_kernel,
        grid_spec=pltpu.PrefetchScalarGridSpec(
            num_scalar_prefetch=2,
            grid=(nblk,),
            in_specs=[
                pl.BlockSpec((BLK, WIDE), lambda b, *_: (b, 1)),
                whole(kv.shape),
                rowblk,
                rowblk,
                rowblk,
                whole(grad_out.shape),
                pl.BlockSpec((WIDE, rows), lambda *_: (0, BACK), pipeline_mode=pl.Buffered(1)),
            ],
            out_specs=[
                scores, scores, colblk, rowblk, rowblk, rowblk, colblk, whole(chunk), whole(chunk)
            ],
            scratch_shapes=[
                pltpu.VMEM((BLK, WIDE), F32),
                pltpu.VMEM((WIDE, rows), BF16),
                pltpu.VMEM((rows, WIDE), BF16),
            ],
        ),
        out_shape=[
            sds((nblk, HEADS, BLK, 4 * BLK), BF16),
            sds((nblk, HEADS, BLK, 4 * BLK), BF16),
            sds((WIDE, rows), BF16),
            sds((rows, WIDE), BF16),
            sds((rows, WIDE), BF16),
            sds((rows, WIDE), BF16),
            sds((WIDE, rows), BF16),
            sds(chunk, BF16),
            sds(chunk, BF16),
        ],
        compiler_params=params(60),
        name="attend",
        cost_estimate=cost(18),
    )(idx, core, acts, kv, acts, slopes, dy, grad_out, normed)


def events_kernel(x_ref, y_ref, wo_ref, ev_ref):
    ev_ref[...] = (x_ref[...].astype(F32) + nn(y_ref[...], wo_ref[...])).astype(BF16)


def events(x, y, w_out):
    rows = x.shape[0]
    tile = pl.BlockSpec((rows, 512), lambda j: (0, j))
    return pl.pallas_call(
        events_kernel,
        grid=(2,),
        in_specs=[tile, whole(y.shape), pl.BlockSpec((WIDE, 512), lambda j: (0, j))],
        out_specs=tile,
        out_shape=sds((rows, WIDE), BF16),
        compiler_params=params(60),
        name="events_out",
        cost_estimate=cost(4),
    )(x, y, w_out)


def bwd_kernel(*refs, first):
    (idx_ref, core_ref, w_ref, g_ref, v_ref, k_ref, do_ref, dot_ref, qt_ref, qslope_ref) = refs[:10]
    (vslope_ref, kslope_ref, normed_ref, wv_ref, wk_ref) = refs[10:15]
    rest = refs[15:]
    if first:
        part_ref = rest[5]
        rest = rest[:5] + rest[6:]
    else:
        part_ref, far_ref, near_ref = rest[0], rest[6], rest[7]
        rest = rest[1:6] + rest[8:]
    (mine_ref, theirs_ref, dpq_ref, dvt_ref, dkt_ref) = rest[:5]
    (dva_ref, dka_ref, dvb_ref, dkb_ref, sum_ref) = rest[5:]
    step = pl.program_id(0)
    rows = dpq_ref.shape[0]
    dva_ref[...] = jnp.zeros_like(dva_ref)
    dka_ref[...] = jnp.zeros_like(dka_ref)

    @pl.when(step == 0)
    def _():
        sum_ref[...] = jnp.zeros_like(sum_ref) if first else part_ref[...].astype(F32)

    def one_block(blk, carry):
        at = pl.multiple_of(blk * BLK, BLK)
        block = pl.ds(at, BLK)
        total = None
        for duo in range(2):
            span = slice(duo * 256, duo * 256 + 256)
            dss = []
            for head in range(4):
                cols = slice(head * HD, head * HD + HD)
                dw = nn(do_ref[block, cols], duo_of(v_ref, idx_ref, blk, duo, cols))
                ds = (dw * g_ref[blk, head, :, span].astype(F32)).astype(BF16)
                dss.append(ds)
                dk = nn(qt_ref[cols, block], ds)
                dv = nn(dot_ref[cols, block], w_ref[blk, head, :, span])
                for side in range(2):
                    place = idx_ref[blk, 2 * duo + side]
                    lanes = slice(side * BLK, side * BLK + BLK)
                    dva_ref[place, cols, :] += dv[:, lanes]
                    dka_ref[place, cols, :] += dk[:, lanes]
            part = nt(jnp.concatenate(dss, axis=0), duo_of(k_ref, idx_ref, blk, duo, slice(None)))
            total = part if total is None else total + part
        dq = diagonal(total) * (HD ** (-0.5) / (4 * BLK))
        dpq_ref[block, :] = (dq * qslope_ref[block, :].astype(F32)).astype(BF16)
        return carry

    lax.fori_loop(0, rows // BLK, one_block, 0)
    for place in range(dva_ref.shape[0]):
        lanes = slice(place * BLK, place * BLK + BLK)
        for acc_ref, slope_ref, out_ref in (
            (dva_ref, vslope_ref, dvb_ref),
            (dka_ref, kslope_ref, dkb_ref),
        ):
            out_ref[:, lanes] = (
                acc_ref[place] * (0.5 / BLK) * slope_ref[:, lanes].astype(F32)
            ).astype(BF16)
    dvt_ref[...] = dvb_ref[:, BACK * rows :]
    dkt_ref[...] = dkb_ref[:, BACK * rows :]
    put_split(core_ref, nt(normed_ref[...], dvb_ref[...]), mine_ref, theirs_ref, 0, slice(None))
    put_split(
        core_ref, nn(normed_ref[:, BACK * rows :], dpq_ref[...]), mine_ref, theirs_ref, 1, slice(None)
    )
    put_split(core_ref, nt(normed_ref[...], dkb_ref[...]), mine_ref, theirs_ref, 2, slice(None))
    for at in range(BACK):
        lanes = slice(at * rows, at * rows + rows)
        left = jnp.concatenate([wv_ref[...], wk_ref[...]], axis=1)
        right = jnp.concatenate([dvb_ref[:, lanes], dkb_ref[:, lanes]], axis=0)
        sum_ref[at] += nn(left, right)

    @pl.when(step == pl.num_programs(0) - 1)
    def _():
        for at in range(BACK):
            done = sum_ref[at].astype(BF16)
            if first:
                part_ref[at] = done
            else:
                (far_ref, near_ref)[at][...] = done


def attend_back(start, idx, core, size, w, g, kv, do, do_t, q_t, slopes, kv_slopes, normed, w_in, part):
    rows = do.shape[0]
    nblk = rows // BLK
    places = kv.shape[0]
    first = part is None
    heads = pl.BlockSpec((nblk, 4, BLK, 4 * BLK), lambda i, *_: (0, start + i, 0, 0))
    tall = (BACK + 1) * rows
    wide = pl.BlockSpec((3, size // 2, WIDE // size, 256), lambda i, *_: (0, 0, 0, i))
    cols = pl.BlockSpec((256, rows), lambda i, *_: (i, 0))
    in_specs = [
        heads,
        heads,
        pl.BlockSpec((places, 256, BLK), lambda i, *_: (0, start + i, 0)),
        pl.BlockSpec((places, 256, BLK), lambda i, *_: (0, 4 + start + i, 0)),
        pl.BlockSpec((rows, 256), lambda i, *_: (0, start + i)),
        pl.BlockSpec((256, rows), lambda i, *_: (start + i, 0)),
        pl.BlockSpec((256, rows), lambda i, *_: (start + i, 0)),
        pl.BlockSpec((rows, 256), lambda i, *_: (0, 4 + start + i)),
        pl.BlockSpec((256, tall), lambda i, *_: (start + i, 0)),
        pl.BlockSpec((256, tall), lambda i, *_: (4 + start + i, 0)),
        whole(normed.shape),
        pl.BlockSpec((WIDE, 256), lambda i, *_: (0, 4 + start + i)),
        pl.BlockSpec((WIDE, 256), lambda i, *_: (0, 12 + start + i)),
    ]
    args = [idx, core, w, g, kv, kv, do, do_t, q_t, slopes, kv_slopes, kv_slopes, normed, w_in, w_in]
    chunk = sds((3, size // 2, WIDE // size, 512), BF16)
    out_specs = [wide, wide, pl.BlockSpec((rows, 256), lambda i, *_: (0, i)), cols, cols]
    out_shape = [chunk, chunk, sds((rows, 512), BF16), sds((512, rows), BF16), sds((512, rows), BF16)]
    if first:
        out_specs.append(whole((BACK, WIDE, rows)))
        out_shape.append(sds((BACK, WIDE, rows), BF16))
    else:
        in_specs.append(whole(part.shape))
        args.append(part)
        out_specs += [whole((WIDE, rows))] * 2
        out_shape += [sds((WIDE, rows), BF16)] * 2
    return pl.pallas_call(
        lambda *refs: bwd_kernel(*refs, first=first),
        grid_spec=pltpu.PrefetchScalarGridSpec(
            num_scalar_prefetch=2,
            grid=(2,),
            in_specs=in_specs,
            out_specs=out_specs,
            scratch_shapes=[
                pltpu.VMEM((places, 256, BLK), F32),
                pltpu.VMEM((places, 256, BLK), F32),
                pltpu.VMEM((256, tall), BF16),
                pltpu.VMEM((256, tall), BF16),
                pltpu.VMEM((BACK, WIDE, rows), F32),
            ],
        ),
        out_shape=out_shape,
        compiler_params=params(60),
        name="attend_back_%d" % start,
        cost_estimate=cost(24),
    )(*args)


def dn_u_kernel(w_ref, dpu_ref, own_ref):
    own_ref[...] = nt(w_ref[...], dpu_ref[...])


def grad_normed_u(w_in, dpu):
    rows = dpu.shape[0]
    return pl.pallas_call(
        dn_u_kernel,
        grid=(2,),
        in_specs=[pl.BlockSpec((WIDE // 2, WIDE), lambda j: (j, 0)), whole(dpu.shape)],
        out_specs=pl.BlockSpec((WIDE // 2, rows), lambda j: (j, 0)),
        out_shape=sds((WIDE, rows), F32),
        compiler_params=params(60),
        name="grad_normed_u",
        cost_estimate=cost(4),
    )(w_in, dpu)


def dn_own_kernel(w_ref, u_ref, qa_ref, qb_ref, va_ref, vb_ref, ka_ref, kb_ref, own_ref):
    step = pl.program_id(0)
    half = WIDE // 2
    left, right = w_ref[:, :half], w_ref[:, half:]

    @pl.when(step == 0)
    def _():
        own_ref[...] = u_ref[...] + nn(left, va_ref[...]) + nn(right, vb_ref[...])

    @pl.when(step == 1)
    def _():
        own_ref[...] += nt(left, qa_ref[...]) + nt(right, qb_ref[...])

    @pl.when(step == 2)
    def _():
        own_ref[...] += nn(left, ka_ref[...]) + nn(right, kb_ref[...])


def grad_normed_own(w_in, from_u, *halves):
    return pl.pallas_call(
        dn_own_kernel,
        grid=(3,),
        in_specs=[pl.BlockSpec((WIDE, WIDE), lambda j: (0, j + 1)), whole(from_u.shape)]
        + [whole(a.shape) for a in halves],
        out_specs=whole(from_u.shape),
        out_shape=sds(from_u.shape, F32),
        compiler_params=params(60),
        name="grad_normed_own",
        cost_estimate=cost(8),
    )(w_in, from_u, *halves)


def last_kernel(own_ref, a_ref, b_ref, c_ref, x_ref, grad_ref, out_ref):
    dn_t = own_ref[...] + a_ref[...].astype(F32) + b_ref[...].astype(F32) + c_ref[...].astype(F32)
    dn = dn_t.T
    cent, rstd = norm_parts(x_ref[...].astype(F32))
    z = cent * rstd
    dx = rstd * (
        dn - jnp.mean(dn, axis=-1, keepdims=True) - z * jnp.mean(dn * z, axis=-1, keepdims=True)
    )
    out_ref[...] = (grad_ref[...].astype(F32) + dx).astype(BF16)


def last(own, one, two, three, x, grad_out):
    rows = x.shape[0]
    colblk = pl.BlockSpec((WIDE, BLK), lambda b: (0, b))
    rowblk = pl.BlockSpec((BLK, WIDE), lambda b: (b, 0))
    return pl.pallas_call(
        last_kernel,
        grid=(rows // BLK,),
        in_specs=[colblk, colblk, colblk, colblk, rowblk, rowblk],
        out_specs=rowblk,
        out_shape=sds((rows, WIDE), BF16),
        compiler_params=params(60),
        name="grad_x",
        cost_estimate=cost(6),
    )(own, one, two, three, x, grad_out)


def send(array, pairs):
    return lax.ppermute(array, "seq", pairs)


class Halving:
    def __init__(self, mine, theirs, size, bits):
        self.size, self.bits, self.at = size, bits, 0
        self.left = list(range(1, size.bit_length() - 1))
        self.keep, self.got = mine, self.swap(theirs, 0)

    def swap(self, array, bit):
        return send(array, [(i, i ^ (1 << bit)) for i in range(self.size)])

    def step(self, *after):
        bit = self.bits[self.at]
        inner = 1 << self.left.index(bit)
        self.at += 1
        groups, count, height, cols = self.keep.shape
        shape = (groups, count // (2 * inner), 2, inner * height, cols)
        keep, got = self.keep.reshape(shape), self.got.reshape(shape)
        if after:
            got = tie(got, *after)
        side = (lax.axis_index("seq") >> bit) & 1

        def added(which):
            parts = [lax.dynamic_index_in_dim(a, which, 2, keepdims=False) for a in (keep, got)]
            total = parts[0].astype(F32) + parts[1].astype(F32)
            return total.astype(BF16).reshape(groups, count // 2, height, cols)

        moving = added(1 - side)
        self.keep, self.got = added(side), self.swap(moving, bit)
        self.left.remove(bit)
        return moving

    def parts(self):
        while self.at < len(self.bits):
            self.step()
        return self.keep, self.got


def finish_kernel(ek_ref, eg_ref, ak_ref, ag_ref, bk_ref, bg_ref, win_ref, wout_ref):
    def total(keep_ref, got_ref, group):
        return keep_ref[group, 0].astype(F32) + got_ref[group, 0].astype(F32)

    wout_ref[...] = total(ek_ref, eg_ref, 0)
    win_ref[:, :WIDE] = total(ek_ref, eg_ref, 1)
    for group in range(3):
        at = (group + 1) * WIDE
        win_ref[:, at : at + 512] = total(ak_ref, ag_ref, group)
        win_ref[:, at + 512 : at + WIDE] = total(bk_ref, bg_ref, group)


def finish(*sums):
    args = [a for pair in sums for a in pair]
    height = args[0].shape[2]
    return pl.pallas_call(
        finish_kernel,
        in_specs=[pl.BlockSpec(memory_space=pltpu.VMEM)] * 6,
        out_specs=[pl.BlockSpec(memory_space=pltpu.VMEM)] * 2,
        out_shape=[sds((height, 4 * WIDE), F32), sds((height, WIDE), F32)],
        compiler_params=pltpu.CompilerParams(vmem_limit_bytes=60 * MIB),
        name="finish_sums",
        cost_estimate=cost(2),
    )(*args)


def on_device(events_in, w_in, w_out, kv_list, counts, grad_out):
    size = lax.axis_size("seq")
    nblk = kv_list.shape[0]
    place = lax.axis_index("seq")
    core = (place % 2).astype(jnp.int32)[None]
    pairs = range(0, size, 2)
    live = jnp.arange(BLK, dtype=jnp.int32)[None, :] < counts[:, None]
    shown = jnp.where(live.reshape(-1)[:, None], events_in, jnp.zeros((), BF16))
    x_near = send(shown, [(i, i + 1) for i in range(size - 1)])
    local = jnp.arange(nblk, dtype=jnp.int32)
    index = jnp.concatenate(
        [kv_list + (BACK - place) * nblk, (local + BACK * nblk)[:, None]], axis=1
    )
    index = jnp.clip(index, 0, (BACK + 1) * nblk - 1)

    kv, kv_slopes, normed, w_kv_t = project_own_kv(counts, events_in, w_in)
    x_even = send(tie(shown, w_kv_t), [(i, i + 2) for i in range(0, size - 2, 2)])
    acts, slopes, dy = project_own_uq(tie(events_in, w_kv_t), grad_out, w_in, w_out)
    x_odd = send(tie(x_near, dy), [(i, i + 1) for i in pairs])
    kv, kv_slopes, normed = project_window(
        [x_even, x_odd, x_near], w_kv_t, (kv, kv_slopes, normed)
    )
    w, g, q_t, y, dpu, do, do_t, mine, theirs = attend(
        index, core, size, acts, slopes, kv, dy, grad_out, normed
    )
    ups = list(range(1, size.bit_length() - 1))
    sum_early = Halving(mine, theirs, size, ups[1:] + ups[:1])
    from_u = grad_normed_u(w_in, tie(dpu, mine))
    sent = sum_early.step(from_u)

    def backward(start, token, part):
        return attend_back(
            start, token, core, size, w, g, kv, do, do_t, q_t, slopes, kv_slopes, normed, w_in, part
        )

    mine, theirs, qa, va, ka, part = backward(0, tie(index, sent), None)
    sent = sum_early.step(qa)
    first = Halving(mine, tie(theirs, sent), size, ups)
    events_out = events(events_in, tie(y, first.keep, sent), w_out)
    sent = first.step(events_out)
    mine, theirs, qb, vb, kb, far, near = backward(2, tie(index, sent), part)
    to_even = [(i + 1, i) for i in pairs]
    far, near, mine, theirs, sum_early.got, first.got = lax.optimization_barrier(
        (far, near, mine, theirs, sum_early.got, first.got)
    )
    far_odd = send(far, to_even)
    second = Halving(mine, theirs, size, ups)
    sent = first.step(sum_early.step(second.keep))
    sent = second.step(sent)
    joined = (near.astype(F32) + far_odd.astype(F32)).astype(BF16)
    first.got = tie(first.got, sent)
    sent = first.step()
    own = grad_normed_own(w_in, tie(from_u, sent, joined), qa, qb, va, vb, ka, kb)
    joined, far, near, first.got, sum_early.got = lax.optimization_barrier(
        (joined, far, near, first.got, sum_early.got, own)
    )[:5]
    back = send(joined, [(i, i - 1) for i in range(2, size, 2)])
    far_even = send(far, [(i + 2, i) for i in range(0, size - 2, 2)])
    near_odd = send(near, to_even)
    grad_x = last(own, near_odd, far_even, back, events_in, grad_out)
    grad_w_in, grad_w_out = finish(sum_early.parts(), first.parts(), second.parts())
    return (events_out, grad_x, grad_w_in, grad_w_out)


def solution(mesh):
    rows = P(("grp", "seq"), None)
    return jax.shard_map(
        on_device,
        mesh=mesh,
        in_specs=(rows, P(), P(), rows, P(("grp", "seq")), rows),
        out_specs=(rows, rows, rows, rows),
        check_vma=False,
    )
```

```python
import jax
import jax.numpy as jnp
from jax import lax
from jax.experimental import pallas as pl
from jax.experimental.pallas import tpu as pltpu
from jax.sharding import PartitionSpec as P

HEADS = 16
HD = 64
BLK = 128
WIDE = 1024
BACK = 2
EPS = 1e-05
F32 = jnp.float32
BF16 = jnp.bfloat16
MIB = 1024 * 1024


def nn(left, right):
    return lax.dot_general(left, right, (((1,), (0,)), ((), ())), preferred_element_type=F32)


def nt(left, right):
    return lax.dot_general(left, right, (((1,), (1,)), ((), ())), preferred_element_type=F32)


def params(mib):
    return pltpu.CompilerParams(dimension_semantics=("arbitrary",), vmem_limit_bytes=mib * MIB)


def cost(micros):
    return pl.CostEstimate(flops=int(micros * 1e9), transcendentals=0, bytes_accessed=1 << 20)


def tie(value, *others):
    return lax.optimization_barrier((value, *others))[0]


def whole(shape):
    zeros = (0,) * len(shape)
    return pl.BlockSpec(shape, lambda *_: zeros, pipeline_mode=pl.Buffered(1))


def sds(shape, dtype):
    return jax.ShapeDtypeStruct(shape, dtype)


def norm_parts(rows):
    mean = jnp.mean(rows, axis=-1, keepdims=True)
    cent = rows - mean
    var = jnp.mean(cent * cent, axis=-1, keepdims=True)
    return cent, lax.rsqrt(var + EPS)


def normed_of(x):
    cent, rstd = norm_parts(x.astype(F32))
    return (cent * rstd).astype(BF16)


def halved(bf):
    return bf * jnp.asarray(0.5, BF16)


def silu_both(half):
    t = jnp.tanh(half)
    p = 1.0 + t
    act = half * p
    return act, p + act * (1.0 - t)


def kv_tile(w_t, normed_t, kv_ref, slope_ref, counts_ref):
    act, slope = silu_both(0.5 * nn(w_t, normed_t))
    slope_ref[...] = slope.astype(BF16)
    lane = lax.broadcasted_iota(jnp.int32, (1, BLK), 1)
    for place in range(act.shape[1] // BLK):
        part = act[:, place * BLK : (place + 1) * BLK]
        if counts_ref is not None:
            part = jnp.where(lane < counts_ref[place], part, 0.0)
        kv_ref[place] = part.astype(BF16)


def own_kernel(
    counts_ref, x_ref, grad_ref, w_ref, wo_ref,
    kv_ref, kvslope_ref, normed_t_ref, w_t_ref, acts_ref, slope_ref, dy_ref, normed_ref,
):
    step = pl.program_id(0)

    @pl.when(step == 0)
    def _():
        normed = normed_of(x_ref[...])
        normed_ref[...] = halved(normed)
        normed_t_ref[...] = normed.T

    @pl.when(step < 4)
    def _():
        w_t_ref[...] = w_ref[...].T
        kv_tile(w_t_ref[...], normed_t_ref[...], kv_ref, kvslope_ref, counts_ref)

    @pl.when(jnp.logical_and(step >= 4, step < 8))
    def _():
        scale = jnp.where(step >= 6, HD ** (-0.5) * 0.5, 1.0).astype(F32)
        act, slope = silu_both(nn(normed_ref[...], w_ref[...]))
        acts_ref[...] = (act * scale).astype(BF16)
        slope_ref[...] = slope.astype(BF16)

    @pl.when(step >= 8)
    def _():
        dy_ref[...] = nt(grad_ref[...], wo_ref[...])


def project_own(counts, x, grad_out, w_in, w_out):
    rows = x.shape[0]
    nblk = rows // BLK

    def w_at(j, _):
        early_tile = j + 2 + 2 * (j // 2)
        later = jnp.minimum(j, 7) - 4
        return (0, jnp.where(j < 4, early_tile, later + 2 * (later // 2)))

    def up_to(last, start=0):
        return lambda j: jnp.clip(j - start, 0, last)

    kv_at, uq_at, dy_at = up_to(3), up_to(3, 4), up_to(1, 8)
    uq = pl.BlockSpec((rows, 512), lambda j, _: (0, uq_at(j)))
    return pl.pallas_call(
        own_kernel,
        grid_spec=pltpu.PrefetchScalarGridSpec(
            num_scalar_prefetch=1,
            grid=(10,),
            in_specs=[
                whole(x.shape),
                whole(grad_out.shape),
                pl.BlockSpec((WIDE, 512), w_at),
                pl.BlockSpec((512, WIDE), lambda j, _: (dy_at(j), 0)),
            ],
            out_specs=[
                pl.BlockSpec((nblk, 512, BLK), lambda j, _: (BACK, kv_at(j), 0)),
                pl.BlockSpec((512, rows), lambda j, _: (kv_at(j), BACK)),
                pl.BlockSpec((WIDE, rows), lambda j, _: (0, BACK)),
                pl.BlockSpec((512, WIDE), lambda j, _: (kv_at(j), 0)),
                uq,
                uq,
                pl.BlockSpec((rows, 512), lambda j, _: (0, dy_at(j))),
            ],
            scratch_shapes=[pltpu.VMEM((rows, WIDE), BF16)],
        ),
        out_shape=[
            sds(((BACK + 1) * nblk, 2 * WIDE, BLK), BF16),
            sds((2 * WIDE, (BACK + 1) * rows), BF16),
            sds((WIDE, (BACK + 1) * rows), BF16),
            sds((2 * WIDE, WIDE), BF16),
            sds((rows, 2 * WIDE), BF16),
            sds((rows, 2 * WIDE), BF16),
            sds((rows, WIDE), F32),
        ],
        compiler_params=params(60),
        name="project_own",
        cost_estimate=cost(13),
    )(counts, x, grad_out, w_in, w_out)


def window_kernel(
    x_even_ref, x_odd_ref, x_near_ref, w_ref, _kv, _slope, _normed,
    kv_ref, slope_ref, normed_t_ref,
):
    rows = x_near_ref.shape[0]

    @pl.when(pl.program_id(0) == 0)
    def _():
        far = x_odd_ref[...].astype(F32) + x_even_ref[...].astype(F32)
        normed_t_ref[:, :rows] = normed_of(far).T
        normed_t_ref[:, rows:] = normed_of(x_near_ref[...]).T

    kv_tile(w_ref[...], normed_t_ref[...], kv_ref, slope_ref, None)


def project_window(xs, w_kv_t, arrays):
    rows = xs[0].shape[0]
    nblk = rows // BLK
    return pl.pallas_call(
        window_kernel,
        grid=(4,),
        in_specs=[whole(x.shape) for x in xs]
        + [pl.BlockSpec((512, WIDE), lambda j: (j, 0))]
        + [pl.BlockSpec(memory_space=pl.ANY)] * 3,
        out_specs=[
            pl.BlockSpec((BACK * nblk, 512, BLK), lambda j: (0, j, 0)),
            pl.BlockSpec((512, BACK * rows), lambda j: (j, 0)),
            pl.BlockSpec((WIDE, BACK * rows), lambda j: (0, 0)),
        ],
        out_shape=[sds(a.shape, BF16) for a in arrays],
        input_output_aliases={len(xs) + 1 + i: i for i in range(3)},
        compiler_params=params(60),
        name="project_window",
        cost_estimate=cost(10),
    )(*xs, w_kv_t, *arrays)


def duo_of(ref, idx_ref, blk, duo, rows):
    return jnp.concatenate([ref[idx_ref[blk, 2 * duo + i], rows, :] for i in range(2)], axis=1)


def diagonal(quad_rows):
    left = lax.broadcasted_iota(jnp.int32, (BLK, BLK), 1) < HD
    pairs = []
    for pair in range(2):
        lanes = slice(pair * BLK, pair * BLK + BLK)
        one = quad_rows[2 * pair * BLK : (2 * pair + 1) * BLK, lanes]
        two = quad_rows[(2 * pair + 1) * BLK : (2 * pair + 2) * BLK, lanes]
        pairs.append(jnp.where(left, one, two))
    return jnp.concatenate(pairs, axis=1)


def put_split(core_ref, val, mine_ref, theirs_ref, group, cols):
    _, pieces, height, _ = mine_ref.shape
    split = val.astype(BF16).reshape(pieces, 2, height, val.shape[1])
    even, odd = split[:, 0], split[:, 1]
    first = core_ref[0] == 0
    mine_ref[group, :, :, cols] = jnp.where(first, even, odd)
    theirs_ref[group, :, :, cols] = jnp.where(first, odd, even)


def fwd_kernel(
    idx_ref, core_ref, q_ref, kv_ref, u_ref, uslope_ref, dy_ref, grad_ref, normed_ref,
    w_ref, g_ref, qt_ref, y_ref, dpu_ref, do_ref, dot_ref, mine_ref, theirs_ref,
    attn_ref, yt_ref, dpu_all_ref,
):
    blk = pl.program_id(0)
    row = lax.broadcasted_iota(jnp.int32, (BLK, BLK), 0)
    col = lax.broadcasted_iota(jnp.int32, (BLK, BLK), 1)
    keep = jnp.concatenate([jnp.full((BLK, BLK), True), col <= row], axis=1)
    qt_ref[...] = q_ref[...].T
    for quad in range(HEADS // 4):
        at = quad * 256
        total = None
        for duo in range(2):
            span = slice(duo * 256, duo * 256 + 256)
            ws = []
            for head in range(4 * quad, 4 * quad + 4):
                cols = slice(head * HD, head * HD + HD)
                keys = duo_of(kv_ref, idx_ref, blk, duo, slice(WIDE + head * HD, WIDE + head * HD + HD))
                w, g = silu_both(nn(q_ref[:, cols], keys))
                if duo == 1:
                    w = jnp.where(keep, w, 0.0)
                    g = jnp.where(keep, g, 0.0)
                w = w.astype(BF16)
                ws.append(w)
                w_ref[0, head, :, span] = w
                g_ref[0, head, :, span] = g.astype(BF16)
            vals = duo_of(kv_ref, idx_ref, blk, duo, slice(at, at + 256))
            part = nt(jnp.concatenate(ws, axis=0), vals)
            total = part if total is None else total + part
        attn_ref[:, at : at + 256] = diagonal(total) * (1.0 / BLK)
    cent, rstd = norm_parts(attn_ref[...])
    z = cent * rstd
    u = u_ref[...].astype(F32)
    dy = dy_ref[...]
    y = (z * u).astype(BF16)
    y_ref[...] = y
    here = pl.ds(pl.multiple_of(blk * BLK, BLK), BLK)
    yt_ref[:, here] = y.T
    dpu = (dy * (0.5 * z) * uslope_ref[...].astype(F32)).astype(BF16)
    dpu_ref[...] = dpu
    dpu_all_ref[here, :] = dpu
    dz = dy * u
    shift = jnp.mean(dz, axis=-1, keepdims=True)
    dattn = rstd * (dz - shift - z * jnp.mean(dz * z, axis=-1, keepdims=True))
    dattn = dattn.astype(BF16)
    do_ref[...] = dattn
    dot_ref[...] = dattn.T

    @pl.when(blk == pl.num_programs(0) - 1)
    def _():
        for group, (left_ref, right_ref) in enumerate(
            ((yt_ref, grad_ref), (normed_ref, dpu_all_ref))
        ):
            for tile in range(2):
                cols = slice(tile * 512, tile * 512 + 512)
                val = nn(left_ref[...], right_ref[:, cols])
                put_split(core_ref, val, mine_ref, theirs_ref, group, cols)


def attend(idx, core, size, acts, slopes, kv, dy, grad_out, normed):
    rows = dy.shape[0]
    nblk = rows // BLK
    scores = pl.BlockSpec((1, HEADS, BLK, 4 * BLK), lambda b, *_: (b, 0, 0, 0))
    rowblk = pl.BlockSpec((BLK, WIDE), lambda b, *_: (b, 0))
    colblk = pl.BlockSpec((WIDE, BLK), lambda b, *_: (0, b))
    chunk = (2, size // 2, WIDE // size, WIDE)
    return pl.pallas_call(
        fwd_kernel,
        grid_spec=pltpu.PrefetchScalarGridSpec(
            num_scalar_prefetch=2,
            grid=(nblk,),
            in_specs=[
                pl.BlockSpec((BLK, WIDE), lambda b, *_: (b, 1)),
                whole(kv.shape),
                rowblk,
                rowblk,
                rowblk,
                whole(grad_out.shape),
                pl.BlockSpec((WIDE, rows), lambda *_: (0, BACK), pipeline_mode=pl.Buffered(1)),
            ],
            out_specs=[
                scores, scores, colblk, rowblk, rowblk, rowblk, colblk, whole(chunk), whole(chunk)
            ],
            scratch_shapes=[
                pltpu.VMEM((BLK, WIDE), F32),
                pltpu.VMEM((WIDE, rows), BF16),
                pltpu.VMEM((rows, WIDE), BF16),
            ],
        ),
        out_shape=[
            sds((nblk, HEADS, BLK, 4 * BLK), BF16),
            sds((nblk, HEADS, BLK, 4 * BLK), BF16),
            sds((WIDE, rows), BF16),
            sds((rows, WIDE), BF16),
            sds((rows, WIDE), BF16),
            sds((rows, WIDE), BF16),
            sds((WIDE, rows), BF16),
            sds(chunk, BF16),
            sds(chunk, BF16),
        ],
        compiler_params=params(60),
        name="attend",
        cost_estimate=cost(18),
    )(idx, core, acts, kv, acts, slopes, dy, grad_out, normed)


def events_kernel(x_ref, y_ref, wo_ref, ev_ref):
    ev_ref[...] = (x_ref[...].astype(F32) + nn(y_ref[...], wo_ref[...])).astype(BF16)


def events(x, y, w_out):
    rows = x.shape[0]
    tile = pl.BlockSpec((rows, 512), lambda j: (0, j))
    return pl.pallas_call(
        events_kernel,
        grid=(2,),
        in_specs=[tile, whole(y.shape), pl.BlockSpec((WIDE, 512), lambda j: (0, j))],
        out_specs=tile,
        out_shape=sds((rows, WIDE), BF16),
        compiler_params=params(60),
        name="events_out",
        cost_estimate=cost(4),
    )(x, y, w_out)


def bwd_kernel(*refs, first):
    (idx_ref, core_ref, w_ref, g_ref, v_ref, k_ref, do_ref, dot_ref, qt_ref, qslope_ref) = refs[:10]
    (vslope_ref, kslope_ref, normed_ref, wv_ref, wk_ref) = refs[10:15]
    rest = refs[15:]
    if first:
        part_ref = rest[5]
        rest = rest[:5] + rest[6:]
    else:
        part_ref, far_ref, near_ref = rest[0], rest[6], rest[7]
        rest = rest[1:6] + rest[8:]
    (mine_ref, theirs_ref, dpq_ref, dvt_ref, dkt_ref) = rest[:5]
    (dva_ref, dka_ref, dvb_ref, dkb_ref, sum_ref) = rest[5:]
    step = pl.program_id(0)
    rows = dpq_ref.shape[0]
    dva_ref[...] = jnp.zeros_like(dva_ref)
    dka_ref[...] = jnp.zeros_like(dka_ref)

    @pl.when(step == 0)
    def _():
        sum_ref[...] = jnp.zeros_like(sum_ref) if first else part_ref[...].astype(F32)

    def one_block(blk, carry):
        at = pl.multiple_of(blk * BLK, BLK)
        block = pl.ds(at, BLK)
        total = None
        for duo in range(2):
            span = slice(duo * 256, duo * 256 + 256)
            dss = []
            for head in range(4):
                cols = slice(head * HD, head * HD + HD)
                dw = nn(do_ref[block, cols], duo_of(v_ref, idx_ref, blk, duo, cols))
                ds = (dw * g_ref[blk, head, :, span].astype(F32)).astype(BF16)
                dss.append(ds)
                dk = nn(qt_ref[cols, block], ds)
                dv = nn(dot_ref[cols, block], w_ref[blk, head, :, span])
                for side in range(2):
                    place = idx_ref[blk, 2 * duo + side]
                    lanes = slice(side * BLK, side * BLK + BLK)
                    dva_ref[place, cols, :] += dv[:, lanes]
                    dka_ref[place, cols, :] += dk[:, lanes]
            part = nt(jnp.concatenate(dss, axis=0), duo_of(k_ref, idx_ref, blk, duo, slice(None)))
            total = part if total is None else total + part
        dq = diagonal(total) * (HD ** (-0.5) / (4 * BLK))
        dpq_ref[block, :] = (dq * qslope_ref[block, :].astype(F32)).astype(BF16)
        return carry

    lax.fori_loop(0, rows // BLK, one_block, 0)
    for place in range(dva_ref.shape[0]):
        lanes = slice(place * BLK, place * BLK + BLK)
        for acc_ref, slope_ref, out_ref in (
            (dva_ref, vslope_ref, dvb_ref),
            (dka_ref, kslope_ref, dkb_ref),
        ):
            out_ref[:, lanes] = (
                acc_ref[place] * (0.5 / BLK) * slope_ref[:, lanes].astype(F32)
            ).astype(BF16)
    dvt_ref[...] = dvb_ref[:, BACK * rows :]
    dkt_ref[...] = dkb_ref[:, BACK * rows :]
    put_split(core_ref, nt(normed_ref[...], dvb_ref[...]), mine_ref, theirs_ref, 0, slice(None))
    put_split(
        core_ref, nn(normed_ref[:, BACK * rows :], dpq_ref[...]), mine_ref, theirs_ref, 1, slice(None)
    )
    put_split(core_ref, nt(normed_ref[...], dkb_ref[...]), mine_ref, theirs_ref, 2, slice(None))
    for at in range(BACK):
        lanes = slice(at * rows, at * rows + rows)
        left = jnp.concatenate([wv_ref[...], wk_ref[...]], axis=1)
        right = jnp.concatenate([dvb_ref[:, lanes], dkb_ref[:, lanes]], axis=0)
        sum_ref[at] += nn(left, right)

    @pl.when(step == pl.num_programs(0) - 1)
    def _():
        for at in range(BACK):
            done = sum_ref[at].astype(BF16)
            if first:
                part_ref[at] = done
            else:
                (far_ref, near_ref)[at][...] = done


def attend_back(start, idx, core, size, w, g, kv, do, do_t, q_t, slopes, kv_slopes, normed, w_in, part):
    rows = do.shape[0]
    nblk = rows // BLK
    places = kv.shape[0]
    first = part is None
    heads = pl.BlockSpec((nblk, 4, BLK, 4 * BLK), lambda i, *_: (0, start + i, 0, 0))
    tall = (BACK + 1) * rows
    wide = pl.BlockSpec((3, size // 2, WIDE // size, 256), lambda i, *_: (0, 0, 0, i))
    cols = pl.BlockSpec((256, rows), lambda i, *_: (i, 0))
    in_specs = [
        heads,
        heads,
        pl.BlockSpec((places, 256, BLK), lambda i, *_: (0, start + i, 0)),
        pl.BlockSpec((places, 256, BLK), lambda i, *_: (0, 4 + start + i, 0)),
        pl.BlockSpec((rows, 256), lambda i, *_: (0, start + i)),
        pl.BlockSpec((256, rows), lambda i, *_: (start + i, 0)),
        pl.BlockSpec((256, rows), lambda i, *_: (start + i, 0)),
        pl.BlockSpec((rows, 256), lambda i, *_: (0, 4 + start + i)),
        pl.BlockSpec((256, tall), lambda i, *_: (start + i, 0)),
        pl.BlockSpec((256, tall), lambda i, *_: (4 + start + i, 0)),
        whole(normed.shape),
        pl.BlockSpec((WIDE, 256), lambda i, *_: (0, 4 + start + i)),
        pl.BlockSpec((WIDE, 256), lambda i, *_: (0, 12 + start + i)),
    ]
    args = [idx, core, w, g, kv, kv, do, do_t, q_t, slopes, kv_slopes, kv_slopes, normed, w_in, w_in]
    chunk = sds((3, size // 2, WIDE // size, 512), BF16)
    out_specs = [wide, wide, pl.BlockSpec((rows, 256), lambda i, *_: (0, i)), cols, cols]
    out_shape = [chunk, chunk, sds((rows, 512), BF16), sds((512, rows), BF16), sds((512, rows), BF16)]
    if first:
        out_specs.append(whole((BACK, WIDE, rows)))
        out_shape.append(sds((BACK, WIDE, rows), BF16))
    else:
        in_specs.append(whole(part.shape))
        args.append(part)
        out_specs += [whole((WIDE, rows))] * 2
        out_shape += [sds((WIDE, rows), BF16)] * 2
    return pl.pallas_call(
        lambda *refs: bwd_kernel(*refs, first=first),
        grid_spec=pltpu.PrefetchScalarGridSpec(
            num_scalar_prefetch=2,
            grid=(2,),
            in_specs=in_specs,
            out_specs=out_specs,
            scratch_shapes=[
                pltpu.VMEM((places, 256, BLK), F32),
                pltpu.VMEM((places, 256, BLK), F32),
                pltpu.VMEM((256, tall), BF16),
                pltpu.VMEM((256, tall), BF16),
                pltpu.VMEM((BACK, WIDE, rows), F32),
            ],
        ),
        out_shape=out_shape,
        compiler_params=params(60),
        name="attend_back_%d" % start,
        cost_estimate=cost(24),
    )(*args)


def dn_u_kernel(w_ref, dpu_ref, own_ref):
    own_ref[...] = nt(w_ref[...], dpu_ref[...])


def grad_normed_u(w_in, dpu):
    rows = dpu.shape[0]
    return pl.pallas_call(
        dn_u_kernel,
        grid=(2,),
        in_specs=[pl.BlockSpec((WIDE // 2, WIDE), lambda j: (j, 0)), whole(dpu.shape)],
        out_specs=pl.BlockSpec((WIDE // 2, rows), lambda j: (j, 0)),
        out_shape=sds((WIDE, rows), F32),
        compiler_params=params(60),
        name="grad_normed_u",
        cost_estimate=cost(4),
    )(w_in, dpu)


def dn_own_kernel(w_ref, u_ref, qa_ref, qb_ref, va_ref, vb_ref, ka_ref, kb_ref, own_ref):
    step = pl.program_id(0)
    half = WIDE // 2
    left, right = w_ref[:, :half], w_ref[:, half:]

    @pl.when(step == 0)
    def _():
        own_ref[...] = u_ref[...] + nn(left, va_ref[...]) + nn(right, vb_ref[...])

    @pl.when(step == 1)
    def _():
        own_ref[...] += nt(left, qa_ref[...]) + nt(right, qb_ref[...])

    @pl.when(step == 2)
    def _():
        own_ref[...] += nn(left, ka_ref[...]) + nn(right, kb_ref[...])


def grad_normed_own(w_in, from_u, *halves):
    return pl.pallas_call(
        dn_own_kernel,
        grid=(3,),
        in_specs=[pl.BlockSpec((WIDE, WIDE), lambda j: (0, j + 1)), whole(from_u.shape)]
        + [whole(a.shape) for a in halves],
        out_specs=whole(from_u.shape),
        out_shape=sds(from_u.shape, F32),
        compiler_params=params(60),
        name="grad_normed_own",
        cost_estimate=cost(8),
    )(w_in, from_u, *halves)


def last_kernel(core_ref, own_ref, near_ref, back_ref, x_ref, grad_ref, out_ref):
    near = jnp.where(core_ref[0] == 0, near_ref[...].astype(F32), 0.0)
    dn = (own_ref[...] + near + back_ref[...].astype(F32)).T
    cent, rstd = norm_parts(x_ref[...].astype(F32))
    z = cent * rstd
    dx = rstd * (
        dn - jnp.mean(dn, axis=-1, keepdims=True) - z * jnp.mean(dn * z, axis=-1, keepdims=True)
    )
    out_ref[...] = (grad_ref[...].astype(F32) + dx).astype(BF16)


def last(core, own, near, back, x, grad_out):
    rows = x.shape[0]
    colblk = pl.BlockSpec((WIDE, 256), lambda b, _: (0, b))
    rowblk = pl.BlockSpec((256, WIDE), lambda b, _: (b, 0))
    return pl.pallas_call(
        last_kernel,
        grid_spec=pltpu.PrefetchScalarGridSpec(
            num_scalar_prefetch=1,
            grid=(rows // 256,),
            in_specs=[colblk, colblk, colblk, rowblk, rowblk],
            out_specs=rowblk,
        ),
        out_shape=sds((rows, WIDE), BF16),
        compiler_params=params(60),
        name="grad_x",
        cost_estimate=cost(6),
    )(core, own, near, back, x, grad_out)


def send(array, pairs):
    return lax.ppermute(array, "seq", pairs)


class Halving:
    def __init__(self, mine, theirs, size, bits):
        self.size, self.bits, self.at = size, bits, 0
        self.left = list(range(1, size.bit_length() - 1))
        self.keep, self.got = mine, self.swap(theirs, 0)

    def swap(self, array, bit):
        return send(array, [(i, i ^ (1 << bit)) for i in range(self.size)])

    def step(self, *after):
        bit = self.bits[self.at]
        inner = 1 << self.left.index(bit)
        self.at += 1
        groups, count, height, cols = self.keep.shape
        shape = (groups, count // (2 * inner), 2, inner * height, cols)
        keep, got = self.keep.reshape(shape), self.got.reshape(shape)
        if after:
            got = tie(got, *after)
        side = (lax.axis_index("seq") >> bit) & 1

        def added(which):
            parts = [lax.dynamic_index_in_dim(a, which, 2, keepdims=False) for a in (keep, got)]
            total = parts[0].astype(F32) + parts[1].astype(F32)
            return total.astype(BF16).reshape(groups, count // 2, height, cols)

        moving = added(1 - side)
        self.keep, self.got = added(side), self.swap(moving, bit)
        self.left.remove(bit)
        return moving

    def parts(self):
        while self.at < len(self.bits):
            self.step()
        return self.keep, self.got


def finish_kernel(ek_ref, eg_ref, ak_ref, ag_ref, bk_ref, bg_ref, win_ref, wout_ref):
    def total(keep_ref, got_ref, group):
        return keep_ref[group, 0].astype(F32) + got_ref[group, 0].astype(F32)

    wout_ref[...] = total(ek_ref, eg_ref, 0)
    win_ref[:, :WIDE] = total(ek_ref, eg_ref, 1)
    for group in range(3):
        at = (group + 1) * WIDE
        win_ref[:, at : at + 512] = total(ak_ref, ag_ref, group)
        win_ref[:, at + 512 : at + WIDE] = total(bk_ref, bg_ref, group)


def finish(*sums):
    args = [a for pair in sums for a in pair]
    height = args[0].shape[2]
    return pl.pallas_call(
        finish_kernel,
        in_specs=[pl.BlockSpec(memory_space=pltpu.VMEM)] * 6,
        out_specs=[pl.BlockSpec(memory_space=pltpu.VMEM)] * 2,
        out_shape=[sds((height, 4 * WIDE), F32), sds((height, WIDE), F32)],
        compiler_params=pltpu.CompilerParams(vmem_limit_bytes=60 * MIB),
        name="finish_sums",
        cost_estimate=cost(2),
    )(*args)


def on_device(events_in, w_in, w_out, kv_list, counts, grad_out):
    size = lax.axis_size("seq")
    nblk = kv_list.shape[0]
    place = lax.axis_index("seq")
    core = (place % 2).astype(jnp.int32)[None]
    pairs = range(0, size, 2)
    live = jnp.arange(BLK, dtype=jnp.int32)[None, :] < counts[:, None]
    shown = jnp.where(live.reshape(-1)[:, None], events_in, jnp.zeros((), BF16))
    x_near = send(shown, [(i, i + 1) for i in range(size - 1)])
    x_even = send(shown, [(i, i + 2) for i in range(0, size - 2, 2)])
    x_odd = send(x_near, [(i, i + 1) for i in pairs])
    local = jnp.arange(nblk, dtype=jnp.int32)
    index = jnp.concatenate(
        [kv_list + (BACK - place) * nblk, (local + BACK * nblk)[:, None]], axis=1
    )
    index = jnp.clip(index, 0, (BACK + 1) * nblk - 1)

    kv, kv_slopes, normed, w_kv_t, acts, slopes, dy = project_own(
        counts, events_in, grad_out, w_in, w_out
    )
    x_odd = send(tie(x_near, dy), [(i, i + 1) for i in pairs])
    kv, kv_slopes, normed = project_window(
        [x_even, x_odd, x_near], w_kv_t, (kv, kv_slopes, normed)
    )
    w, g, q_t, y, dpu, do, do_t, mine, theirs = attend(
        index, core, size, acts, slopes, kv, dy, grad_out, normed
    )
    ups = list(range(1, size.bit_length() - 1))
    sum_early = Halving(mine, theirs, size, ups[1:] + ups[:1])
    from_u = grad_normed_u(w_in, tie(dpu, mine))
    sent = sum_early.step(from_u)

    def backward(start, token, part):
        return attend_back(
            start, token, core, size, w, g, kv, do, do_t, q_t, slopes, kv_slopes, normed, w_in, part
        )

    mine, theirs, qa, va, ka, part = backward(0, tie(index, sent), None)
    sent = sum_early.step(qa)
    first = Halving(mine, tie(theirs, sent), size, ups)
    events_out = events(events_in, tie(y, first.keep, sent), w_out)
    sent = first.step(events_out)
    mine, theirs, qb, vb, kb, far, near = backward(2, tie(index, sent), part)
    far, near, mine, theirs, sum_early.got, first.got = lax.optimization_barrier(
        (far, near, mine, theirs, sum_early.got, first.got)
    )
    swapped = send(near, [(i, i ^ 1) for i in range(size)])
    second = Halving(mine, theirs, size, ups)
    sent = first.step(sum_early.step(second.keep))
    sent = second.step(sent)
    onward = jnp.where(core[0] == 1, swapped.astype(F32), 0.0)
    joined = (far.astype(F32) + onward).astype(BF16)
    first.got = tie(first.got, sent)
    sent = first.step()
    own = grad_normed_own(w_in, tie(from_u, sent, joined), qa, qb, va, vb, ka, kb)
    joined, first.got, sum_early.got, _ = lax.optimization_barrier(
        (joined, first.got, sum_early.got, own)
    )
    back = send(joined, [(i + 2, i) for i in range(size - 2)])
    grad_x = last(core, own, swapped, back, events_in, grad_out)
    grad_w_in, grad_w_out = finish(sum_early.parts(), first.parts(), second.parts())
    return (events_out, grad_x, grad_w_in, grad_w_out)


def solution(mesh):
    rows = P(("grp", "seq"), None)
    return jax.shard_map(
        on_device,
        mesh=mesh,
        in_specs=(rows, P(), P(), rows, P(("grp", "seq")), rows),
        out_specs=(rows, rows, rows, rows),
        check_vma=False,
    )
```

```python
import jax
import jax.numpy as jnp
from jax import lax
from jax.experimental import pallas as pl
from jax.experimental.pallas import tpu as pltpu
from jax.sharding import PartitionSpec as P

HEADS = 16
HD = 64
BLK = 128
WIDE = 1024
BACK = 2
EPS = 1e-05
F32 = jnp.float32
BF16 = jnp.bfloat16
MIB = 1024 * 1024


def nn(left, right):
    return lax.dot_general(left, right, (((1,), (0,)), ((), ())), preferred_element_type=F32)


def nt(left, right):
    return lax.dot_general(left, right, (((1,), (1,)), ((), ())), preferred_element_type=F32)


def params(mib):
    return pltpu.CompilerParams(dimension_semantics=("arbitrary",), vmem_limit_bytes=mib * MIB)


def cost(micros):
    return pl.CostEstimate(flops=int(micros * 1e9), transcendentals=0, bytes_accessed=1 << 20)


def tie(value, *others):
    return lax.optimization_barrier((value, *others))[0]


def whole(shape):
    zeros = (0,) * len(shape)
    return pl.BlockSpec(shape, lambda *_: zeros, pipeline_mode=pl.Buffered(1))


def sds(shape, dtype):
    return jax.ShapeDtypeStruct(shape, dtype)


def norm_parts(rows):
    mean = jnp.mean(rows, axis=-1, keepdims=True)
    cent = rows - mean
    var = jnp.mean(cent * cent, axis=-1, keepdims=True)
    return cent, lax.rsqrt(var + EPS)


def normed_of(x):
    cent, rstd = norm_parts(x.astype(F32))
    return (cent * rstd).astype(BF16)


def halved(bf):
    return bf * jnp.asarray(0.5, BF16)


def silu_both(half):
    t = jnp.tanh(half)
    p = 1.0 + t
    act = half * p
    return act, p + act * (1.0 - t)


def kv_tile(w_t, normed_t, kv_ref, slope_ref, counts_ref):
    act, slope = silu_both(0.5 * nn(w_t, normed_t))
    slope_ref[...] = slope.astype(BF16)
    lane = lax.broadcasted_iota(jnp.int32, (1, BLK), 1)
    for place in range(act.shape[1] // BLK):
        part = act[:, place * BLK : (place + 1) * BLK]
        if counts_ref is not None:
            part = jnp.where(lane < counts_ref[place], part, 0.0)
        kv_ref[place] = part.astype(BF16)


def own_kernel(
    counts_ref, x_ref, grad_ref, w_ref, wo_ref,
    kv_ref, kvslope_ref, normed_t_ref, w_t_ref, acts_ref, slope_ref, dy_ref, normed_ref,
):
    step = pl.program_id(0)

    @pl.when(step == 0)
    def _():
        normed = normed_of(x_ref[...])
        normed_ref[...] = halved(normed)
        normed_t_ref[...] = normed.T

    @pl.when(step < 4)
    def _():
        w_t_ref[...] = w_ref[...].T
        kv_tile(w_t_ref[...], normed_t_ref[...], kv_ref, kvslope_ref, counts_ref)

    @pl.when(jnp.logical_and(step >= 4, step < 8))
    def _():
        scale = jnp.where(step >= 6, HD ** (-0.5) * 0.5, 1.0).astype(F32)
        act, slope = silu_both(nn(normed_ref[...], w_ref[...]))
        acts_ref[...] = (act * scale).astype(BF16)
        slope_ref[...] = slope.astype(BF16)

    @pl.when(step >= 8)
    def _():
        dy_ref[...] = nt(grad_ref[...], wo_ref[...])


def project_own(counts, x, grad_out, w_in, w_out):
    rows = x.shape[0]
    nblk = rows // BLK

    def w_at(j, _):
        early_tile = j + 2 + 2 * (j // 2)
        later = jnp.minimum(j, 7) - 4
        return (0, jnp.where(j < 4, early_tile, later + 2 * (later // 2)))

    def up_to(last, start=0):
        return lambda j: jnp.clip(j - start, 0, last)

    kv_at, uq_at, dy_at = up_to(3), up_to(3, 4), up_to(1, 8)
    uq = pl.BlockSpec((rows, 512), lambda j, _: (0, uq_at(j)))
    return pl.pallas_call(
        own_kernel,
        grid_spec=pltpu.PrefetchScalarGridSpec(
            num_scalar_prefetch=1,
            grid=(10,),
            in_specs=[
                whole(x.shape),
                whole(grad_out.shape),
                pl.BlockSpec((WIDE, 512), w_at),
                pl.BlockSpec((512, WIDE), lambda j, _: (dy_at(j), 0)),
            ],
            out_specs=[
                pl.BlockSpec((nblk, 512, BLK), lambda j, _: (BACK, kv_at(j), 0)),
                pl.BlockSpec((512, rows), lambda j, _: (kv_at(j), BACK)),
                pl.BlockSpec((WIDE, rows), lambda j, _: (0, BACK)),
                pl.BlockSpec((512, WIDE), lambda j, _: (kv_at(j), 0)),
                uq,
                uq,
                pl.BlockSpec((rows, 512), lambda j, _: (0, dy_at(j))),
            ],
            scratch_shapes=[pltpu.VMEM((rows, WIDE), BF16)],
        ),
        out_shape=[
            sds(((BACK + 1) * nblk, 2 * WIDE, BLK), BF16),
            sds((2 * WIDE, (BACK + 1) * rows), BF16),
            sds((WIDE, (BACK + 1) * rows), BF16),
            sds((2 * WIDE, WIDE), BF16),
            sds((rows, 2 * WIDE), BF16),
            sds((rows, 2 * WIDE), BF16),
            sds((rows, WIDE), F32),
        ],
        compiler_params=params(54),
        name="project_own",
        cost_estimate=cost(13),
    )(counts, x, grad_out, w_in, w_out)


def window_kernel(
    x_even_ref, x_odd_ref, x_near_ref, w_ref, _kv, _slope, _normed,
    kv_ref, slope_ref, normed_t_ref,
):
    rows = x_near_ref.shape[0]

    @pl.when(pl.program_id(0) == 0)
    def _():
        far = x_odd_ref[...].astype(F32) + x_even_ref[...].astype(F32)
        normed_t_ref[:, :rows] = normed_of(far).T
        normed_t_ref[:, rows:] = normed_of(x_near_ref[...]).T

    kv_tile(w_ref[...], normed_t_ref[...], kv_ref, slope_ref, None)


def project_window(xs, w_kv_t, arrays):
    rows = xs[0].shape[0]
    nblk = rows // BLK
    return pl.pallas_call(
        window_kernel,
        grid=(4,),
        in_specs=[whole(x.shape) for x in xs]
        + [pl.BlockSpec((512, WIDE), lambda j: (j, 0))]
        + [pl.BlockSpec(memory_space=pl.ANY)] * 3,
        out_specs=[
            pl.BlockSpec((BACK * nblk, 512, BLK), lambda j: (0, j, 0)),
            pl.BlockSpec((512, BACK * rows), lambda j: (j, 0)),
            pl.BlockSpec((WIDE, BACK * rows), lambda j: (0, 0)),
        ],
        out_shape=[sds(a.shape, BF16) for a in arrays],
        input_output_aliases={len(xs) + 1 + i: i for i in range(3)},
        compiler_params=params(54),
        name="project_window",
        cost_estimate=cost(10),
    )(*xs, w_kv_t, *arrays)


def duo_of(ref, idx_ref, blk, duo, rows):
    return jnp.concatenate([ref[idx_ref[blk, 2 * duo + i], rows, :] for i in range(2)], axis=1)


def diagonal(quad_rows):
    left = lax.broadcasted_iota(jnp.int32, (BLK, BLK), 1) < HD
    pairs = []
    for pair in range(2):
        lanes = slice(pair * BLK, pair * BLK + BLK)
        one = quad_rows[2 * pair * BLK : (2 * pair + 1) * BLK, lanes]
        two = quad_rows[(2 * pair + 1) * BLK : (2 * pair + 2) * BLK, lanes]
        pairs.append(jnp.where(left, one, two))
    return jnp.concatenate(pairs, axis=1)


def put_split(core_ref, val, mine_ref, theirs_ref, group, cols):
    _, pieces, height, _ = mine_ref.shape
    split = val.astype(BF16).reshape(pieces, 2, height, val.shape[1])
    even, odd = split[:, 0], split[:, 1]
    first = core_ref[0] == 0
    mine_ref[group, :, :, cols] = jnp.where(first, even, odd)
    theirs_ref[group, :, :, cols] = jnp.where(first, odd, even)


def fwd_kernel(
    idx_ref, core_ref, q_ref, kv_ref, u_ref, uslope_ref, dy_ref, grad_ref, normed_ref,
    w_ref, g_ref, qt_ref, y_ref, dpu_ref, do_ref, dot_ref, mine_ref, theirs_ref,
    attn_ref, yt_ref, dpu_all_ref,
):
    blk = pl.program_id(0)
    row = lax.broadcasted_iota(jnp.int32, (BLK, BLK), 0)
    col = lax.broadcasted_iota(jnp.int32, (BLK, BLK), 1)
    keep = jnp.concatenate([jnp.full((BLK, BLK), True), col <= row], axis=1)
    qt_ref[...] = q_ref[...].T
    for quad in range(HEADS // 4):
        at = quad * 256
        total = None
        for duo in range(2):
            span = slice(duo * 256, duo * 256 + 256)
            ws = []
            for head in range(4 * quad, 4 * quad + 4):
                cols = slice(head * HD, head * HD + HD)
                keys = duo_of(kv_ref, idx_ref, blk, duo, slice(WIDE + head * HD, WIDE + head * HD + HD))
                w, g = silu_both(nn(q_ref[:, cols], keys))
                if duo == 1:
                    w = jnp.where(keep, w, 0.0)
                    g = jnp.where(keep, g, 0.0)
                w = w.astype(BF16)
                ws.append(w)
                w_ref[0, head, :, span] = w
                g_ref[0, head, :, span] = g.astype(BF16)
            vals = duo_of(kv_ref, idx_ref, blk, duo, slice(at, at + 256))
            part = nt(jnp.concatenate(ws, axis=0), vals)
            total = part if total is None else total + part
        attn_ref[:, at : at + 256] = diagonal(total) * (1.0 / BLK)
    cent, rstd = norm_parts(attn_ref[...])
    z = cent * rstd
    u = u_ref[...].astype(F32)
    dy = dy_ref[...]
    y = (z * u).astype(BF16)
    y_ref[...] = y
    here = pl.ds(pl.multiple_of(blk * BLK, BLK), BLK)
    yt_ref[:, here] = y.T
    dpu = (dy * (0.5 * z) * uslope_ref[...].astype(F32)).astype(BF16)
    dpu_ref[...] = dpu
    dpu_all_ref[here, :] = dpu
    dz = dy * u
    shift = jnp.mean(dz, axis=-1, keepdims=True)
    dattn = rstd * (dz - shift - z * jnp.mean(dz * z, axis=-1, keepdims=True))
    dattn = dattn.astype(BF16)
    do_ref[...] = dattn
    dot_ref[...] = dattn.T

    @pl.when(blk == pl.num_programs(0) - 1)
    def _():
        for group, (left_ref, right_ref) in enumerate(
            ((yt_ref, grad_ref), (normed_ref, dpu_all_ref))
        ):
            for tile in range(2):
                cols = slice(tile * 512, tile * 512 + 512)
                val = nn(left_ref[...], right_ref[:, cols])
                put_split(core_ref, val, mine_ref, theirs_ref, group, cols)


def attend(idx, core, size, acts, slopes, kv, dy, grad_out, normed):
    rows = dy.shape[0]
    nblk = rows // BLK
    scores = pl.BlockSpec((1, HEADS, BLK, 4 * BLK), lambda b, *_: (b, 0, 0, 0))
    rowblk = pl.BlockSpec((BLK, WIDE), lambda b, *_: (b, 0))
    colblk = pl.BlockSpec((WIDE, BLK), lambda b, *_: (0, b))
    chunk = (2, size // 2, WIDE // size, WIDE)
    return pl.pallas_call(
        fwd_kernel,
        grid_spec=pltpu.PrefetchScalarGridSpec(
            num_scalar_prefetch=2,
            grid=(nblk,),
            in_specs=[
                pl.BlockSpec((BLK, WIDE), lambda b, *_: (b, 1)),
                whole(kv.shape),
                rowblk,
                rowblk,
                rowblk,
                whole(grad_out.shape),
                pl.BlockSpec((WIDE, rows), lambda *_: (0, BACK), pipeline_mode=pl.Buffered(1)),
            ],
            out_specs=[
                scores, scores, colblk, rowblk, rowblk, rowblk, colblk, whole(chunk), whole(chunk)
            ],
            scratch_shapes=[
                pltpu.VMEM((BLK, WIDE), F32),
                pltpu.VMEM((WIDE, rows), BF16),
                pltpu.VMEM((rows, WIDE), BF16),
            ],
        ),
        out_shape=[
            sds((nblk, HEADS, BLK, 4 * BLK), BF16),
            sds((nblk, HEADS, BLK, 4 * BLK), BF16),
            sds((WIDE, rows), BF16),
            sds((rows, WIDE), BF16),
            sds((rows, WIDE), BF16),
            sds((rows, WIDE), BF16),
            sds((WIDE, rows), BF16),
            sds(chunk, BF16),
            sds(chunk, BF16),
        ],
        compiler_params=params(54),
        name="attend",
        cost_estimate=cost(18),
    )(idx, core, acts, kv, acts, slopes, dy, grad_out, normed)


def events_kernel(x_ref, y_ref, wo_ref, ev_ref):
    ev_ref[...] = (x_ref[...].astype(F32) + nn(y_ref[...], wo_ref[...])).astype(BF16)


def events(x, y, w_out):
    rows = x.shape[0]
    tile = pl.BlockSpec((rows, 512), lambda j: (0, j))
    return pl.pallas_call(
        events_kernel,
        grid=(2,),
        in_specs=[tile, whole(y.shape), pl.BlockSpec((WIDE, 512), lambda j: (0, j))],
        out_specs=tile,
        out_shape=sds((rows, WIDE), BF16),
        compiler_params=params(54),
        name="events_out",
        cost_estimate=cost(4),
    )(x, y, w_out)


def bwd_kernel(*refs, first):
    (idx_ref, core_ref, w_ref, g_ref, v_ref, k_ref, do_ref, dot_ref, qt_ref, qslope_ref) = refs[:10]
    (vslope_ref, kslope_ref, normed_ref, wv_ref, wk_ref) = refs[10:15]
    rest = refs[15:]
    if first:
        part_ref = rest[5]
        rest = rest[:5] + rest[6:]
    else:
        part_ref, far_ref, near_ref = rest[0], rest[6], rest[7]
        rest = rest[1:6] + rest[8:]
    (mine_ref, theirs_ref, dpq_ref, dvt_ref, dkt_ref) = rest[:5]
    (dva_ref, dka_ref, dvb_ref, dkb_ref, sum_ref) = rest[5:]
    step = pl.program_id(0)
    rows = dpq_ref.shape[0]
    dva_ref[...] = jnp.zeros_like(dva_ref)
    dka_ref[...] = jnp.zeros_like(dka_ref)

    @pl.when(step == 0)
    def _():
        sum_ref[...] = jnp.zeros_like(sum_ref) if first else part_ref[...].astype(F32)

    def one_block(blk, carry):
        at = pl.multiple_of(blk * BLK, BLK)
        block = pl.ds(at, BLK)
        total = None
        for duo in range(2):
            span = slice(duo * 256, duo * 256 + 256)
            dss = []
            for head in range(4):
                cols = slice(head * HD, head * HD + HD)
                dw = nn(do_ref[block, cols], duo_of(v_ref, idx_ref, blk, duo, cols))
                ds = (dw * g_ref[blk, head, :, span].astype(F32)).astype(BF16)
                dss.append(ds)
                dk = nn(qt_ref[cols, block], ds)
                dv = nn(dot_ref[cols, block], w_ref[blk, head, :, span])
                for side in range(2):
                    place = idx_ref[blk, 2 * duo + side]
                    lanes = slice(side * BLK, side * BLK + BLK)
                    dva_ref[place, cols, :] += dv[:, lanes]
                    dka_ref[place, cols, :] += dk[:, lanes]
            part = nt(jnp.concatenate(dss, axis=0), duo_of(k_ref, idx_ref, blk, duo, slice(None)))
            total = part if total is None else total + part
        dq = diagonal(total) * (HD ** (-0.5) / (4 * BLK))
        dpq_ref[block, :] = (dq * qslope_ref[block, :].astype(F32)).astype(BF16)
        return carry

    lax.fori_loop(0, rows // BLK, one_block, 0)
    for place in range(dva_ref.shape[0]):
        lanes = slice(place * BLK, place * BLK + BLK)
        for acc_ref, slope_ref, out_ref in (
            (dva_ref, vslope_ref, dvb_ref),
            (dka_ref, kslope_ref, dkb_ref),
        ):
            out_ref[:, lanes] = (
                acc_ref[place] * (0.5 / BLK) * slope_ref[:, lanes].astype(F32)
            ).astype(BF16)
    dvt_ref[...] = dvb_ref[:, BACK * rows :]
    dkt_ref[...] = dkb_ref[:, BACK * rows :]
    put_split(core_ref, nt(normed_ref[...], dvb_ref[...]), mine_ref, theirs_ref, 0, slice(None))
    put_split(
        core_ref, nn(normed_ref[:, BACK * rows :], dpq_ref[...]), mine_ref, theirs_ref, 1, slice(None)
    )
    put_split(core_ref, nt(normed_ref[...], dkb_ref[...]), mine_ref, theirs_ref, 2, slice(None))
    for at in range(BACK):
        lanes = slice(at * rows, at * rows + rows)
        left = jnp.concatenate([wv_ref[...], wk_ref[...]], axis=1)
        right = jnp.concatenate([dvb_ref[:, lanes], dkb_ref[:, lanes]], axis=0)
        sum_ref[at] += nn(left, right)

    @pl.when(step == pl.num_programs(0) - 1)
    def _():
        for at in range(BACK):
            done = sum_ref[at].astype(BF16)
            if first:
                part_ref[at] = done
            else:
                (far_ref, near_ref)[at][...] = done


def attend_back(start, idx, core, size, w, g, kv, do, do_t, q_t, slopes, kv_slopes, normed, w_in, part):
    rows = do.shape[0]
    nblk = rows // BLK
    places = kv.shape[0]
    first = part is None
    heads = pl.BlockSpec((nblk, 4, BLK, 4 * BLK), lambda i, *_: (0, start + i, 0, 0))
    tall = (BACK + 1) * rows
    wide = pl.BlockSpec((3, size // 2, WIDE // size, 256), lambda i, *_: (0, 0, 0, i))
    cols = pl.BlockSpec((256, rows), lambda i, *_: (i, 0))
    in_specs = [
        heads,
        heads,
        pl.BlockSpec((places, 256, BLK), lambda i, *_: (0, start + i, 0)),
        pl.BlockSpec((places, 256, BLK), lambda i, *_: (0, 4 + start + i, 0)),
        pl.BlockSpec((rows, 256), lambda i, *_: (0, start + i)),
        pl.BlockSpec((256, rows), lambda i, *_: (start + i, 0)),
        pl.BlockSpec((256, rows), lambda i, *_: (start + i, 0)),
        pl.BlockSpec((rows, 256), lambda i, *_: (0, 4 + start + i)),
        pl.BlockSpec((256, tall), lambda i, *_: (start + i, 0)),
        pl.BlockSpec((256, tall), lambda i, *_: (4 + start + i, 0)),
        whole(normed.shape),
        pl.BlockSpec((WIDE, 256), lambda i, *_: (0, 4 + start + i)),
        pl.BlockSpec((WIDE, 256), lambda i, *_: (0, 12 + start + i)),
    ]
    args = [idx, core, w, g, kv, kv, do, do_t, q_t, slopes, kv_slopes, kv_slopes, normed, w_in, w_in]
    chunk = sds((3, size // 2, WIDE // size, 512), BF16)
    out_specs = [wide, wide, pl.BlockSpec((rows, 256), lambda i, *_: (0, i)), cols, cols]
    out_shape = [chunk, chunk, sds((rows, 512), BF16), sds((512, rows), BF16), sds((512, rows), BF16)]
    if first:
        out_specs.append(whole((BACK, WIDE, rows)))
        out_shape.append(sds((BACK, WIDE, rows), BF16))
    else:
        in_specs.append(whole(part.shape))
        args.append(part)
        out_specs += [whole((WIDE, rows))] * 2
        out_shape += [sds((WIDE, rows), BF16)] * 2
    return pl.pallas_call(
        lambda *refs: bwd_kernel(*refs, first=first),
        grid_spec=pltpu.PrefetchScalarGridSpec(
            num_scalar_prefetch=2,
            grid=(2,),
            in_specs=in_specs,
            out_specs=out_specs,
            scratch_shapes=[
                pltpu.VMEM((places, 256, BLK), F32),
                pltpu.VMEM((places, 256, BLK), F32),
                pltpu.VMEM((256, tall), BF16),
                pltpu.VMEM((256, tall), BF16),
                pltpu.VMEM((BACK, WIDE, rows), F32),
            ],
        ),
        out_shape=out_shape,
        compiler_params=params(54),
        name="attend_back_%d" % start,
        cost_estimate=cost(24),
    )(*args)


def dn_u_kernel(w_ref, dpu_ref, own_ref):
    own_ref[...] = nt(w_ref[...], dpu_ref[...])


def grad_normed_u(w_in, dpu):
    rows = dpu.shape[0]
    return pl.pallas_call(
        dn_u_kernel,
        grid=(2,),
        in_specs=[pl.BlockSpec((WIDE // 2, WIDE), lambda j: (j, 0)), whole(dpu.shape)],
        out_specs=pl.BlockSpec((WIDE // 2, rows), lambda j: (j, 0)),
        out_shape=sds((WIDE, rows), F32),
        compiler_params=params(54),
        name="grad_normed_u",
        cost_estimate=cost(4),
    )(w_in, dpu)


def dn_own_kernel(w_ref, u_ref, qa_ref, qb_ref, va_ref, vb_ref, ka_ref, kb_ref, own_ref):
    step = pl.program_id(0)
    half = WIDE // 2
    left, right = w_ref[:, :half], w_ref[:, half:]

    @pl.when(step == 0)
    def _():
        own_ref[...] = u_ref[...] + nn(left, va_ref[...]) + nn(right, vb_ref[...])

    @pl.when(step == 1)
    def _():
        own_ref[...] += nt(left, qa_ref[...]) + nt(right, qb_ref[...])

    @pl.when(step == 2)
    def _():
        own_ref[...] += nn(left, ka_ref[...]) + nn(right, kb_ref[...])


def grad_normed_own(w_in, from_u, *halves):
    return pl.pallas_call(
        dn_own_kernel,
        grid=(3,),
        in_specs=[pl.BlockSpec((WIDE, WIDE), lambda j: (0, j + 1)), whole(from_u.shape)]
        + [whole(a.shape) for a in halves],
        out_specs=whole(from_u.shape),
        out_shape=sds(from_u.shape, F32),
        compiler_params=params(54),
        name="grad_normed_own",
        cost_estimate=cost(8),
    )(w_in, from_u, *halves)


def last_kernel(core_ref, own_ref, near_ref, back_ref, x_ref, grad_ref, out_ref):
    near = jnp.where(core_ref[0] == 0, near_ref[...].astype(F32), 0.0)
    dn = (own_ref[...] + near + back_ref[...].astype(F32)).T
    cent, rstd = norm_parts(x_ref[...].astype(F32))
    z = cent * rstd
    dx = rstd * (
        dn - jnp.mean(dn, axis=-1, keepdims=True) - z * jnp.mean(dn * z, axis=-1, keepdims=True)
    )
    out_ref[...] = (grad_ref[...].astype(F32) + dx).astype(BF16)


def last(core, own, near, back, x, grad_out):
    rows = x.shape[0]
    colblk = pl.BlockSpec((WIDE, 256), lambda b, _: (0, b))
    rowblk = pl.BlockSpec((256, WIDE), lambda b, _: (b, 0))
    return pl.pallas_call(
        last_kernel,
        grid_spec=pltpu.PrefetchScalarGridSpec(
            num_scalar_prefetch=1,
            grid=(rows // 256,),
            in_specs=[colblk, colblk, colblk, rowblk, rowblk],
            out_specs=rowblk,
        ),
        out_shape=sds((rows, WIDE), BF16),
        compiler_params=params(54),
        name="grad_x",
        cost_estimate=cost(6),
    )(core, own, near, back, x, grad_out)


def send(array, pairs):
    return lax.ppermute(array, "seq", pairs)


class Halving:
    def __init__(self, mine, theirs, size, bits):
        self.size, self.bits, self.at = size, bits, 0
        self.left = list(range(1, size.bit_length() - 1))
        self.keep, self.got = mine, self.swap(theirs, 0)

    def swap(self, array, bit):
        return send(array, [(i, i ^ (1 << bit)) for i in range(self.size)])

    def step(self, *after):
        bit = self.bits[self.at]
        inner = 1 << self.left.index(bit)
        self.at += 1
        groups, count, height, cols = self.keep.shape
        shape = (groups, count // (2 * inner), 2, inner * height, cols)
        keep, got = self.keep.reshape(shape), self.got.reshape(shape)
        if after:
            got = tie(got, *after)
        side = (lax.axis_index("seq") >> bit) & 1

        def added(which):
            parts = [lax.dynamic_index_in_dim(a, which, 2, keepdims=False) for a in (keep, got)]
            total = parts[0].astype(F32) + parts[1].astype(F32)
            return total.astype(BF16).reshape(groups, count // 2, height, cols)

        moving = added(1 - side)
        self.keep, self.got = added(side), self.swap(moving, bit)
        self.left.remove(bit)
        return moving

    def parts(self):
        while self.at < len(self.bits):
            self.step()
        return self.keep, self.got


def finish_kernel(ek_ref, eg_ref, ak_ref, ag_ref, bk_ref, bg_ref, win_ref, wout_ref):
    def total(keep_ref, got_ref, group):
        return keep_ref[group, 0].astype(F32) + got_ref[group, 0].astype(F32)

    wout_ref[...] = total(ek_ref, eg_ref, 0)
    win_ref[:, :WIDE] = total(ek_ref, eg_ref, 1)
    for group in range(3):
        at = (group + 1) * WIDE
        win_ref[:, at : at + 512] = total(ak_ref, ag_ref, group)
        win_ref[:, at + 512 : at + WIDE] = total(bk_ref, bg_ref, group)


def finish(*sums):
    args = [a for pair in sums for a in pair]
    height = args[0].shape[2]
    return pl.pallas_call(
        finish_kernel,
        in_specs=[pl.BlockSpec(memory_space=pltpu.VMEM)] * 6,
        out_specs=[pl.BlockSpec(memory_space=pltpu.VMEM)] * 2,
        out_shape=[sds((height, 4 * WIDE), F32), sds((height, WIDE), F32)],
        compiler_params=pltpu.CompilerParams(vmem_limit_bytes=60 * MIB),
        name="finish_sums",
        cost_estimate=cost(2),
    )(*args)


def on_device(events_in, w_in, w_out, kv_list, counts, grad_out):
    size = lax.axis_size("seq")
    nblk = kv_list.shape[0]
    place = lax.axis_index("seq")
    core = (place % 2).astype(jnp.int32)[None]
    pairs = range(0, size, 2)
    live = jnp.arange(BLK, dtype=jnp.int32)[None, :] < counts[:, None]
    shown = jnp.where(live.reshape(-1)[:, None], events_in, jnp.zeros((), BF16))
    x_near = send(shown, [(i, i + 1) for i in range(size - 1)])
    x_even = send(shown, [(i, i + 2) for i in range(0, size - 2, 2)])
    x_odd = send(x_near, [(i, i + 1) for i in pairs])
    local = jnp.arange(nblk, dtype=jnp.int32)
    index = jnp.concatenate(
        [kv_list + (BACK - place) * nblk, (local + BACK * nblk)[:, None]], axis=1
    )
    index = jnp.clip(index, 0, (BACK + 1) * nblk - 1)

    kv, kv_slopes, normed, w_kv_t, acts, slopes, dy = project_own(
        counts, events_in, grad_out, w_in, w_out
    )
    x_odd = send(tie(x_near, dy), [(i, i + 1) for i in pairs])
    kv, kv_slopes, normed = project_window(
        [x_even, x_odd, x_near], w_kv_t, (kv, kv_slopes, normed)
    )
    w, g, q_t, y, dpu, do, do_t, mine, theirs = attend(
        index, core, size, acts, slopes, kv, dy, grad_out, normed
    )
    ups = list(range(1, size.bit_length() - 1))
    sum_early = Halving(mine, theirs, size, ups[1:] + ups[:1])
    from_u = grad_normed_u(w_in, tie(dpu, mine))
    sent = sum_early.step(from_u)

    def backward(start, token, part):
        return attend_back(
            start, token, core, size, w, g, kv, do, do_t, q_t, slopes, kv_slopes, normed, w_in, part
        )

    mine, theirs, qa, va, ka, part = backward(0, tie(index, sent), None)
    sent = sum_early.step(qa)
    first = Halving(mine, tie(theirs, sent), size, ups)
    events_out = events(events_in, tie(y, first.keep, sent), w_out)
    sent = first.step(events_out)
    mine, theirs, qb, vb, kb, far, near = backward(2, tie(index, sent), part)
    far, near, mine, theirs, sum_early.got, first.got = lax.optimization_barrier(
        (far, near, mine, theirs, sum_early.got, first.got)
    )
    swapped = send(near, [(i, i ^ 1) for i in range(size)])
    second = Halving(mine, theirs, size, ups)
    sent = first.step(sum_early.step(second.keep))
    sent = second.step(sent)
    onward = jnp.where(core[0] == 1, swapped.astype(F32), 0.0)
    joined = (far.astype(F32) + onward).astype(BF16)
    first.got = tie(first.got, sent)
    sent = first.step()
    own = grad_normed_own(w_in, tie(from_u, sent, joined), qa, qb, va, vb, ka, kb)
    joined, first.got, sum_early.got, _ = lax.optimization_barrier(
        (joined, first.got, sum_early.got, own)
    )
    back = send(joined, [(i + 2, i) for i in range(size - 2)])
    grad_x = last(core, own, swapped, back, events_in, grad_out)
    grad_w_in, grad_w_out = finish(sum_early.parts(), first.parts(), second.parts())
    return (events_out, grad_x, grad_w_in, grad_w_out)


def solution(mesh):
    rows = P(("grp", "seq"), None)
    return jax.shard_map(
        on_device,
        mesh=mesh,
        in_specs=(rows, P(), P(), rows, P(("grp", "seq")), rows),
        out_specs=(rows, rows, rows, rows),
        check_vma=False,
    )
```
